32 devices in a mesh: row: 8 (over y, x, core), col: 4 (over z).
Axes of the slice: x: 2, y: 2, z: 4, core: 2. Of those that a mesh axis runs over, the one named last changes fastest.
Arguments:
- hidden_in: bfloat16 [10240, 640], P(('row', 'col')), may hold values from -6 to 6
- cotangent: float32 [10240, 640], P(('row', 'col')), may hold values from -12 to 12
- segment_ids: int32 [8, 1280], P('row'), may hold values from 0 to 2, never falling along the last dimension, each value on 1 to 1024 neighbouring positions
- w_qkv: float32 [2, 640, 1920], P(None, 'row', 'col'), may hold values from -0.3125 to 0.3125
- w_out: float32 [2, 640, 640], P(None, 'row', 'col'), may hold values from -1 to 1
- w_up: float32 [2, 640, 5120], P(None, 'row', 'col'), may hold values from -0.25 to 0.25
- w_down: float32 [2, 5120, 640], P(None, 'col', 'row'), may hold values from -0.078125 to 0.078125
- vectors: float32 [2, 10240], replicated, may hold values from -1.3 to 1.3
- m_qkv: float32 [2, 640, 1920], P(None, 'row', 'col'), may hold values from -64 to 64
- v_qkv: float32 [2, 640, 1920], P(None, 'row', 'col'), may hold values from 10.24 to 40.96
- m_out: float32 [2, 640, 640], P(None, 'row', 'col'), may hold values from -32 to 32
- v_out: float32 [2, 640, 640], P(None, 'row', 'col'), may hold values from 2.56 to 10.24
- m_up: float32 [2, 640, 5120], P(None, 'row', 'col'), may hold values from -40 to 40
- v_up: float32 [2, 640, 5120], P(None, 'row', 'col'), may hold values from 4.096 to 16.384
- m_down: float32 [2, 5120, 640], P(None, 'col', 'row'), may hold values from -48 to 48
- v_down: float32 [2, 5120, 640], P(None, 'col', 'row'), may hold values from 5.12 to 20.48
- m_vectors: float32 [2, 10240], replicated, may hold values from -44.524869 to 44.524869
- v_vectors: float32 [2, 10240], replicated, may hold values from 4.096 to 40.96
Outputs:
- hidden_out: float32 [10240, 640], P(('row', 'col'))
- grad_in: float32 [10240, 640], P(('row', 'col'))
- grad_qkv: float32 [2, 640, 1920], P(None, 'row', 'col')
- grad_out: float32 [2, 640, 640], P(None, 'row', 'col')
- grad_up: float32 [2, 640, 5120], P(None, 'row', 'col')
- grad_down: float32 [2, 5120, 640], P(None, 'col', 'row')
- grad_vectors: float32 [2, 10240], replicated
- new_m_qkv: float32 [2, 640, 1920], P(None, 'row', 'col')
- new_v_qkv: float32 [2, 640, 1920], P(None, 'row', 'col')
- new_m_out: float32 [2, 640, 640], P(None, 'row', 'col')
- new_v_out: float32 [2, 640, 640], P(None, 'row', 'col')
- new_m_up: float32 [2, 640, 5120], P(None, 'row', 'col')
- new_v_up: float32 [2, 640, 5120], P(None, 'row', 'col')
- new_m_down: float32 [2, 5120, 640], P(None, 'col', 'row')
- new_v_down: float32 [2, 5120, 640], P(None, 'col', 'row')
- new_m_vectors: float32 [2, 10240], replicated
- new_v_vectors: float32 [2, 10240], replicated
- new_w_qkv: float32 [2, 640, 1920], P(None, 'row', 'col')
- new_w_out: float32 [2, 640, 640], P(None, 'row', 'col')
- new_w_up: float32 [2, 640, 5120], P(None, 'row', 'col')
- new_w_down: float32 [2, 5120, 640], P(None, 'col', 'row')
- new_vectors: float32 [2, 10240], replicated
- copy_qkv: bfloat16 [2, 640, 1920], P(None, 'row', 'col')
- copy_out: bfloat16 [2, 640, 640], P(None, 'row', 'col')
- copy_up: bfloat16 [2, 640, 5120], P(None, 'row', 'col')
- copy_down: bfloat16 [2, 5120, 640], P(None, 'col', 'row')
- lamb_norms: float32 [2, 4, 2], replicated
The draws below stay inside these ranges and needn't reach their ends.
Inputs may be any that keep to these rules, and one draw needn't show every extreme that they name: `segment_ids`: along each row the ids never fall; ids 0 to 2 each name one sequence of consecutive tokens of at most 1024, and in every row one sequence has exactly 1024 tokens.
All inputs are finite; a program needn't handle non-finite values.
Results may differ from the reference program's by a relative error of at most 0.022.
Values may be sent and summed in bfloat16 or wider, within the bound.
A program may use at most 256 MiB of HBM per device.

```python
import math
import jax
import jax.numpy as jnp
import numpy as np
from jax import lax

D = 640
HDIM = 32
FF = 5120
LAYERS = 2
ROWTOK = 1280
MAXLEN = 1024
STEP = 5
GROUPS = 8
TOKENS = 10240
SEQS = 3


def piece_scale():
    column = jnp.arange(8 * D + FF)
    return jnp.where(column < 8 * D, 1.0, 0.4).astype(jnp.float32) * TOKENS


def draw_vectors(key, part):
    first_key, second_key = jax.random.split(jax.random.fold_in(key, 11))
    shape = (LAYERS, 8 * D + FF)
    biases = 0.3 * jax.random.truncated_normal(first_key, -4.0, 4.0, shape, jnp.float32)
    gains = jax.random.uniform(second_key, shape, jnp.float32, 0.7, 1.3)
    column = jnp.arange(8 * D + FF) // D
    chosen = (column == 0) | (column == 5)
    return jnp.where(chosen[None, :], gains, biases)


def draw_m_vectors(key, part):
    shape = (LAYERS, 8 * D + FF)
    spread = jnp.sqrt(piece_scale())
    return 0.11 * spread[None, :] * jax.random.truncated_normal(jax.random.fold_in(key, 23), -4.0, 4.0, shape, jnp.float32)


def draw_v_vectors(key, part):
    shape = (LAYERS, 8 * D + FF)
    level = jax.random.uniform(jax.random.fold_in(key, 37), shape, jnp.float32, 0.0, math.log(4.0))
    return 0.001 * piece_scale()[None, :] * jnp.exp(level)


def with_spikes(values, own_key, source, target, parts, factor):
    def block_of(position):
        return (jnp.arange(values.shape[position]) // (values.shape[position] // parts)).reshape((-1,) + (1,) * (values.ndim - 1 - position))

    first = jax.random.permutation(own_key, parts)[block_of(target)]
    other_side = (block_of(target) + parts // 2) % parts
    return jnp.where((block_of(source) == first) | (block_of(source) == other_side), factor * values, values)


def block_scale(stream_key, extent, shards, smallest, largest):
    gain, own = 1.0, jax.random.fold_in(stream_key, 6)
    for position, shards_of in shards:
        draws = jnp.exp(jax.random.uniform(jax.random.fold_in(own, position), (shards_of,), jnp.float32, smallest / len(shards), largest / len(shards)))
        gain = gain * jnp.repeat(draws, extent[position] // shards_of).reshape([-1 if axis == position else 1 for axis in range(len(extent))])
    return gain


def split_up(count, total, bound, slope):
    loads = [(1 << 20) // math.isqrt(grade ** slope) + 1 for grade in range(2, count + 1)]
    rest, given = total - bound - (count - 1), [1] * (count - 1)
    while rest > 0:
        free = [i for i in range(count - 1) if given[i] < bound]
        whole, remaining = sum([loads[i] for i in free]), rest
        for i in free:
            more = min(bound - given[i], max(1, remaining * loads[i] // whole), rest)
            given[i] = given[i] + more
            rest = rest - more
    return np.array([bound] + given)


def ragged(stream_key, amount, total, bound, lean):
    if amount == 2:
        one = jax.random.randint(stream_key, (), max(1, total - bound), min(bound, total - 1) + 1)
        return jnp.stack([one, total - one])
    sizes = jnp.asarray(split_up(amount, total, bound, lean), jnp.int32)
    couples = (amount - 1) // 2
    donor, sink = sizes[1:1 + 2 * couples:2], sizes[2:2 + 2 * couples:2]
    slack = jnp.minimum(donor - 1, bound - sink)
    passed = jax.random.randint(jax.random.fold_in(stream_key, 1), (couples,), 0, 1 << 20) % (slack + 1)
    sizes = sizes.at[1:1 + 2 * couples:2].set(donor - passed).at[2:2 + 2 * couples:2].set(sink + passed)
    return sizes[jax.random.permutation(jax.random.fold_in(stream_key, 2), amount)]


def bell_draw(key, shape, deviation, reach, pieces=(), dtype=jnp.bfloat16):
    array = deviation * jax.random.normal(key, shape, jnp.float32)
    if pieces:
        array = array * block_scale(key, shape, pieces, -0.22, 0.18)
    return jnp.clip(array, -reach, reach).astype(dtype)


def bell_draw_with(stream_key, shape, deviation, reach, cuts, heavy, held_as=jnp.bfloat16):
    result = deviation * jax.random.normal(stream_key, shape, jnp.float32)
    if cuts:
        result = result * block_scale(stream_key, shape, cuts, -0.22, 0.18)
    return jnp.clip(with_spikes(result, jax.random.fold_in(stream_key, 3), *heavy), -reach, reach).astype(held_as)


def setup_inputs(seed: int = 0) -> dict:
    splits = jax.random.split(jax.random.key(seed), 19)
    hidden_in = bell_draw(splits[0], (TOKENS, D), 1.0, 6.0, ((0, 32),))
    cotangent = bell_draw_with(splits[1], (TOKENS, D), 1.0, 12.0, ((0, 32),), (0, 1, 32, 2.75), jnp.float32)
    segment_ids = jax.vmap(lambda own: jnp.searchsorted(jnp.cumsum(ragged(own, SEQS, ROWTOK, MAXLEN, 2)), jnp.arange(ROWTOK), side="right"))(jax.random.split(splits[2], GROUPS)).reshape((GROUPS, ROWTOK)).astype(jnp.int32)
    w_qkv = bell_draw(splits[3], (LAYERS, D, 3 * D), (D // 2) ** -0.5, 0.3125, ((1, 8), (2, 4)), jnp.float32)
    w_out = bell_draw(splits[4], (LAYERS, D, D), (D // 16) ** -0.5, 1.0, ((1, 8), (2, 4)), jnp.float32)
    w_up = bell_draw(splits[5], (LAYERS, D, FF), D ** -0.5, 0.25, ((1, 8), (2, 4)), jnp.float32)
    w_down = bell_draw(splits[6], (LAYERS, FF, D), FF ** -0.5, 0.078125, ((1, 4), (2, 8)), jnp.float32)
    vectors = draw_vectors(jax.random.fold_in(splits[18], 71), 0)
    m_qkv = bell_draw(splits[8], (LAYERS, D, 3 * D), (0.11 * TOKENS ** 0.5), 64.0, ((1, 8), (2, 4)), jnp.float32)
    v_qkv = jnp.clip(jnp.exp(math.log(40.96) - 1.3862944 * jax.random.uniform(splits[9], (LAYERS, D, 3 * D), jnp.float32) ** block_scale(splits[9], (LAYERS, D, 3 * D), ((1, 8), (2, 4)), -0.2, 0.2)), 10.24, 40.96)
    m_out = bell_draw(splits[10], (LAYERS, D, D), (0.055 * TOKENS ** 0.5), 32.0, ((1, 8), (2, 4)), jnp.float32)
    v_out = jnp.clip(jnp.exp(math.log(10.24) - 1.3862944 * jax.random.uniform(splits[11], (LAYERS, D, D), jnp.float32) ** block_scale(splits[11], (LAYERS, D, D), ((1, 8), (2, 4)), -0.2, 0.2)), 2.56, 10.24)
    m_up = bell_draw(splits[12], (LAYERS, D, FF), (0.07 * TOKENS ** 0.5), 40.0, ((1, 8), (2, 4)), jnp.float32)
    v_up = jnp.clip(jnp.exp(math.log(16.384) - 1.3862944 * jax.random.uniform(splits[13], (LAYERS, D, FF), jnp.float32) ** block_scale(splits[13], (LAYERS, D, FF), ((1, 8), (2, 4)), -0.2, 0.2)), 4.096, 16.384)
    m_down = bell_draw(splits[14], (LAYERS, FF, D), (0.078 * TOKENS ** 0.5), 48.0, ((1, 4), (2, 8)), jnp.float32)
    v_down = jnp.clip(jnp.exp(math.log(20.48) - 1.3862944 * jax.random.uniform(splits[15], (LAYERS, FF, D), jnp.float32) ** block_scale(splits[15], (LAYERS, FF, D), ((1, 4), (2, 8)), -0.2, 0.2)), 5.12, 20.48)
    m_vectors = draw_m_vectors(jax.random.fold_in(splits[18], 71), 0)
    v_vectors = draw_v_vectors(jax.random.fold_in(splits[18], 71), 0)
    return dict(hidden_in=hidden_in, cotangent=cotangent, segment_ids=segment_ids, w_qkv=w_qkv, w_out=w_out, w_up=w_up, w_down=w_down, vectors=vectors, m_qkv=m_qkv, v_qkv=v_qkv, m_out=m_out, v_out=v_out, m_up=m_up, v_up=v_up, m_down=m_down, v_down=v_down, m_vectors=m_vectors, v_vectors=v_vectors)


@jax.custom_vjp
def low(v):
    return lax.optimization_barrier(v.astype(jnp.bfloat16)).astype(jnp.float32)

@jax.custom_vjp
def low_back(v):
    return v

def low_keep(v):
    return (low(v), None)

def low_pass(kept, grad):
    return (grad,)

def back_keep(v):
    return (v, None)

def back_low(kept, grad):
    return (low(grad),)
low.defvjp(low_keep, low_pass)
low_back.defvjp(back_keep, back_low)

def matmul(left, right):
    return jnp.dot(left, right, precision=lax.Precision.HIGHEST, preferred_element_type=jnp.float32)

def layer_norm(values_in, norm_gain, norm_bias):
    average = lax.optimization_barrier(jnp.mean(values_in, axis=-1, keepdims=True))
    centered = values_in - average
    variance = lax.optimization_barrier(jnp.mean(centered * centered, axis=-1, keepdims=True))
    return centered * lax.rsqrt(variance + 1e-05) * norm_gain + norm_bias

def block(state_rows, group_ids, qkv_w, out_w, up_w, down_w, vector):
    features = state_rows.shape[1]
    tokens = state_rows.shape[0]
    normed = low(layer_norm(state_rows, vector[0:features], vector[features:2 * features]))
    projected = matmul(normed, qkv_w)
    queries = low(low_back(projected[:, :features] + vector[2 * features:3 * features]))
    key_rows = low(low_back(projected[:, features:2 * features]))
    value_rows = low(low_back(projected[:, 2 * features:] + vector[3 * features:4 * features]))
    q_heads = queries.reshape(tokens, -1, HDIM)
    k_heads = key_rows.reshape(tokens, -1, HDIM)
    v_heads = value_rows.reshape(tokens, -1, HDIM)
    scores = jnp.einsum('qhd,khd->hqk', q_heads, k_heads, precision=lax.Precision.HIGHEST) * HDIM ** (-0.5)
    same_seq = group_ids[:, None] == group_ids[None, :]
    scores = low_back(jnp.where(same_seq[None, :, :], scores, -1e+30))
    row_max = lax.optimization_barrier(jnp.max(scores, axis=-1, keepdims=True))
    raised = jnp.exp(scores - row_max)
    softmax = low(raised / lax.optimization_barrier(jnp.sum(raised, axis=-1, keepdims=True)))
    attended = jnp.einsum('hqk,khd->qhd', softmax, v_heads, precision=lax.Precision.HIGHEST).reshape(tokens, features)
    attended = low(low_back(attended))
    middle = state_rows + low_back(matmul(attended, out_w) + vector[4 * features:5 * features])
    normed_ffn = low(layer_norm(middle, vector[5 * features:6 * features], vector[6 * features:7 * features]))
    before = low_back(matmul(normed_ffn, up_w) + vector[8 * features:])
    hidden = low(jax.nn.gelu(before, approximate=False))
    return middle + low_back(matmul(hidden, down_w) + vector[7 * features:8 * features])

def adam_direction(weight, gradient, first_mom, second_mom, decay_rate):
    first_new = 0.9 * first_mom + 0.1 * gradient
    second_new = 0.999 * second_mom + 0.001 * gradient * gradient
    direction = first_new / (1.0 - 0.9 ** STEP) / (jnp.sqrt(second_new / (1.0 - 0.999 ** STEP)) + 1e-06) + decay_rate * weight
    return (first_new, second_new, direction)

def matrix_sums(weight, direction):
    return (lax.optimization_barrier(jnp.sum(weight * weight, axis=(1, 2))), lax.optimization_barrier(jnp.sum(direction * direction, axis=(1, 2))))

def vector_update(vector, gradient, first_mom, second_mom):
    first_new, second_new, direction = adam_direction(vector, gradient, first_mom, second_mom, 0.0)
    depth_count = vector.shape[0]
    head_part = 8 * D

    def ratio_of(weight_part, step_part):
        return jnp.sqrt(lax.optimization_barrier(jnp.sum(weight_part * weight_part, axis=-1, keepdims=True))) / jnp.sqrt(lax.optimization_barrier(jnp.sum(step_part * step_part, axis=-1, keepdims=True)))
    lead_ratio = ratio_of(vector[:, :head_part].reshape(depth_count, 8, D), direction[:, :head_part].reshape(depth_count, 8, D))
    tail_ratio = ratio_of(vector[:, head_part:], direction[:, head_part:])
    trust_ratio = jnp.concatenate([jnp.broadcast_to(lead_ratio, (depth_count, 8, D)).reshape(depth_count, head_part), jnp.broadcast_to(tail_ratio, (depth_count, FF))], axis=1)
    return (first_new, second_new, vector - 0.5 * trust_ratio * direction)

def reference(hidden_in, cotangent, segment_ids, w_qkv, w_out, w_up, w_down, vectors, m_qkv, v_qkv, m_out, v_out, m_up, v_up, m_down, v_down, m_vectors, v_vectors):
    features = hidden_in.shape[1]
    group_count = segment_ids.shape[0]
    group_rows = segment_ids.shape[1]
    starts = hidden_in.astype(jnp.float32).reshape(group_count, group_rows, features)
    backward_in = cotangent.reshape(group_count, group_rows, features)

    def forward(states, params):
        qkv_all, out_all, up_all, down_all, vector_all = params
        qkv_all = low(qkv_all)
        out_all = low(out_all)
        up_all = low(up_all)
        down_all = low(down_all)

        def run_group(state_rows, group_ids):
            for depth_at in range(LAYERS):
                state_rows = block(state_rows, group_ids, qkv_all[depth_at], out_all[depth_at], up_all[depth_at], down_all[depth_at], vector_all[depth_at])
            return state_rows
        checked = jax.checkpoint(run_group)
        return lax.map(lambda members: checked(members[0], members[1]), (states, segment_ids))
    outputs, pullback = jax.vjp(forward, starts, (w_qkv, w_out, w_up, w_down, vectors))
    grad_states, grads = pullback(backward_in)
    grad_qkv, grad_out, grad_up, grad_down, grad_vectors = grads
    masters = (w_qkv, w_out, w_up, w_down)
    gradients = (grad_qkv, grad_out, grad_up, grad_down)
    firsts = (m_qkv, m_out, m_up, m_down)
    seconds = (v_qkv, v_out, v_up, v_down)
    new_firsts = []
    new_seconds = []
    new_masters = []
    norm_rows = []
    for kind in range(4):
        first_new, second_new, direction = adam_direction(masters[kind], gradients[kind], firsts[kind], seconds[kind], 0.01)
        weight_sq, step_sq = matrix_sums(masters[kind], direction)
        weight_norm = jnp.sqrt(weight_sq)
        step_norm = jnp.sqrt(step_sq)
        new_firsts.append(first_new)
        new_seconds.append(second_new)
        new_masters.append(masters[kind] - 0.5 * (weight_norm / step_norm)[:, None, None] * direction)
        norm_rows.append(jnp.stack([weight_norm, step_norm], axis=1))
    lamb_norms = jnp.stack(norm_rows, axis=1)
    vec_first, vec_second, new_vectors = vector_update(vectors, grad_vectors, m_vectors, v_vectors)
    return (outputs.reshape(-1, features), grad_states.reshape(-1, features), grad_qkv, grad_out, grad_up, grad_down, grad_vectors, new_firsts[0], new_seconds[0], new_firsts[1], new_seconds[1], new_firsts[2], new_seconds[2], new_firsts[3], new_seconds[3], vec_first, vec_second, new_masters[0], new_masters[1], new_masters[2], new_masters[3], new_vectors, new_masters[0].astype(jnp.bfloat16), new_masters[1].astype(jnp.bfloat16), new_masters[2].astype(jnp.bfloat16), new_masters[3].astype(jnp.bfloat16), lamb_norms)
```

```python
import functools
from functools import partial

import jax
import jax.numpy as jnp
from jax import lax
from jax.experimental import pallas as pl
from jax.experimental.pallas import tpu as pltpu
from jax.sharding import PartitionSpec as P

D = 640
HDIM = 32
FF = 5120
STEP = 5


head_groups = 4
negative = -1e30


def layer_norm(values_in, norm_gain, norm_bias):
    average = jnp.mean(values_in, axis=-1, keepdims=True)
    centered = values_in - average
    variance = jnp.mean(centered * centered, axis=-1, keepdims=True)
    return centered * lax.rsqrt(variance + 1e-05) * norm_gain + norm_bias


def to_groups(matrix):
    tokens = matrix.shape[0]
    return matrix.reshape(tokens, head_groups, -1, HDIM).transpose(1, 2, 0, 3)


def from_groups(blocks):
    return blocks.transpose(2, 0, 1, 3).reshape(blocks.shape[2], -1)


def contract_rows(left, right):
    return lax.dot_general(
        left, right, (((0,), (0,)), ((), ())), preferred_element_type=jnp.float32
    )


def contract_cols(left, right):
    return lax.dot_general(
        left, right, (((1,), (1,)), ((), ())), preferred_element_type=jnp.float32
    )


def column_total(matrix):
    return jnp.sum(matrix.astype(jnp.float32), axis=0)


def masked_scores(query_block, key_block, allowed):
    scores = jnp.einsum(
        "hqd,hkd->hqk", query_block, key_block, preferred_element_type=jnp.float32
    ) * HDIM ** (-0.5)
    return jnp.where(allowed[None, :, :], scores, negative)


def attend(queries, all_kv, allowed, kept_lse):
    features = queries.shape[1]
    tokens = queries.shape[0]
    q_groups = to_groups(queries)
    k_groups = to_groups(all_kv[:, :features])
    v_groups = to_groups(all_kv[:, features:])
    if kept_lse is None:

        def first_group(members):
            q_block, k_block, v_block = members
            scores = masked_scores(q_block, k_block, allowed)
            row_max = jnp.max(scores, axis=-1)
            log_total = row_max + jnp.log(jnp.sum(jnp.exp(scores - row_max[..., None]), axis=-1))
            softmax = jnp.exp(scores - log_total[..., None]).astype(jnp.bfloat16)
            return (
                jnp.einsum("hqk,hkd->hqd", softmax, v_block, preferred_element_type=jnp.float32),
                log_total,
            )

        attended, log_total = lax.map(first_group, (q_groups, k_groups, v_groups))
    else:
        log_total = kept_lse.reshape(head_groups, -1, tokens)

        def again_group(members):
            q_block, k_block, v_block, lse_block = members
            softmax = jnp.exp(
                masked_scores(q_block, k_block, allowed) - lse_block[..., None]
            ).astype(jnp.bfloat16)
            return jnp.einsum("hqk,hkd->hqd", softmax, v_block, preferred_element_type=jnp.float32)

        attended = lax.map(again_group, (q_groups, k_groups, v_groups, log_total))
    return (from_groups(attended).astype(jnp.bfloat16), log_total.reshape(-1, tokens))


def attention_back(queries, all_kv, grad_mixed, kept_lse, allowed):
    features = queries.shape[1]
    tokens = queries.shape[0]
    inv_root = HDIM ** (-0.5)
    q_groups = to_groups(queries)
    k_groups = to_groups(all_kv[:, :features])
    v_groups = to_groups(all_kv[:, features:])
    g_groups = to_groups(grad_mixed)
    lse_groups = kept_lse.reshape(head_groups, -1, tokens)

    def one_group(members):
        q_block, k_block, v_block, g_block, lse_block = members
        softmax = jnp.exp(masked_scores(q_block, k_block, allowed) - lse_block[..., None])
        grad_probs = jnp.einsum(
            "hqd,hkd->hqk", g_block, v_block, preferred_element_type=jnp.float32
        )
        row_dot = jnp.sum(softmax * grad_probs, axis=-1, keepdims=True)
        grad_scores = (softmax * (grad_probs - row_dot)).astype(jnp.bfloat16)
        grad_q = (
            jnp.einsum("hqk,hkd->hqd", grad_scores, k_block, preferred_element_type=jnp.float32)
            * inv_root
        )
        grad_k = (
            jnp.einsum("hqk,hqd->hkd", grad_scores, q_block, preferred_element_type=jnp.float32)
            * inv_root
        )
        grad_v = jnp.einsum(
            "hqk,hqd->hkd",
            softmax.astype(jnp.bfloat16),
            g_block,
            preferred_element_type=jnp.float32,
        )
        return (grad_q, grad_k, grad_v)

    grad_q, grad_k, grad_v = lax.map(
        one_group, (q_groups, k_groups, v_groups, g_groups, lse_groups)
    )
    return (
        from_groups(grad_q),
        jnp.concatenate([from_groups(grad_k), from_groups(grad_v)], axis=1),
    )


def layer_forward(state_in, weights, vector, allowed, kept_lse):
    w_qkv_full, w_out_full, w_up_part, w_down_part = weights
    features = state_in.shape[1]
    normed = layer_norm(state_in, vector[0:features], vector[features : 2 * features]).astype(
        jnp.bfloat16
    )
    projected = jnp.dot(normed, w_qkv_full, preferred_element_type=jnp.float32)
    queries = (projected[:, :features] + vector[2 * features : 3 * features]).astype(jnp.bfloat16)
    kv_bias = jnp.concatenate(
        [jnp.zeros((features,), jnp.float32), vector[3 * features : 4 * features]]
    )
    own_kv = (projected[:, features:] + kv_bias).astype(jnp.bfloat16)
    all_kv = lax.all_gather(own_kv, "col", axis=0, tiled=True)
    attended, log_total = attend(queries, all_kv, allowed, kept_lse)
    middle = state_in + (
        jnp.dot(attended, w_out_full, preferred_element_type=jnp.float32)
        + vector[4 * features : 5 * features]
    )
    normed_ffn = layer_norm(
        middle, vector[5 * features : 6 * features], vector[6 * features : 7 * features]
    ).astype(jnp.bfloat16)
    before = (
        jnp.dot(normed_ffn, w_up_part, preferred_element_type=jnp.float32) + vector[8 * features :]
    )
    hidden = jax.nn.gelu(before, approximate=False).astype(jnp.bfloat16)
    branch = jnp.dot(hidden, w_down_part, preferred_element_type=jnp.float32)
    state_out = middle + (branch + vector[7 * features : 8 * features])
    kept_vals = (normed, queries, all_kv, log_total, attended, middle, normed_ffn, before, hidden)
    return (state_out, kept_vals)


def layer_backward(grad_state, state_in, kept_vals, weights, vector, allowed):
    w_qkv_full, w_out_full, w_up_part, w_down_part = weights
    normed, queries, all_kv, log_total, attended, middle, ffn_rows, before, hidden = kept_vals
    features = state_in.shape[1]
    grad_branch = grad_state.astype(jnp.bfloat16)
    gelu_vjp = jax.vjp(partial(jax.nn.gelu, approximate=False), before)[1]
    grad_down = contract_rows(hidden, grad_branch)
    grad_before = gelu_vjp(contract_cols(grad_branch, w_down_part))[0].astype(jnp.bfloat16)
    grad_up = contract_rows(ffn_rows, grad_before)
    grad_up_bias = column_total(grad_before)
    grad_normed_ffn = contract_cols(grad_before, w_up_part)
    norm_two = jax.vjp(
        layer_norm, middle, vector[5 * features : 6 * features], vector[6 * features : 7 * features]
    )[1]
    grad_middle_norm, grad_gain_two, grad_bias_two = norm_two(grad_normed_ffn)
    grad_middle = grad_state + grad_middle_norm
    grad_attn_out = grad_middle.astype(jnp.bfloat16)
    grad_out_w = contract_rows(attended, grad_attn_out)
    grad_mixed = contract_cols(grad_attn_out, w_out_full).astype(jnp.bfloat16)
    grad_queries, kv_terms = attention_back(queries, all_kv, grad_mixed, log_total, allowed)
    grad_kv = lax.psum_scatter(
        kv_terms.astype(jnp.bfloat16), "col", scatter_dimension=0, tiled=True
    )
    grad_queries = grad_queries.astype(jnp.bfloat16)
    grad_proj = jnp.concatenate([grad_queries, grad_kv], axis=1)
    grad_qkv_w = contract_rows(normed, grad_proj)
    grad_normed = contract_cols(grad_proj, w_qkv_full)
    norm_one = jax.vjp(layer_norm, state_in, vector[0:features], vector[features : 2 * features])[1]
    grad_input_norm, grad_gain_one, grad_bias_one = norm_one(grad_normed)
    grad_input = grad_middle + grad_input_norm
    grad_vector = jnp.concatenate(
        [
            grad_gain_one,
            grad_bias_one,
            column_total(grad_queries),
            column_total(grad_kv[:, features:]),
            column_total(grad_attn_out),
            grad_gain_two,
            grad_bias_two,
            column_total(grad_branch),
            grad_up_bias,
        ]
    )
    return (grad_input, (grad_qkv_w, grad_out_w, grad_up, grad_down), grad_vector)


def adam_direction(weight, gradient, first_mom, second_mom, decay_rate):
    first_new = 0.9 * first_mom + 0.1 * gradient
    second_new = 0.999 * second_mom + 0.001 * gradient * gradient
    direction = (
        first_new / (1.0 - 0.9**STEP) / (jnp.sqrt(second_new / (1.0 - 0.999**STEP)) + 1e-06)
        + decay_rate * weight
    )
    return (first_new, second_new, direction)


def matrix_sums(weight, direction):
    return (jnp.sum(weight * weight, axis=(1, 2)), jnp.sum(direction * direction, axis=(1, 2)))


def vector_update(vector, gradient, first_mom, second_mom):
    first_new, second_new, direction = adam_direction(vector, gradient, first_mom, second_mom, 0.0)
    depth_count = vector.shape[0]
    head_part = 8 * D

    def ratio_of(weight_part, step_part):
        return jnp.sqrt(jnp.sum(weight_part * weight_part, axis=-1, keepdims=True)) / jnp.sqrt(
            jnp.sum(step_part * step_part, axis=-1, keepdims=True)
        )

    lead_ratio = ratio_of(
        vector[:, :head_part].reshape(depth_count, 8, D),
        direction[:, :head_part].reshape(depth_count, 8, D),
    )
    tail_ratio = ratio_of(vector[:, head_part:], direction[:, head_part:])
    trust_ratio = jnp.concatenate(
        [
            jnp.broadcast_to(lead_ratio, (depth_count, 8, D)).reshape(depth_count, head_part),
            jnp.broadcast_to(tail_ratio, (depth_count, FF)),
        ],
        axis=1,
    )
    return (first_new, second_new, vector - 0.5 * trust_ratio * direction)


def per_device_any(
    hidden_in,
    cotangent,
    segment_ids,
    w_qkv,
    w_out,
    w_up,
    w_down,
    vectors,
    m_qkv,
    v_qkv,
    m_out,
    v_out,
    m_up,
    v_up,
    m_down,
    v_down,
    m_vectors,
    v_vectors,
):
    tokens = hidden_in.shape[0]
    depth_count = w_qkv.shape[0]
    group_ids = segment_ids[0]
    own_ids = lax.dynamic_slice_in_dim(group_ids, lax.axis_index("col") * tokens, tokens)
    allowed = own_ids[:, None] == group_ids[None, :]

    def gather_weights(layer_at):
        qkv_raw = w_qkv[layer_at].astype(jnp.bfloat16)
        out_raw = w_out[layer_at].astype(jnp.bfloat16)
        up_raw = w_up[layer_at].astype(jnp.bfloat16)
        down_raw = w_down[layer_at].astype(jnp.bfloat16)
        qkv_cols, out_cols, up_cols, down_cols = (
            lax.all_gather(qkv_raw, "col", axis=1, tiled=True),
            lax.all_gather(out_raw, "col", axis=1, tiled=True),
            lax.all_gather(up_raw, "col", axis=1, tiled=True),
            lax.all_gather(down_raw, "col", axis=0, tiled=True),
        )
        return (
            lax.all_gather(qkv_cols, "row", axis=0, tiled=True),
            lax.all_gather(out_cols, "row", axis=0, tiled=True),
            lax.all_gather(up_cols, "row", axis=0, tiled=True),
            lax.all_gather(down_cols, "row", axis=1, tiled=True),
        )

    current = hidden_in.astype(jnp.float32)
    layer_inputs = []
    kept_runs = []
    kept_weights = []
    for layer_at in range(depth_count):
        weights = gather_weights(layer_at)
        layer_inputs.append(current)
        current, kept_vals = layer_forward(current, weights, vectors[layer_at], allowed, None)
        kept_runs.append(kept_vals)
        kept_weights.append(weights)
    grad_current = cotangent
    grads_by_layer = [None] * depth_count
    vector_grads = [None] * depth_count
    for layer_at in reversed(range(depth_count)):
        weights = gather_weights(layer_at)
        unused_out, kept_vals = layer_forward(
            layer_inputs[layer_at], weights, vectors[layer_at], allowed, kept_runs[layer_at][3]
        )
        grad_current, matrix_grads, vector_grad = layer_backward(
            grad_current, layer_inputs[layer_at], kept_vals, weights, vectors[layer_at], allowed
        )
        rows_done = (
            lax.psum_scatter(
                matrix_grads[0].astype(jnp.bfloat16), "row", scatter_dimension=0, tiled=True
            ).astype(jnp.float32),
            lax.psum_scatter(
                matrix_grads[1].astype(jnp.bfloat16), "row", scatter_dimension=0, tiled=True
            ).astype(jnp.float32),
            lax.psum_scatter(
                matrix_grads[2].astype(jnp.bfloat16), "row", scatter_dimension=0, tiled=True
            ).astype(jnp.float32),
            lax.psum_scatter(
                matrix_grads[3].astype(jnp.bfloat16), "row", scatter_dimension=1, tiled=True
            ).astype(jnp.float32),
        )
        shards = (
            lax.psum_scatter(
                rows_done[0].astype(jnp.bfloat16), "col", scatter_dimension=1, tiled=True
            ).astype(jnp.float32),
            lax.psum_scatter(
                rows_done[1].astype(jnp.bfloat16), "col", scatter_dimension=1, tiled=True
            ).astype(jnp.float32),
            lax.psum_scatter(
                rows_done[2].astype(jnp.bfloat16), "col", scatter_dimension=1, tiled=True
            ).astype(jnp.float32),
            lax.psum_scatter(
                rows_done[3].astype(jnp.bfloat16), "col", scatter_dimension=0, tiled=True
            ).astype(jnp.float32),
        )
        grads_by_layer[layer_at] = shards
        vector_grads[layer_at] = vector_grad
    masters = (w_qkv, w_out, w_up, w_down)
    firsts = (m_qkv, m_out, m_up, m_down)
    seconds = (v_qkv, v_out, v_up, v_down)
    gradients = tuple(
        (
            jnp.stack([grads_by_layer[layer_at][kind] for layer_at in range(depth_count)])
            for kind in range(4)
        )
    )
    updates = [
        adam_direction(masters[kind], gradients[kind], firsts[kind], seconds[kind], 0.01)
        for kind in range(4)
    ]
    partial_sums = jnp.stack(
        [jnp.stack(matrix_sums(masters[kind], updates[kind][2]), axis=1) for kind in range(4)],
        axis=1,
    )
    grad_vectors, total_sums = lax.psum((jnp.stack(vector_grads), partial_sums), ("row", "col"))
    lamb_norms = jnp.sqrt(total_sums)
    trust_ratio = lamb_norms[:, :, 0] / lamb_norms[:, :, 1]
    new_masters = [
        masters[kind] - 0.5 * trust_ratio[:, kind, None, None] * updates[kind][2]
        for kind in range(4)
    ]
    vec_first, vec_second, new_vectors = vector_update(vectors, grad_vectors, m_vectors, v_vectors)
    return (
        current,
        grad_current,
        gradients[0],
        gradients[1],
        gradients[2],
        gradients[3],
        grad_vectors,
        updates[0][0],
        updates[0][1],
        updates[1][0],
        updates[1][1],
        updates[2][0],
        updates[2][1],
        updates[3][0],
        updates[3][1],
        vec_first,
        vec_second,
        new_masters[0],
        new_masters[1],
        new_masters[2],
        new_masters[3],
        new_vectors,
        new_masters[0].astype(jnp.bfloat16),
        new_masters[1].astype(jnp.bfloat16),
        new_masters[2].astype(jnp.bfloat16),
        new_masters[3].astype(jnp.bfloat16),
        lamb_norms,
    )


MESH = pl.DeviceIdType.MESH
F32 = jnp.float32
BF16 = jnp.bfloat16
NT = (((1,), (1,)), ((), ()))
CHUNK = 640
SCALE = HDIM ** (-0.5)
HEADS = 5
HW = HEADS * HDIM


def where_am_i():
    r = lax.axis_index("row")
    z = lax.axis_index("col")
    return r // 4, (r // 2) % 2, r % 2, z


def row_of(y, x, c):
    return (y * 2 + x) * 2 + c


def trade_partners(y, x, c, z):
    yf = y + (1 - c) * (1 - 2 * y)
    xf = x + c * (1 - 2 * x)
    yg = y + c * (1 - 2 * y)
    xg = x + (1 - c) * (1 - 2 * x)
    return (yf, xf), (yg, xg), (1 - y, 1 - x)


def greet(peers):
    barrier = pltpu.get_barrier_semaphore()
    for peer in peers:
        pl.semaphore_signal(barrier, inc=1, device_id=peer, device_id_type=MESH)
    pl.semaphore_wait(barrier, len(peers))


def remote(src, dst, send_sem, recv_sem, peer):
    return pltpu.make_async_remote_copy(
        src_ref=src, dst_ref=dst, send_sem=send_sem, recv_sem=recv_sem,
        device_id=peer, device_id_type=MESH,
    )


def rows_at(row):
    return pl.ds(pl.multiple_of(row * 80, 80), 80)


def gather_kernel(nchunks, s_ref, w_ref, zs, zr, ps, pr, own_sem):
    y, x, c, z = where_am_i()
    r = row_of(y, x, c)
    (yf, xf), (yg, xg), (yd, xd) = trade_partners(y, x, c, z)
    rf, rg, rd = row_of(yf, xf, c), row_of(yg, xg, c), row_of(yd, xd, c)
    zpeers = [(r, lax.rem(z + k, 4)) for k in (1, 2, 3)]
    pf, pg, sib = (rf, z), (rg, z), (row_of(y, x, 1 - c), z)
    per_layer = 3200 // CHUNK

    def cols(t):
        return t // per_layer, pl.ds((t % per_layer) * CHUNK, CHUNK)

    def zcopies(t):
        layer, cs = cols(t)
        src = s_ref.at[layer, :, cs]
        out = []
        for k in range(3):
            out.append(remote(src, w_ref.at[layer, z, rows_at(r), cs], zs.at[t, k], zr.at[t, k], zpeers[k]))
        return out

    def own(t):
        layer, cs = cols(t)
        return pltpu.make_async_copy(s_ref.at[layer, :, cs], w_ref.at[layer, z, rows_at(r), cs], own_sem.at[t])

    def block(t, row):
        layer, cs = cols(t)
        return w_ref.at[layer, :, rows_at(row), cs]

    def hop(t, which):
        row, peer = ((r, pf), (r, pg), (rf, pg), (r, sib), (rf, sib), (rg, sib), (rd, sib))[which]
        return remote(block(t, row), block(t, row), ps.at[t, which], pr.at[t, which], peer)

    greet(zpeers + [pf, pg, sib])

    def start_z(t):
        for cp in zcopies(t):
            cp.start()
        own(t).start()

    start_z(0)
    start_z(1)
    for t in range(nchunks + 3):
        if t < nchunks:
            for cp in zcopies(t):
                cp.wait()
            own(t).wait()
            if t + 2 < nchunks:
                start_z(t + 2)
            for which in (0, 1, 3):
                hop(t, which).start()
        if 0 <= t - 1 < nchunks:
            hop(t - 1, 0).wait()
            for which in (2, 4):
                hop(t - 1, which).start()
        if 0 <= t - 2 < nchunks:
            hop(t - 2, 1).wait()
            hop(t - 2, 2).wait()
            for which in (5, 6):
                hop(t - 2, which).start()
        if 0 <= t - 3 < nchunks:
            for which in (3, 4, 5, 6):
                hop(t - 3, which).wait()


def gather_weights_fast(shards):
    depth = shards.shape[0]
    n = depth * (3200 // CHUNK)
    return pl.pallas_call(
        partial(gather_kernel, n),
        name="gather",
        out_shape=jax.ShapeDtypeStruct((depth, 4, 640, 3200), BF16),
        in_specs=[pl.BlockSpec(memory_space=pl.ANY)],
        out_specs=pl.BlockSpec(memory_space=pl.ANY),
        scratch_shapes=[
            pltpu.SemaphoreType.DMA((n, 3)),
            pltpu.SemaphoreType.DMA((n, 3)),
            pltpu.SemaphoreType.DMA((n, 7)),
            pltpu.SemaphoreType.DMA((n, 7)),
            pltpu.SemaphoreType.DMA((n,)),
        ],
        compiler_params=pltpu.CompilerParams(collective_id=0, has_side_effects=True),
    )(shards)


def scatter_kernel(order, g_ref, out_ref, own, sibr, p2r, p1r, zr,
                   own_sem, s_send, s_recv, p2_send, p2_recv, p1_send, p1_recv, z_send, z_recv):
    y, x, c, z = where_am_i()
    r = row_of(y, x, c)
    (yf, xf), (yg, xg), (yd, xd) = trade_partners(y, x, c, z)
    q, qf, qg, qd = y * 2 + x, yf * 2 + xf, yg * 2 + xg, yd * 2 + xd
    zpeers = [(r, lax.rem(z + k, 4)) for k in (1, 2, 3)]
    pf, pg, sib = (qf * 2 + c, z), (qg * 2 + c, z), (row_of(y, x, 1 - c), z)
    greet(zpeers + [pf, pg, sib])
    n = len(order)

    def part(t, chip, core):
        return g_ref.at[:, rows_at(chip * 2 + core), pl.ds(order[t] * CHUNK, CHUNK)]

    def own_copy(t, chip):
        return pltpu.make_async_copy(part(t, chip, c), own.at[t, chip], own_sem.at[t, chip])

    def sib_copy(t, chip):
        return remote(part(t, chip, 1 - c), sibr.at[t, chip], s_send.at[t, chip], s_recv.at[t, chip], sib)

    def p2_copy(t, k):
        return remote(own.at[t, (qg, qd)[k]], p2r.at[t, k], p2_send.at[t, k], p2_recv.at[t, k], pg)

    def p1_copy(t):
        return remote(own.at[t, qf], p1r.at[t], p1_send.at[t], p1_recv.at[t], pf)

    def z_copy(t, k):
        return remote(own.at[t, q, lax.rem(z + k + 1, 4)], zr.at[t, k], z_send.at[t, k], z_recv.at[t, k], zpeers[k])

    def add(dst, src):
        dst[...] = (dst[...].astype(F32) + src[...].astype(F32)).astype(BF16)

    for t in range(n + 4):
        if t < n:
            for chip in range(4):
                sib_copy(t, chip).start()
                own_copy(t, chip).start()
        if 0 <= t - 1 < n:
            u = t - 1
            for chip in range(4):
                sib_copy(u, chip).wait()
                own_copy(u, chip).wait()

            @pl.loop(0, 4)
            def _(chip):
                add(own.at[u, chip], sibr.at[u, chip])

            for k in range(2):
                p2_copy(u, k).start()
        if 0 <= t - 2 < n:
            u = t - 2
            for k in range(2):
                p2_copy(u, k).wait()
            add(own.at[u, q], p2r.at[u, 0])
            add(own.at[u, qf], p2r.at[u, 1])
            p1_copy(u).start()
        if 0 <= t - 3 < n:
            u = t - 3
            p1_copy(u).wait()
            add(own.at[u, q], p1r.at[u])
            for k in range(3):
                z_copy(u, k).start()
        if 0 <= t - 4 < n:
            u = t - 4
            for k in range(3):
                z_copy(u, k).wait()
            total = own[u, q, z].astype(F32)
            for k in range(3):
                total = total + zr[u, k].astype(F32)
            out_ref[:, order[u] * CHUNK : (order[u] + 1) * CHUNK] = total


def scatter_grads(grads, order, cid):
    n = len(order)
    dma = pltpu.SemaphoreType.DMA
    return pl.pallas_call(
        partial(scatter_kernel, order),
        name="scatter",
        out_shape=jax.ShapeDtypeStruct((80, n * CHUNK), F32),
        in_specs=[pl.BlockSpec(memory_space=pl.ANY)],
        out_specs=pl.BlockSpec(memory_space=pltpu.VMEM),
        scratch_shapes=[
            pltpu.VMEM((n, 4, 4, 80, CHUNK), BF16),
            pltpu.VMEM((n, 4, 4, 80, CHUNK), BF16),
            pltpu.VMEM((n, 2, 4, 80, CHUNK), BF16),
            pltpu.VMEM((n, 4, 80, CHUNK), BF16),
            pltpu.VMEM((n, 3, 80, CHUNK), BF16),
            dma((n, 4)), dma((n, 4)), dma((n, 4)),
            dma((n, 2)), dma((n, 2)), dma((n,)), dma((n,)), dma((n, 3)), dma((n, 3)),
        ],
        compiler_params=pltpu.CompilerParams(
            collective_id=cid, has_side_effects=True, vmem_limit_bytes=48 << 20
        ),
    )(grads)


def total_kernel(x_ref, o_ref, got, send, recv):
    y, x, c, z = where_am_i()
    peers = [
        (row_of(y, x, 1 - c), z),
        (row_of(y, 1 - x, c), z),
        (row_of(1 - y, x, c), z),
        (row_of(y, x, c), z + 1 - 2 * (z % 2)),
        (row_of(y, x, c), lax.rem(z + 2, 4)),
    ]
    greet(peers)
    o_ref[0] = x_ref[...]
    for step, peer in enumerate(peers):
        cp = remote(o_ref.at[step], got.at[step], send.at[step], recv.at[step], peer)
        cp.start()
        cp.wait()
        o_ref[step + 1] = o_ref[step] + got[step]


def total_over_devices(x, cid):
    return pl.pallas_call(
        total_kernel,
        name="total",
        out_shape=jax.ShapeDtypeStruct((6,) + x.shape, F32),
        in_specs=[pl.BlockSpec(memory_space=pltpu.VMEM)],
        out_specs=pl.BlockSpec(memory_space=pltpu.VMEM),
        scratch_shapes=[
            pltpu.VMEM((5,) + x.shape, F32),
            pltpu.SemaphoreType.DMA((5,)),
            pltpu.SemaphoreType.DMA((5,)),
        ],
        compiler_params=pltpu.CompilerParams(collective_id=cid, has_side_effects=True),
    )(x)[5]


def attention_peers(y, x, c, z):
    return c * 2 + z % 2, lambda b: (row_of(y, x, b // 2), (z // 2) * 2 + b % 2)


def norm_parts(values):
    average = jnp.mean(values, axis=-1, keepdims=True)
    centered = values - average
    variance = jnp.mean(centered * centered, axis=-1, keepdims=True)
    spread = lax.rsqrt(variance + 1e-05)
    return centered * spread, spread


def dot(a, b):
    return jnp.dot(a, b, preferred_element_type=F32)


def dot_nt(a, b):
    return lax.dot_general(a, b, NT, preferred_element_type=F32)


def piece(vec_ref, at, count=640):
    return vec_ref[0:1, at : at + count]


def exchange(me, peer_of, sbuf, rbuf, ss, rs):
    y, x, c, z = where_am_i()
    out = []
    for k in (1, 2, 3):
        b = lax.rem(me + k, 4)
        out.append(remote(sbuf.at[b], rbuf.at[me], ss.at[k], rs.at[k], peer_of(b)))
    for cp in out:
        cp.start()
    return out


def head_mask(h, rows):
    lane = lax.broadcasted_iota(jnp.int32, (rows, HW), 1)
    return (lane >= h * HDIM) & (lane < (h + 1) * HDIM)


QB = 256


def forward_kernel(layer, x_ref, vec_ref, segr_ref, segc_ref, w_ref,
                   xo_ref, xm_ref, o_ref, hdn_ref, gp_ref, q_ref, k_ref, v_ref, oh_ref, lse_ref,
                   wa, wb, wc, abuf, sbuf, rbuf, osbuf, orbuf, vt, ot,
                   wsem, ss, rs, oss, ors):
    y, x, c, z = where_am_i()
    me, peer_of = attention_peers(y, x, c, z)
    loads = [
        pltpu.make_async_copy(w_ref.at[layer, :, :, pl.ds(0, 640)], wa, wsem.at[0]),
        pltpu.make_async_copy(w_ref.at[layer, :, :, pl.ds(640, 1280)], wb, wsem.at[1]),
        pltpu.make_async_copy(w_ref.at[layer, :, :, pl.ds(1920, 1280)], wc, wsem.at[2]),
    ]
    for load in loads:
        load.start()
    greet([peer_of(lax.rem(me + k, 4)) for k in (1, 2, 3)])

    n1, _ = norm_parts(x_ref[...])
    a = (n1 * piece(vec_ref, 0) + piece(vec_ref, 640)).astype(BF16)
    loads[0].wait()
    parts = [dot(a, wa[i, :, 0:512])[:, 0:480] for i in range(4)]
    blocks = [parts[b // 3][:, (b % 3) * HW : (b % 3 + 1) * HW] for b in range(12)]
    pad = jnp.zeros((320, 32), F32)
    for b in range(4):
        q = blocks[b] + vec_ref[0:1, 1280 + HW * b : 1280 + HW * (b + 1)]
        v = blocks[8 + b] + vec_ref[0:1, 1920 + HW * b : 1920 + HW * (b + 1)]
        sbuf[b] = jnp.concatenate([q, blocks[4 + b], v, pad], axis=1).astype(BF16)
    copies = exchange(me, peer_of, sbuf, rbuf, ss, rs)
    rbuf[me] = sbuf[me]
    for cp in copies:
        cp.wait()

    for b in range(4):
        rows = slice(320 * b, 320 * (b + 1))
        got = rbuf[b].astype(F32)
        q_ref[rows, :] = got[:, 0:HW].astype(BF16)
        k_ref[rows, :] = got[:, HW : 2 * HW].astype(BF16)
        v_ref[rows, :] = got[:, 2 * HW : 3 * HW].astype(BF16)
    vt[...] = v_ref[...].astype(F32).T.astype(BF16)
    lse_ref[...] = jnp.zeros_like(lse_ref)

    @pl.loop(0, 25)
    def _(step):
        h = step // 5
        at = pl.multiple_of((step % 5) * QB, QB)
        qm = jnp.where(head_mask(h, QB), q_ref[pl.ds(at, QB), :], jnp.zeros((), BF16))
        s = dot_nt(k_ref[...], qm) * SCALE
        s = jnp.where(segc_ref[...] == segr_ref[0:1, pl.ds(at, QB)], s, negative)
        top = jnp.max(s, axis=0, keepdims=True)
        p = jnp.exp(s - top)
        total = jnp.sum(p, axis=0, keepdims=True)
        rows = pl.ds(pl.multiple_of(h * HDIM, HDIM), HDIM)
        ot[rows, pl.ds(at, QB)] = dot(vt[rows, :], p.astype(BF16)) / total
        lse_ref[pl.ds(h, 1), pl.ds(at, QB)] = top + jnp.log(total)

    oh_ref[...] = ot[...].T.astype(BF16)
    for b in range(4):
        osbuf[b] = oh_ref[320 * b : 320 * (b + 1), :]
    copies = exchange(me, peer_of, osbuf, orbuf, oss, ors)
    orbuf[me] = osbuf[me]
    for cp in copies:
        cp.wait()
    o = jnp.concatenate([orbuf[b].astype(F32) for b in range(4)], axis=1).astype(BF16)
    o_ref[...] = o
    yv = jnp.concatenate([dot(o, wa[i, :, 384:640])[:, 96:256] for i in range(4)], axis=1)
    xm = x_ref[...] + (yv + piece(vec_ref, 2560))
    xm_ref[...] = xm
    n2, _ = norm_parts(xm)
    abuf[...] = (n2 * piece(vec_ref, 3200) + piece(vec_ref, 3840)).astype(BF16)
    loads[1].wait()

    @pl.loop(0, 20)
    def _(step):
        i = step // 5
        at = pl.multiple_of((step % 5) * 256, 256)
        to = pl.multiple_of(step * 256, 256)
        u = dot(abuf[...], wb[i, :, pl.ds(at, 256)]) + vec_ref[0:1, pl.ds(5120 + to, 256)]
        cdf = 0.5 * (1.0 + lax.erf(u * (0.5**0.5)))
        hdn_ref[:, pl.ds(to, 256)] = (u * cdf).astype(BF16)
        gp_ref[:, pl.ds(to, 256)] = (cdf + u * (jnp.exp(-0.5 * u * u) * 0.3989422804014327)).astype(BF16)

    loads[2].wait()
    yv = dot_nt(hdn_ref[:, 0:1280], wc[0])
    for i in range(1, 4):
        yv = yv + dot_nt(hdn_ref[:, 1280 * i : 1280 * (i + 1)], wc[i])
    xo_ref[...] = xm + (yv + piece(vec_ref, 4480))


VM = pl.BlockSpec(memory_space=pltpu.VMEM)
ANY = pl.BlockSpec(memory_space=pl.ANY)


def forward_layer(x, vec, segr, segc, weights, layer, cid):
    dma = pltpu.SemaphoreType.DMA
    sds = jax.ShapeDtypeStruct
    return pl.pallas_call(
        partial(forward_kernel, layer),
        name="forward",
        out_shape=(
            sds((320, 640), F32), sds((320, 640), F32), sds((320, 640), BF16),
            sds((320, 5120), BF16), sds((320, 5120), BF16),
            sds((1280, HW), BF16), sds((1280, HW), BF16), sds((1280, HW), BF16), sds((1280, HW), BF16),
            sds((8, 1280), F32),
        ),
        in_specs=[VM, VM, VM, VM, ANY],
        out_specs=(VM,) * 10,
        scratch_shapes=[
            pltpu.VMEM((4, 640, 640), BF16), pltpu.VMEM((4, 640, 1280), BF16), pltpu.VMEM((4, 640, 1280), BF16),
            pltpu.VMEM((320, 640), BF16),
            pltpu.VMEM((4, 320, 512), BF16), pltpu.VMEM((4, 320, 512), BF16),
            pltpu.VMEM((4, 320, HW), BF16), pltpu.VMEM((4, 320, HW), BF16),
            pltpu.VMEM((HW, 1280), BF16), pltpu.VMEM((HW, 1280), F32),
            dma((3,)), dma((4,)), dma((4,)), dma((4,)), dma((4,)),
        ],
        compiler_params=pltpu.CompilerParams(
            collective_id=cid, has_side_effects=True, vmem_limit_bytes=56 << 20
        ),
    )(x, vec, segr, segc, weights)


def norm_back(dy, n, spread, gain):
    dn = dy * gain
    mean1 = jnp.mean(dn, axis=-1, keepdims=True)
    mean2 = jnp.mean(dn * n, axis=-1, keepdims=True)
    return spread * (dn - mean1 - n * mean2)


def col_sum(values):
    return jnp.sum(values, axis=0, keepdims=True)


def backward_kernel(layer, dx_ref, x_ref, xm_ref, o_ref, hdn_ref, gp_ref, q_ref, k_ref, v_ref, oh_ref, lse_ref,
                    vec_ref, segr_ref, segc_ref, w_ref,
                    dxo_ref, gv_ref, g_ref,
                    wa, wb, wc, gbuf, at_s, dy, dyt, da2, dosend, dorecv, dos, kt, dqt, dk, dv, delta, psend, precv,
                    wsem, gsem, ss, rs, oss, ors):
    y, x, c, z = where_am_i()
    me, peer_of = attention_peers(y, x, c, z)
    loads = [
        pltpu.make_async_copy(w_ref.at[layer, :, :, pl.ds(0, 640)], wa, wsem.at[0]),
        pltpu.make_async_copy(w_ref.at[layer, :, :, pl.ds(640, 1280)], wb, wsem.at[1]),
        pltpu.make_async_copy(w_ref.at[layer, :, :, pl.ds(1920, 1280)], wc, wsem.at[2]),
    ]
    for load in (loads[2], loads[1], loads[0]):
        load.start()
    greet([peer_of(lax.rem(me + k, 4)) for k in (1, 2, 3)])

    dx_out = dx_ref[...]
    dy[...] = dx_out.astype(BF16)
    dyf = dy[...].astype(F32)
    dyt[...] = dyf.T.astype(BF16)
    gv_ref[0:1, 4480:5120] = col_sum(dyf)
    n2, spread2 = norm_parts(xm_ref[...])
    g2 = piece(vec_ref, 3200)
    at_s[...] = (n2 * g2 + piece(vec_ref, 3840)).T.astype(BF16)
    da2[...] = jnp.zeros_like(da2)
    loads[2].wait()
    loads[1].wait()

    def put(slot, i, col):
        return pltpu.make_async_copy(gbuf.at[slot], g_ref.at[i, :, pl.ds(col, 256)], gsem.at[slot])

    @pl.loop(0, 20)
    def _(step):
        i = step // 5
        at = pl.multiple_of((step % 5) * 256, 256)
        to = pl.multiple_of(step * 256, 256)

        @pl.when(step > 0)
        def _():
            put(0, 0, 0).wait()
            put(1, 0, 0).wait()

        hdn = hdn_ref[:, pl.ds(to, 256)]
        gbuf[0] = dot(dyt[...], hdn).astype(BF16)
        put(0, i, 1920 + at).start()
        dh = dot(dy[...], wc[i, :, pl.ds(at, 256)])
        du = (dh * gp_ref[:, pl.ds(to, 256)].astype(F32)).astype(BF16)
        gv_ref[0:1, pl.ds(5120 + to, 256)] = col_sum(du.astype(F32))
        gbuf[1] = dot(at_s[...], du).astype(BF16)
        put(1, i, 640 + at).start()
        da2[...] += dot_nt(du, wb[i, :, pl.ds(at, 256)])

    put(0, 0, 0).wait()
    put(1, 0, 0).wait()
    da2v = da2[...]
    gv_ref[0:1, 3200:3840] = col_sum(da2v * n2)
    gv_ref[0:1, 3840:4480] = col_sum(da2v)
    dxm = dx_out + norm_back(da2v, n2, spread2, g2)
    dy1f = dxm.astype(BF16).astype(F32)
    gv_ref[0:1, 2560:3200] = col_sum(dy1f)
    loads[0].wait()
    zpad = jnp.zeros((320, 96), F32)
    dof = None
    for i in range(4):
        dpad = jnp.concatenate([zpad, dy1f[:, HW * i : HW * (i + 1)]], axis=1).astype(BF16)
        term = dot_nt(dpad, wa[i, :, 384:640])
        dof = term if dof is None else dof + term
    for b in range(4):
        dosend[b] = dof[:, HW * b : HW * (b + 1)].astype(BF16)
    copies = exchange(me, peer_of, dosend, dorecv, oss, ors)
    dorecv[me] = dosend[me]
    kt[...] = k_ref[...].astype(F32).T.astype(BF16)
    dk[...] = jnp.zeros_like(dk)
    dv[...] = jnp.zeros_like(dv)
    for cp in copies:
        cp.wait()
    for b in range(4):
        dos[320 * b : 320 * (b + 1), :] = dorecv[b]
    lane = lax.broadcasted_iota(jnp.int32, (8, HW), 1)
    head = lax.broadcasted_iota(jnp.int32, (8, HW), 0)
    pick = jnp.where((lane >= head * HDIM) & (lane < (head + 1) * HDIM), 1.0, 0.0).astype(F32)
    delta[...] = lax.dot_general(
        pick, dos[...].astype(F32) * oh_ref[...].astype(F32), NT,
        precision=lax.Precision.HIGHEST, preferred_element_type=F32,
    )

    @pl.loop(0, 25)
    def _(step):
        h = step // 5
        at = pl.multiple_of((step % 5) * QB, QB)
        zero = jnp.zeros((), BF16)
        mask = head_mask(h, QB)
        qm = jnp.where(mask, q_ref[pl.ds(at, QB), :], zero)
        dm = jnp.where(mask, dos[pl.ds(at, QB), :], zero)
        s = dot_nt(k_ref[...], qm) * SCALE
        s = jnp.where(segc_ref[...] == segr_ref[0:1, pl.ds(at, QB)], s, negative)
        p = jnp.exp(s - lse_ref[pl.ds(h, 1), pl.ds(at, QB)])
        dp = dot_nt(v_ref[...], dm)
        ds = (p * (dp - delta[pl.ds(h, 1), pl.ds(at, QB)])).astype(BF16)
        dv[...] += dot(p.astype(BF16), dm)
        dk[...] += dot(ds, qm)
        rows = pl.ds(pl.multiple_of(h * HDIM, HDIM), HDIM)
        dqt[rows, pl.ds(at, QB)] = dot(kt[rows, :], ds)

    dq = dqt[...].T * SCALE
    zpad = jnp.zeros((320, 32), F32)
    for b in range(4):
        rows = slice(320 * b, 320 * (b + 1))
        psend[b] = jnp.concatenate([dq[rows], dk[rows, :] * SCALE, dv[rows, :], zpad], axis=1).astype(BF16)
    copies = exchange(me, peer_of, psend, precv, ss, rs)
    precv[me] = psend[me]
    n1, spread1 = norm_parts(x_ref[...])
    g1 = piece(vec_ref, 0)
    at_s[...] = (n1 * g1 + piece(vec_ref, 640)).T.astype(BF16)
    otr = o_ref[...].astype(F32).T.astype(BF16)
    gos = [dot(otr, dy1f[:, HW * i : HW * (i + 1)].astype(BF16)) for i in range(4)]
    for cp in copies:
        cp.wait()
    got = [precv[b].astype(F32) for b in range(4)]
    gv_ref[0:1, 1280:1920] = jnp.concatenate([col_sum(got[b][:, 0:HW]) for b in range(4)], axis=1)
    gv_ref[0:1, 1920:2560] = jnp.concatenate([col_sum(got[b][:, 2 * HW : 3 * HW]) for b in range(4)], axis=1)
    blocks = [got[b % 4][:, (b // 4) * HW : (b // 4 + 1) * HW] for b in range(12)]
    da = None
    for i in range(4):
        dpi = jnp.concatenate(blocks[3 * i : 3 * i + 3] + [zpad], axis=1).astype(BF16)
        wa_g = jnp.concatenate([dot(at_s[...], dpi)[:, 0:480], gos[i]], axis=1).astype(BF16)
        term = dot_nt(dpi, wa[i, :, 0:512])
        da = term if da is None else da + term
        wa[i] = wa_g
    last = pltpu.make_async_copy(wa, g_ref.at[:, :, pl.ds(0, 640)], wsem.at[0])
    last.start()
    gv_ref[0:1, 0:640] = col_sum(da * n1)
    gv_ref[0:1, 640:1280] = col_sum(da)
    dxo_ref[...] = dxm + norm_back(da, n1, spread1, g1)
    last.wait()


def backward_layer(dx, x, kept, vec, segr, segc, weights, layer, cid):
    dma = pltpu.SemaphoreType.DMA
    sds = jax.ShapeDtypeStruct
    return pl.pallas_call(
        partial(backward_kernel, layer),
        name="backward",
        out_shape=(sds((320, 640), F32), sds((1, 10240), F32), sds((4, 640, 3200), BF16)),
        in_specs=[VM] * 14 + [ANY],
        out_specs=(VM, VM, ANY),
        scratch_shapes=[
            pltpu.VMEM((4, 640, 640), BF16), pltpu.VMEM((4, 640, 1280), BF16), pltpu.VMEM((4, 640, 1280), BF16),
            pltpu.VMEM((2, 640, 256), BF16),
            pltpu.VMEM((640, 320), BF16),
            pltpu.VMEM((320, 640), BF16), pltpu.VMEM((640, 320), BF16), pltpu.VMEM((320, 640), F32),
            pltpu.VMEM((4, 320, HW), BF16), pltpu.VMEM((4, 320, HW), BF16), pltpu.VMEM((1280, HW), BF16),
            pltpu.VMEM((HW, 1280), BF16), pltpu.VMEM((HW, 1280), F32),
            pltpu.VMEM((1280, HW), F32), pltpu.VMEM((1280, HW), F32), pltpu.VMEM((8, 1280), F32),
            pltpu.VMEM((4, 320, 512), BF16), pltpu.VMEM((4, 320, 512), BF16),
            dma((3,)), dma((2,)), dma((4,)), dma((4,)), dma((4,)), dma((4,)),
        ],
        compiler_params=pltpu.CompilerParams(
            collective_id=cid, has_side_effects=True, vmem_limit_bytes=58 << 20
        ),
    )(dx, x, *kept, vec, segr, segc, weights)


def device_index(y, x, c, z):
    return row_of(y, x, c) * 4 + z


def token_moves():
    there = []
    for y in range(2):
        for x in range(2):
            for c in range(2):
                for b in range(4):
                    there.append((device_index(y, x, c, b), device_index(y, x, b // 2, 2 * c + b % 2)))
    return there, [(t, s) for s, t in there]


def per_device_fast(
    hidden_in, cotangent, segment_ids, w_qkv, w_out, w_up, w_down, vectors,
    m_qkv, v_qkv, m_out, v_out, m_up, v_up, m_down, v_down, m_vectors, v_vectors,
):
    depth = w_qkv.shape[0]
    both = ("row", "col")
    there, back = token_moves()
    swap = [(device_index(y, x, c, z), device_index(y, x, 1 - c, z))
            for y in range(2) for x in range(2) for c in range(2) for z in range(4)]
    shards = jnp.concatenate(
        [w_qkv.astype(BF16), w_out.astype(BF16), w_up.astype(BF16), w_down.astype(BF16).transpose(0, 2, 1)], axis=2
    )
    x = lax.ppermute(hidden_in, both, there).astype(F32)
    dx = lax.ppermute(cotangent, both, there)
    other_ids = lax.ppermute(segment_ids, both, swap)
    core = lax.axis_index("row") % 2
    segr = jnp.where(core == lax.axis_index("col") // 2, segment_ids, other_ids)
    segc = segr.reshape(-1, 1)
    weights = gather_weights_fast(shards)
    inputs, kepts = [], []
    for layer in range(depth):
        inputs.append(x)
        x, *kept = forward_layer(x, vectors[layer : layer + 1], segr, segc, weights, layer, 1 + layer)
        kepts.append(kept)
    grads, vector_grads = [None] * depth, [None] * depth
    order = (3, 4, 1, 2, 0)
    for layer in reversed(range(depth)):
        dx, vector_grads[layer], full = backward_layer(
            dx, inputs[layer], kepts[layer], vectors[layer : layer + 1], segr, segc, weights, layer, 3 + layer
        )
        grads[layer] = scatter_grads(full, order, 5)
    hidden_out = lax.ppermute(x, both, back)
    grad_in = lax.ppermute(dx, both, back)
    grad_all = jnp.stack(grads)
    gradients = (
        grad_all[:, :, 0:480], grad_all[:, :, 480:640], grad_all[:, :, 640:1920],
        grad_all[:, :, 1920:3200].transpose(0, 2, 1),
    )
    grad_vectors = total_over_devices(jnp.concatenate(vector_grads, axis=1).reshape(-1, 128), 6).reshape(depth, -1)
    masters = (w_qkv, w_out, w_up, w_down)
    firsts = (m_qkv, m_out, m_up, m_down)
    seconds = (v_qkv, v_out, v_up, v_down)
    updates = [
        adam_direction(masters[kind], gradients[kind], firsts[kind], seconds[kind], 0.01) for kind in range(4)
    ]
    partial_sums = jnp.stack(
        [jnp.stack(matrix_sums(masters[kind], updates[kind][2]), axis=1) for kind in range(4)], axis=1
    )
    flat = jnp.pad(partial_sums.reshape(1, -1), ((0, 7), (0, 128 - partial_sums.size)))
    total_sums = total_over_devices(flat, 7)[0, : partial_sums.size].reshape(partial_sums.shape)
    lamb_norms = jnp.sqrt(total_sums)
    trust_ratio = lamb_norms[:, :, 0] / lamb_norms[:, :, 1]
    new_masters = [
        masters[kind] - 0.5 * trust_ratio[:, kind, None, None] * updates[kind][2] for kind in range(4)
    ]
    vec_first, vec_second, new_vectors = vector_update(vectors, grad_vectors, m_vectors, v_vectors)
    moments = [part for kind in range(4) for part in updates[kind][:2]]
    return (
        hidden_out, grad_in, *gradients, grad_vectors, *moments, vec_first, vec_second,
        *new_masters, new_vectors, *[w.astype(BF16) for w in new_masters], lamb_norms,
    )


def solution(mesh):
    fast = mesh.shape["row"] == 8 and mesh.shape["col"] == 4
    per_device = per_device_fast if fast else per_device_any
    return jax.shard_map(
        per_device,
        mesh=mesh,
        in_specs=(
            P(("row", "col"), None),
            P(("row", "col"), None),
            P("row", None),
            P(None, "row", "col"),
            P(None, "row", "col"),
            P(None, "row", "col"),
            P(None, "col", "row"),
            P(),
            P(None, "row", "col"),
            P(None, "row", "col"),
            P(None, "row", "col"),
            P(None, "row", "col"),
            P(None, "row", "col"),
            P(None, "row", "col"),
            P(None, "col", "row"),
            P(None, "col", "row"),
            P(),
            P(),
        ),
        out_specs=(
            P(("row", "col"), None),
            P(("row", "col"), None),
            P(None, "row", "col"),
            P(None, "row", "col"),
            P(None, "row", "col"),
            P(None, "col", "row"),
            P(),
            P(None, "row", "col"),
            P(None, "row", "col"),
            P(None, "row", "col"),
            P(None, "row", "col"),
            P(None, "row", "col"),
            P(None, "row", "col"),
            P(None, "col", "row"),
            P(None, "col", "row"),
            P(),
            P(),
            P(None, "row", "col"),
            P(None, "row", "col"),
            P(None, "row", "col"),
            P(None, "col", "row"),
            P(),
            P(None, "row", "col"),
            P(None, "row", "col"),
            P(None, "row", "col"),
            P(None, "col", "row"),
            P(),
        ),
        check_vma=False,
    )
```

```python
import functools
from functools import partial

import jax
import jax.numpy as jnp
from jax import lax
from jax.experimental import pallas as pl
from jax.experimental.pallas import tpu as pltpu
from jax.sharding import PartitionSpec as P

D = 640
HDIM = 32
FF = 5120
STEP = 5


head_groups = 4
negative = -1e30


def layer_norm(values_in, norm_gain, norm_bias):
    average = jnp.mean(values_in, axis=-1, keepdims=True)
    centered = values_in - average
    variance = jnp.mean(centered * centered, axis=-1, keepdims=True)
    return centered * lax.rsqrt(variance + 1e-05) * norm_gain + norm_bias


def to_groups(matrix):
    tokens = matrix.shape[0]
    return matrix.reshape(tokens, head_groups, -1, HDIM).transpose(1, 2, 0, 3)


def from_groups(blocks):
    return blocks.transpose(2, 0, 1, 3).reshape(blocks.shape[2], -1)


def contract_rows(left, right):
    return lax.dot_general(
        left, right, (((0,), (0,)), ((), ())), preferred_element_type=jnp.float32
    )


def contract_cols(left, right):
    return lax.dot_general(
        left, right, (((1,), (1,)), ((), ())), preferred_element_type=jnp.float32
    )


def column_total(matrix):
    return jnp.sum(matrix.astype(jnp.float32), axis=0)


def masked_scores(query_block, key_block, allowed):
    scores = jnp.einsum(
        "hqd,hkd->hqk", query_block, key_block, preferred_element_type=jnp.float32
    ) * HDIM ** (-0.5)
    return jnp.where(allowed[None, :, :], scores, negative)


def attend(queries, all_kv, allowed, kept_lse):
    features = queries.shape[1]
    tokens = queries.shape[0]
    q_groups = to_groups(queries)
    k_groups = to_groups(all_kv[:, :features])
    v_groups = to_groups(all_kv[:, features:])
    if kept_lse is None:

        def first_group(members):
            q_block, k_block, v_block = members
            scores = masked_scores(q_block, k_block, allowed)
            row_max = jnp.max(scores, axis=-1)
            log_total = row_max + jnp.log(jnp.sum(jnp.exp(scores - row_max[..., None]), axis=-1))
            softmax = jnp.exp(scores - log_total[..., None]).astype(jnp.bfloat16)
            return (
                jnp.einsum("hqk,hkd->hqd", softmax, v_block, preferred_element_type=jnp.float32),
                log_total,
            )

        attended, log_total = lax.map(first_group, (q_groups, k_groups, v_groups))
    else:
        log_total = kept_lse.reshape(head_groups, -1, tokens)

        def again_group(members):
            q_block, k_block, v_block, lse_block = members
            softmax = jnp.exp(
                masked_scores(q_block, k_block, allowed) - lse_block[..., None]
            ).astype(jnp.bfloat16)
            return jnp.einsum("hqk,hkd->hqd", softmax, v_block, preferred_element_type=jnp.float32)

        attended = lax.map(again_group, (q_groups, k_groups, v_groups, log_total))
    return (from_groups(attended).astype(jnp.bfloat16), log_total.reshape(-1, tokens))


def attention_back(queries, all_kv, grad_mixed, kept_lse, allowed):
    features = queries.shape[1]
    tokens = queries.shape[0]
    inv_root = HDIM ** (-0.5)
    q_groups = to_groups(queries)
    k_groups = to_groups(all_kv[:, :features])
    v_groups = to_groups(all_kv[:, features:])
    g_groups = to_groups(grad_mixed)
    lse_groups = kept_lse.reshape(head_groups, -1, tokens)

    def one_group(members):
        q_block, k_block, v_block, g_block, lse_block = members
        softmax = jnp.exp(masked_scores(q_block, k_block, allowed) - lse_block[..., None])
        grad_probs = jnp.einsum(
            "hqd,hkd->hqk", g_block, v_block, preferred_element_type=jnp.float32
        )
        row_dot = jnp.sum(softmax * grad_probs, axis=-1, keepdims=True)
        grad_scores = (softmax * (grad_probs - row_dot)).astype(jnp.bfloat16)
        grad_q = (
            jnp.einsum("hqk,hkd->hqd", grad_scores, k_block, preferred_element_type=jnp.float32)
            * inv_root
        )
        grad_k = (
            jnp.einsum("hqk,hqd->hkd", grad_scores, q_block, preferred_element_type=jnp.float32)
            * inv_root
        )
        grad_v = jnp.einsum(
            "hqk,hqd->hkd",
            softmax.astype(jnp.bfloat16),
            g_block,
            preferred_element_type=jnp.float32,
        )
        return (grad_q, grad_k, grad_v)

    grad_q, grad_k, grad_v = lax.map(
        one_group, (q_groups, k_groups, v_groups, g_groups, lse_groups)
    )
    return (
        from_groups(grad_q),
        jnp.concatenate([from_groups(grad_k), from_groups(grad_v)], axis=1),
    )


def layer_forward(state_in, weights, vector, allowed, kept_lse):
    w_qkv_full, w_out_full, w_up_part, w_down_part = weights
    features = state_in.shape[1]
    normed = layer_norm(state_in, vector[0:features], vector[features : 2 * features]).astype(
        jnp.bfloat16
    )
    projected = jnp.dot(normed, w_qkv_full, preferred_element_type=jnp.float32)
    queries = (projected[:, :features] + vector[2 * features : 3 * features]).astype(jnp.bfloat16)
    kv_bias = jnp.concatenate(
        [jnp.zeros((features,), jnp.float32), vector[3 * features : 4 * features]]
    )
    own_kv = (projected[:, features:] + kv_bias).astype(jnp.bfloat16)
    all_kv = lax.all_gather(own_kv, "col", axis=0, tiled=True)
    attended, log_total = attend(queries, all_kv, allowed, kept_lse)
    middle = state_in + (
        jnp.dot(attended, w_out_full, preferred_element_type=jnp.float32)
        + vector[4 * features : 5 * features]
    )
    normed_ffn = layer_norm(
        middle, vector[5 * features : 6 * features], vector[6 * features : 7 * features]
    ).astype(jnp.bfloat16)
    before = (
        jnp.dot(normed_ffn, w_up_part, preferred_element_type=jnp.float32) + vector[8 * features :]
    )
    hidden = jax.nn.gelu(before, approximate=False).astype(jnp.bfloat16)
    branch = jnp.dot(hidden, w_down_part, preferred_element_type=jnp.float32)
    state_out = middle + (branch + vector[7 * features : 8 * features])
    kept_vals = (normed, queries, all_kv, log_total, attended, middle, normed_ffn, before, hidden)
    return (state_out, kept_vals)


def layer_backward(grad_state, state_in, kept_vals, weights, vector, allowed):
    w_qkv_full, w_out_full, w_up_part, w_down_part = weights
    normed, queries, all_kv, log_total, attended, middle, ffn_rows, before, hidden = kept_vals
    features = state_in.shape[1]
    grad_branch = grad_state.astype(jnp.bfloat16)
    gelu_vjp = jax.vjp(partial(jax.nn.gelu, approximate=False), before)[1]
    grad_down = contract_rows(hidden, grad_branch)
    grad_before = gelu_vjp(contract_cols(grad_branch, w_down_part))[0].astype(jnp.bfloat16)
    grad_up = contract_rows(ffn_rows, grad_before)
    grad_up_bias = column_total(grad_before)
    grad_normed_ffn = contract_cols(grad_before, w_up_part)
    norm_two = jax.vjp(
        layer_norm, middle, vector[5 * features : 6 * features], vector[6 * features : 7 * features]
    )[1]
    grad_middle_norm, grad_gain_two, grad_bias_two = norm_two(grad_normed_ffn)
    grad_middle = grad_state + grad_middle_norm
    grad_attn_out = grad_middle.astype(jnp.bfloat16)
    grad_out_w = contract_rows(attended, grad_attn_out)
    grad_mixed = contract_cols(grad_attn_out, w_out_full).astype(jnp.bfloat16)
    grad_queries, kv_terms = attention_back(queries, all_kv, grad_mixed, log_total, allowed)
    grad_kv = lax.psum_scatter(
        kv_terms.astype(jnp.bfloat16), "col", scatter_dimension=0, tiled=True
    )
    grad_queries = grad_queries.astype(jnp.bfloat16)
    grad_proj = jnp.concatenate([grad_queries, grad_kv], axis=1)
    grad_qkv_w = contract_rows(normed, grad_proj)
    grad_normed = contract_cols(grad_proj, w_qkv_full)
    norm_one = jax.vjp(layer_norm, state_in, vector[0:features], vector[features : 2 * features])[1]
    grad_input_norm, grad_gain_one, grad_bias_one = norm_one(grad_normed)
    grad_input = grad_middle + grad_input_norm
    grad_vector = jnp.concatenate(
        [
            grad_gain_one,
            grad_bias_one,
            column_total(grad_queries),
            column_total(grad_kv[:, features:]),
            column_total(grad_attn_out),
            grad_gain_two,
            grad_bias_two,
            column_total(grad_branch),
            grad_up_bias,
        ]
    )
    return (grad_input, (grad_qkv_w, grad_out_w, grad_up, grad_down), grad_vector)


def adam_direction(weight, gradient, first_mom, second_mom, decay_rate):
    first_new = 0.9 * first_mom + 0.1 * gradient
    second_new = 0.999 * second_mom + 0.001 * gradient * gradient
    direction = (
        first_new / (1.0 - 0.9**STEP) / (jnp.sqrt(second_new / (1.0 - 0.999**STEP)) + 1e-06)
        + decay_rate * weight
    )
    return (first_new, second_new, direction)


def matrix_sums(weight, direction):
    return (jnp.sum(weight * weight, axis=(1, 2)), jnp.sum(direction * direction, axis=(1, 2)))


def vector_update(vector, gradient, first_mom, second_mom):
    first_new, second_new, direction = adam_direction(vector, gradient, first_mom, second_mom, 0.0)
    depth_count = vector.shape[0]
    head_part = 8 * D

    def ratio_of(weight_part, step_part):
        return jnp.sqrt(jnp.sum(weight_part * weight_part, axis=-1, keepdims=True)) / jnp.sqrt(
            jnp.sum(step_part * step_part, axis=-1, keepdims=True)
        )

    lead_ratio = ratio_of(
        vector[:, :head_part].reshape(depth_count, 8, D),
        direction[:, :head_part].reshape(depth_count, 8, D),
    )
    tail_ratio = ratio_of(vector[:, head_part:], direction[:, head_part:])
    trust_ratio = jnp.concatenate(
        [
            jnp.broadcast_to(lead_ratio, (depth_count, 8, D)).reshape(depth_count, head_part),
            jnp.broadcast_to(tail_ratio, (depth_count, FF)),
        ],
        axis=1,
    )
    return (first_new, second_new, vector - 0.5 * trust_ratio * direction)


def per_device_any(
    hidden_in,
    cotangent,
    segment_ids,
    w_qkv,
    w_out,
    w_up,
    w_down,
    vectors,
    m_qkv,
    v_qkv,
    m_out,
    v_out,
    m_up,
    v_up,
    m_down,
    v_down,
    m_vectors,
    v_vectors,
):
    tokens = hidden_in.shape[0]
    depth_count = w_qkv.shape[0]
    group_ids = segment_ids[0]
    own_ids = lax.dynamic_slice_in_dim(group_ids, lax.axis_index("col") * tokens, tokens)
    allowed = own_ids[:, None] == group_ids[None, :]

    def gather_weights(layer_at):
        qkv_raw = w_qkv[layer_at].astype(jnp.bfloat16)
        out_raw = w_out[layer_at].astype(jnp.bfloat16)
        up_raw = w_up[layer_at].astype(jnp.bfloat16)
        down_raw = w_down[layer_at].astype(jnp.bfloat16)
        qkv_cols, out_cols, up_cols, down_cols = (
            lax.all_gather(qkv_raw, "col", axis=1, tiled=True),
            lax.all_gather(out_raw, "col", axis=1, tiled=True),
            lax.all_gather(up_raw, "col", axis=1, tiled=True),
            lax.all_gather(down_raw, "col", axis=0, tiled=True),
        )
        return (
            lax.all_gather(qkv_cols, "row", axis=0, tiled=True),
            lax.all_gather(out_cols, "row", axis=0, tiled=True),
            lax.all_gather(up_cols, "row", axis=0, tiled=True),
            lax.all_gather(down_cols, "row", axis=1, tiled=True),
        )

    current = hidden_in.astype(jnp.float32)
    layer_inputs = []
    kept_runs = []
    kept_weights = []
    for layer_at in range(depth_count):
        weights = gather_weights(layer_at)
        layer_inputs.append(current)
        current, kept_vals = layer_forward(current, weights, vectors[layer_at], allowed, None)
        kept_runs.append(kept_vals)
        kept_weights.append(weights)
    grad_current = cotangent
    grads_by_layer = [None] * depth_count
    vector_grads = [None] * depth_count
    for layer_at in reversed(range(depth_count)):
        weights = gather_weights(layer_at)
        unused_out, kept_vals = layer_forward(
            layer_inputs[layer_at], weights, vectors[layer_at], allowed, kept_runs[layer_at][3]
        )
        grad_current, matrix_grads, vector_grad = layer_backward(
            grad_current, layer_inputs[layer_at], kept_vals, weights, vectors[layer_at], allowed
        )
        rows_done = (
            lax.psum_scatter(
                matrix_grads[0].astype(jnp.bfloat16), "row", scatter_dimension=0, tiled=True
            ).astype(jnp.float32),
            lax.psum_scatter(
                matrix_grads[1].astype(jnp.bfloat16), "row", scatter_dimension=0, tiled=True
            ).astype(jnp.float32),
            lax.psum_scatter(
                matrix_grads[2].astype(jnp.bfloat16), "row", scatter_dimension=0, tiled=True
            ).astype(jnp.float32),
            lax.psum_scatter(
                matrix_grads[3].astype(jnp.bfloat16), "row", scatter_dimension=1, tiled=True
            ).astype(jnp.float32),
        )
        shards = (
            lax.psum_scatter(
                rows_done[0].astype(jnp.bfloat16), "col", scatter_dimension=1, tiled=True
            ).astype(jnp.float32),
            lax.psum_scatter(
                rows_done[1].astype(jnp.bfloat16), "col", scatter_dimension=1, tiled=True
            ).astype(jnp.float32),
            lax.psum_scatter(
                rows_done[2].astype(jnp.bfloat16), "col", scatter_dimension=1, tiled=True
            ).astype(jnp.float32),
            lax.psum_scatter(
                rows_done[3].astype(jnp.bfloat16), "col", scatter_dimension=0, tiled=True
            ).astype(jnp.float32),
        )
        grads_by_layer[layer_at] = shards
        vector_grads[layer_at] = vector_grad
    masters = (w_qkv, w_out, w_up, w_down)
    firsts = (m_qkv, m_out, m_up, m_down)
    seconds = (v_qkv, v_out, v_up, v_down)
    gradients = tuple(
        (
            jnp.stack([grads_by_layer[layer_at][kind] for layer_at in range(depth_count)])
            for kind in range(4)
        )
    )
    updates = [
        adam_direction(masters[kind], gradients[kind], firsts[kind], seconds[kind], 0.01)
        for kind in range(4)
    ]
    partial_sums = jnp.stack(
        [jnp.stack(matrix_sums(masters[kind], updates[kind][2]), axis=1) for kind in range(4)],
        axis=1,
    )
    grad_vectors, total_sums = lax.psum((jnp.stack(vector_grads), partial_sums), ("row", "col"))
    lamb_norms = jnp.sqrt(total_sums)
    trust_ratio = lamb_norms[:, :, 0] / lamb_norms[:, :, 1]
    new_masters = [
        masters[kind] - 0.5 * trust_ratio[:, kind, None, None] * updates[kind][2]
        for kind in range(4)
    ]
    vec_first, vec_second, new_vectors = vector_update(vectors, grad_vectors, m_vectors, v_vectors)
    return (
        current,
        grad_current,
        gradients[0],
        gradients[1],
        gradients[2],
        gradients[3],
        grad_vectors,
        updates[0][0],
        updates[0][1],
        updates[1][0],
        updates[1][1],
        updates[2][0],
        updates[2][1],
        updates[3][0],
        updates[3][1],
        vec_first,
        vec_second,
        new_masters[0],
        new_masters[1],
        new_masters[2],
        new_masters[3],
        new_vectors,
        new_masters[0].astype(jnp.bfloat16),
        new_masters[1].astype(jnp.bfloat16),
        new_masters[2].astype(jnp.bfloat16),
        new_masters[3].astype(jnp.bfloat16),
        lamb_norms,
    )


MESH = pl.DeviceIdType.MESH
F32 = jnp.float32
BF16 = jnp.bfloat16
NT = (((1,), (1,)), ((), ()))
CHUNK = 640
VM = pl.BlockSpec(memory_space=pltpu.VMEM)
ANY = pl.BlockSpec(memory_space=pl.ANY)
SCALE = HDIM ** (-0.5)
HEADS = 5
HW = HEADS * HDIM


def where_am_i():
    r = lax.axis_index("row")
    z = lax.axis_index("col")
    return r // 4, (r // 2) % 2, r % 2, z


def row_of(y, x, c):
    return (y * 2 + x) * 2 + c


def trade_partners(y, x, c, z):
    yf = y + (1 - c) * (1 - 2 * y)
    xf = x + c * (1 - 2 * x)
    yg = y + c * (1 - 2 * y)
    xg = x + (1 - c) * (1 - 2 * x)
    return (yf, xf), (yg, xg), (1 - y, 1 - x)


def greet(peers):
    barrier = pltpu.get_barrier_semaphore()
    for peer in peers:
        pl.semaphore_signal(barrier, inc=1, device_id=peer, device_id_type=MESH)
    pl.semaphore_wait(barrier, len(peers))


def remote(src, dst, send_sem, recv_sem, peer):
    return pltpu.make_async_remote_copy(
        src_ref=src, dst_ref=dst, send_sem=send_sem, recv_sem=recv_sem,
        device_id=peer, device_id_type=MESH,
    )


def rows_at(row):
    return pl.ds(pl.multiple_of(row * 80, 80), 80)


def total_kernel(x_ref, o_ref, rows, cols, rs_send, rs_recv, cs_send, cs_recv):
    y, x, c, z = where_am_i()
    r = row_of(y, x, c)
    row_peers = [(lax.rem(r + k, 8), z) for k in range(1, 8)]
    col_peers = [(r, lax.rem(z + k, 4)) for k in range(1, 4)]
    greet(row_peers + col_peers)
    rows[r] = x_ref[...]
    copies = [
        remote(x_ref, rows.at[r], rs_send.at[k], rs_recv.at[k], peer) for k, peer in enumerate(row_peers)
    ]
    for cp in copies:
        cp.start()
    for cp in copies:
        cp.wait()
    total = rows[0]
    for k in range(1, 8):
        total = total + rows[k]
    cols[z] = total
    copies = [
        remote(cols.at[z], cols.at[z], cs_send.at[k], cs_recv.at[k], peer) for k, peer in enumerate(col_peers)
    ]
    for cp in copies:
        cp.start()
    for cp in copies:
        cp.wait()
    o_ref[...] = cols[0] + cols[1] + cols[2] + cols[3]


def total_over_devices(x, cid):
    dma = pltpu.SemaphoreType.DMA
    return pl.pallas_call(
        total_kernel,
        name="total",
        out_shape=jax.ShapeDtypeStruct(x.shape, F32),
        in_specs=[VM],
        out_specs=VM,
        scratch_shapes=[
            pltpu.VMEM((8,) + x.shape, F32), pltpu.VMEM((4,) + x.shape, F32),
            dma((7,)), dma((7,)), dma((3,)), dma((3,)),
        ],
        compiler_params=pltpu.CompilerParams(collective_id=cid, has_side_effects=True),
    )(x)


def attention_peers(y, x, c, z):
    return c * 2 + z % 2, lambda b: (row_of(y, x, b // 2), (z // 2) * 2 + b % 2)


def norm_parts(values):
    average = jnp.mean(values, axis=-1, keepdims=True)
    centered = values - average
    variance = jnp.mean(centered * centered, axis=-1, keepdims=True)
    spread = lax.rsqrt(variance + 1e-05)
    return centered * spread, spread


def dot(a, b):
    return jnp.dot(a, b, preferred_element_type=F32)


def dot_nt(a, b):
    return lax.dot_general(a, b, NT, preferred_element_type=F32)


def piece(vec_ref, at, count=640):
    return vec_ref[0:1, at : at + count]


def exchange(me, peer_of, sbuf, rbuf, ss, rs):
    y, x, c, z = where_am_i()
    out = []
    for k in (1, 2, 3):
        b = lax.rem(me + k, 4)
        out.append(remote(sbuf.at[b], rbuf.at[me], ss.at[k], rs.at[k], peer_of(b)))
    for cp in out:
        cp.start()
    return out


def head_mask(h, rows):
    lane = lax.broadcasted_iota(jnp.int32, (rows, HW), 1)
    return (lane >= h * HDIM) & (lane < (h + 1) * HDIM)


def fold(rows):
    return jnp.concatenate([rows[80 * j : 80 * (j + 1)].astype(F32) for j in range(4)], axis=1).astype(BF16)


QB = 256
LAYERS = 2
NCH = LAYERS * 5


class Gather:
    def __init__(self, s_ref, w_ref, wbuf, zs, zr, ps, pr, own_sem, load_sem):
        y, x, c, z = where_am_i()
        self.s_ref, self.w_ref, self.wbuf = s_ref, w_ref, wbuf
        self.sems = zs, zr, ps, pr, own_sem, load_sem
        (yf, xf), (yg, xg), (yd, xd) = trade_partners(y, x, c, z)
        self.z, self.r = z, row_of(y, x, c)
        self.rf, self.rg, self.rd = row_of(yf, xf, c), row_of(yg, xg, c), row_of(yd, xd, c)
        self.zpeers = [(self.r, lax.rem(z + k, 4)) for k in (1, 2, 3)]
        self.pf, self.pg, self.sib = (self.rf, z), (self.rg, z), (row_of(y, x, 1 - c), z)

    def cols(self, t):
        return t // 5, pl.ds((t % 5) * CHUNK, CHUNK)

    def zcopy(self, t, k):
        layer, cs = self.cols(t)
        zs, zr = self.sems[:2]
        return remote(
            self.s_ref.at[layer, :, cs], self.w_ref.at[layer, self.z, rows_at(self.r), cs],
            zs.at[t, k], zr.at[t, k], self.zpeers[k],
        )

    def own(self, t):
        layer, cs = self.cols(t)
        return pltpu.make_async_copy(
            self.s_ref.at[layer, :, cs], self.w_ref.at[layer, self.z, rows_at(self.r), cs], self.sems[4].at[t]
        )

    def hop(self, t, which):
        layer, cs = self.cols(t)
        row, peer = (
            (self.r, self.pf), (self.r, self.pg), (self.rf, self.pg),
            (self.r, self.sib), (self.rf, self.sib), (self.rg, self.sib), (self.rd, self.sib),
        )[which]
        block = self.w_ref.at[layer, :, rows_at(row), cs]
        return remote(block, block, self.sems[2].at[t, which], self.sems[3].at[t, which], peer)

    def load(self, t):
        layer, cs = self.cols(t)
        return pltpu.make_async_copy(self.w_ref.at[layer, :, :, cs], self.wbuf.at[t % 5], self.sems[5].at[t])

    def step(self, name, t):
        if name == "Z":
            for k in range(3):
                self.zcopy(t, k).start()
            self.own(t).start()
        elif name == "z":
            for k in range(3):
                self.zcopy(t, k).wait()
            self.own(t).wait()
            for which in (0, 1, 3):
                self.hop(t, which).start()
        elif name == "f":
            self.hop(t, 0).wait()
            for which in (2, 4):
                self.hop(t, which).start()
        elif name == "g":
            self.hop(t, 1).wait()
            self.hop(t, 2).wait()
            for which in (5, 6):
                self.hop(t, which).start()
        elif name == "s":
            for which in (3, 4, 5, 6):
                self.hop(t, which).wait()
        elif name == "L":
            self.load(t).start()
        elif name == "l":
            self.load(t).wait()

    def run(self, plan):
        for at in range(0, len(plan), 2):
            self.step(plan[at], int(plan[at + 1]))


PLAN = {
    "start": "Z0",
    "first": "z0Z1Z2f0z1Z3g0s0L0l0",
    "sent0": "f1z2g1z3",
    "heads0": ["f2s1L1Z4Z5", "g2", "f3s2L2", "z4Z6", "g3"],
    "osent0": "z5f4s3",
    "up0": ["l1L3g4Z7", "", "l2f5z6", "s4L4Z8"],
    "down0": ["l3", "l4g5"],
    "qkv1": "s5L5l5",
    "sent1": "f6z7g6z8",
    "heads1": ["f7s6L6Z9", "g7", "f8s7L7", "z9g8", "s8L8"],
    "osent1": "f9",
    "up1": ["l6", "g9", "l7s9L9", ""],
    "down1": ["l8", "l9"],
}


def swap_partner(y, x, c, z):
    return row_of(y, x, 1 - c), lax.rem(z + 2, 4)


def move_tokens(src, dst, send, recv, then):
    y, x, c, z = where_am_i()
    goes = c != z // 2
    copy = remote(src, dst, send, recv, swap_partner(y, x, c, z))
    stay = pltpu.make_async_copy(src, dst, send)

    @pl.when(goes)
    def _():
        copy.wait() if then else copy.start()

    @pl.when(jnp.logical_not(goes))
    def _():
        stay.wait() if then else stay.start()


SAVED = ("x", "xm", "o", "hdn", "gp", "q", "k", "v", "oh", "lse")


def forward_kernel(hid_ref, cot_ref, seg_ref, vec_ref, s_ref,
                   w_ref, xo_ref, dx_ref, segr_ref, segc_ref,
                   x_out, xm_out, o_out, hdn_out, gp_out, q_out, k_out, v_out, oh_out, lse_out,
                   wbuf, hid, xcur, xm_s, o_s, hdn_s, gp_s, q_s, k_s, v_s, oh_s, lse_s,
                   abuf, ubuf, segbuf, sbuf, rbuf, osbuf, orbuf, vt, ot,
                   zs, zr, ps, pr, own_sem, load_sem, ss, rs, oss, ors, save_sem, mv_s, mv_r):
    y, x, c, z = where_am_i()
    me, peer_of = attention_peers(y, x, c, z)
    net = Gather(s_ref, w_ref, wbuf, zs, zr, ps, pr, own_sem, load_sem)
    zx = z + 1 - 2 * lax.rem(z, 2)
    greet(net.zpeers + [net.pf, net.pg, net.sib, (row_of(y, x, 1 - c), zx), swap_partner(y, x, c, z)])
    move_tokens(hid_ref, hid, mv_s.at[0], mv_r.at[0], 0)
    seg_copy = remote(seg_ref, segbuf.at[1], mv_s.at[1], mv_r.at[1], net.sib)
    seg_copy.start()
    net.run(PLAN["start"])
    move_tokens(hid_ref, hid, mv_s.at[0], mv_r.at[0], 1)
    seg_copy.wait()
    segbuf[0] = seg_ref[...]
    segr_ref[...] = jnp.where(c == z // 2, segbuf[0], segbuf[1])
    segc_ref[...] = jnp.broadcast_to(segr_ref[...].astype(F32), (8, 1280)).T[:, 0:1].astype(jnp.int32)
    xcur[...] = hid[...].astype(F32)

    kept = dict(zip(SAVED, (
        (xcur, x_out), (xm_s, xm_out), (o_s, o_out), (hdn_s, hdn_out), (gp_s, gp_out),
        (q_s, q_out), (k_s, k_out), (v_s, v_out), (oh_s, oh_out), (lse_s, lse_out))))

    def save(name, layer):
        src, dst = kept[name]
        return pltpu.make_async_copy(src, dst.at[layer], save_sem.at[layer, SAVED.index(name)])

    def before(name, layer):
        if layer:
            save(name, layer - 1).wait()

    for layer in range(LAYERS):
        vl = vec_ref.at[pl.ds(layer, 1), :]
        wa, wb, wc = wbuf.at[0], wbuf.at[pl.ds(1, 2)], wbuf.at[pl.ds(3, 2)]
        save("x", layer).start()
        n1, _ = norm_parts(xcur[...])
        a = (n1 * piece(vl, 0) + piece(vl, 640)).astype(BF16)
        net.run(PLAN["qkv1" if layer else "first"])
        parts = [dot(a, wa[i, :, 0:512])[:, 0:480] for i in range(4)]
        blocks = [parts[b // 3][:, (b % 3) * HW : (b % 3 + 1) * HW] for b in range(12)]
        pad = jnp.zeros((320, 32), F32)
        for b in range(4):
            q = blocks[b] + vl[0:1, 1280 + HW * b : 1280 + HW * (b + 1)]
            v = blocks[8 + b] + vl[0:1, 1920 + HW * b : 1920 + HW * (b + 1)]
            sbuf[b] = jnp.concatenate([q, blocks[4 + b], v, pad], axis=1).astype(BF16)
        copies = exchange(me, peer_of, sbuf, rbuf, ss.at[layer], rs.at[layer])
        rbuf[me] = sbuf[me]
        for name in ("q", "k", "v", "oh", "lse"):
            before(name, layer)
        net.run(PLAN["sent%d" % layer])
        for cp in copies:
            cp.wait()

        for b in range(4):
            rows = slice(320 * b, 320 * (b + 1))
            got = rbuf[b].astype(F32)
            q_s[rows, :] = got[:, 0:HW].astype(BF16)
            k_s[rows, :] = got[:, HW : 2 * HW].astype(BF16)
            v_s[rows, :] = got[:, 2 * HW : 3 * HW].astype(BF16)
        for name in ("q", "k", "v"):
            save(name, layer).start()
        vt[...] = v_s[...].astype(F32).T.astype(BF16)
        lse_s[...] = jnp.zeros_like(lse_s)

        @pl.loop(0, HEADS)
        def _(h):
            for i, plan in enumerate(PLAN["heads%d" % layer]):
                @pl.when(h == i)
                def _():
                    net.run(plan)

            @pl.loop(0, 5)
            def _(step):
                at = pl.multiple_of(step * QB, QB)
                qm = jnp.where(head_mask(h, QB), q_s[pl.ds(at, QB), :], jnp.zeros((), BF16))
                s = dot_nt(k_s[...], qm) * SCALE
                s = jnp.where(segc_ref[...] == segr_ref[0:1, pl.ds(at, QB)], s, negative)
                top = jnp.max(s, axis=0, keepdims=True)
                p = jnp.exp(s - top)
                total = jnp.sum(p, axis=0, keepdims=True)
                rows = pl.ds(pl.multiple_of(h * HDIM, HDIM), HDIM)
                ot[rows, pl.ds(at, QB)] = dot(vt[rows, :], p.astype(BF16)) / total
                lse_s[pl.ds(h, 1), pl.ds(at, QB)] = top + jnp.log(total)

        save("lse", layer).start()
        oh_s[...] = ot[...].T.astype(BF16)
        save("oh", layer).start()
        for b in range(4):
            osbuf[b] = fold(oh_s[320 * b : 320 * (b + 1), :])
        copies = exchange(me, peer_of, osbuf, orbuf, oss.at[layer], ors.at[layer])
        orbuf[me] = osbuf[me]
        for name in ("o", "xm", "hdn", "gp"):
            before(name, layer)
        net.run(PLAN["osent%d" % layer])
        for cp in copies:
            cp.wait()
        for j in range(4):
            o_s[80 * j : 80 * (j + 1), :] = jnp.concatenate(
                [orbuf[b, :, HW * j : HW * (j + 1)].astype(F32) for b in range(4)], axis=1
            ).astype(BF16)
        o = o_s[...]
        save("o", layer).start()
        yv = jnp.concatenate([dot(o, wa[i, :, 384:640])[:, 96:256] for i in range(4)], axis=1)
        xm = xcur[...] + (yv + piece(vl, 2560))
        xm_s[...] = xm
        save("xm", layer).start()
        n2, _ = norm_parts(xm)
        abuf[...] = (n2 * piece(vl, 3200) + piece(vl, 3840)).astype(BF16)
        if layer == 0:
            move_tokens(cot_ref, dx_ref, mv_s.at[2], mv_r.at[2], 0)

        for half in range(2):
            @pl.loop(0, 4)
            def _(i):
                for at, plan in ((0, PLAN["up%d" % layer][2 * half]), (1, PLAN["up%d" % layer][2 * half + 1])):
                    @pl.when(i == at)
                    def _():
                        net.run(plan)

                to = pl.multiple_of(i * 1280 + half * 640, 640)
                ubuf[...] = dot(abuf[...], wb[half, i]) + vl[0:1, pl.ds(5120 + to, 640)]

                @pl.loop(0, 10)
                def _(j):
                    rows = pl.ds(pl.multiple_of(j * 32, 32), 32)
                    u = ubuf[rows, :]
                    cdf = 0.5 * (1.0 + lax.erf(u * (0.5**0.5)))
                    hdn_s[rows, pl.ds(to, 640)] = (u * cdf).astype(BF16)
                    gp_s[rows, pl.ds(to, 640)] = (
                        cdf + u * (jnp.exp(-0.5 * u * u) * 0.3989422804014327)
                    ).astype(BF16)

        save("hdn", layer).start()
        save("gp", layer).start()
        yv = None
        for half in range(2):
            net.run(PLAN["down%d" % layer][half])
            for i in range(4):
                term = dot_nt(hdn_s[:, 1280 * i + 640 * half : 1280 * i + 640 * (half + 1)], wc[half, i])
                yv = term if yv is None else yv + term
        save("x", layer).wait()
        xcur[...] = xm_s[...] + (yv + piece(vl, 4480))

    xo_ref[...] = xcur[...]
    for name in SAVED[1:]:
        save(name, LAYERS - 1).wait()
    move_tokens(cot_ref, dx_ref, mv_s.at[2], mv_r.at[2], 1)


def forward_all(hidden, cotangent, segments, vectors, shards):
    dma = pltpu.SemaphoreType.DMA
    sds = jax.ShapeDtypeStruct
    vmem = pltpu.VMEM
    return pl.pallas_call(
        forward_kernel,
        name="forward",
        out_shape=(
            sds((LAYERS, 4, 640, 3200), BF16), sds((320, 640), F32), sds((320, 640), F32),
            sds((1, 1280), jnp.int32), sds((1280, 1), jnp.int32),
            sds((LAYERS, 320, 640), F32), sds((LAYERS, 320, 640), F32), sds((LAYERS, 320, 640), BF16),
            sds((LAYERS, 320, 5120), BF16), sds((LAYERS, 320, 5120), BF16),
            sds((LAYERS, 1280, HW), BF16), sds((LAYERS, 1280, HW), BF16), sds((LAYERS, 1280, HW), BF16),
            sds((LAYERS, 1280, HW), BF16), sds((LAYERS, 8, 1280), F32),
        ),
        in_specs=[ANY, ANY, VM, VM, ANY],
        out_specs=(ANY, VM, ANY, VM, VM) + (ANY,) * 10,
        scratch_shapes=[
            vmem((5, 4, 640, CHUNK), BF16), vmem((320, 640), BF16), vmem((320, 640), F32),
            vmem((320, 640), F32), vmem((320, 640), BF16), vmem((320, 5120), BF16), vmem((320, 5120), BF16),
            vmem((1280, HW), BF16), vmem((1280, HW), BF16), vmem((1280, HW), BF16), vmem((1280, HW), BF16),
            vmem((8, 1280), F32),
            vmem((320, 640), BF16), vmem((320, 640), F32), vmem((2, 1, 1280), jnp.int32),
            vmem((4, 320, 512), BF16), vmem((4, 320, 512), BF16),
            vmem((4, 80, 640), BF16), vmem((4, 80, 640), BF16),
            vmem((HW, 1280), BF16), vmem((HW, 1280), F32),
            dma((NCH, 3)), dma((NCH, 3)), dma((NCH, 7)), dma((NCH, 7)), dma((NCH,)), dma((NCH,)),
            dma((LAYERS, 4)), dma((LAYERS, 4)), dma((LAYERS, 4)), dma((LAYERS, 4)),
            dma((LAYERS, len(SAVED))), dma((3,)), dma((3,)),
        ],
        compiler_params=pltpu.CompilerParams(
            collective_id=0, has_side_effects=True, vmem_limit_bytes=56 << 20
        ),
    )(hidden, cotangent, segments, vectors, shards)


def norm_back(dy, n, spread, gain):
    dn = dy * gain
    mean1 = jnp.mean(dn, axis=-1, keepdims=True)
    mean2 = jnp.mean(dn * n, axis=-1, keepdims=True)
    return spread * (dn - mean1 - n * mean2)


def col_sum(values):
    return jnp.sum(values, axis=0, keepdims=True)


ORDER = (3, 1, 4, 2, 0)
OWN, LAND = 4, 2
HELD = {(1, 3): 0, (1, 1): 1, (1, 4): 2, (1, 2): 3, (1, 0): 0, (0, 3): 1, (0, 1): 2, (0, 4): 3, (0, 2): 0, (0, 0): 1}


class Scatter:
    def __init__(self, g_ref, out_ref, own, sibr, p2r, p1r, zr, fin, fsem, sems):
        y, x, c, z = where_am_i()
        (yf, xf), (yg, xg), (yd, xd) = trade_partners(y, x, c, z)
        self.c, self.z = c, z
        self.q, self.qf, self.qg, self.qd = y * 2 + x, yf * 2 + xf, yg * 2 + xg, yd * 2 + xd
        r = row_of(y, x, c)
        self.zpeers = [(r, lax.rem(z + k, 4)) for k in (1, 2, 3)]
        self.pf, self.pg = (self.qf * 2 + c, z), (self.qg * 2 + c, z)
        self.sib = (row_of(y, x, 1 - c), z)
        self.g_ref, self.out_ref = g_ref, out_ref
        self.own, self.sibr, self.p2r, self.p1r, self.zr = own, sibr, p2r, p1r, zr
        self.fin, self.fsem, self.sems = fin, fsem, sems

    def where(self, t):
        return LAYERS - 1 - t // 5, ORDER[t % 5] * CHUNK

    def part(self, t, chip, core):
        layer, col = self.where(t)
        return self.g_ref.at[layer, :, rows_at(chip * 2 + core), pl.ds(col, CHUNK)]

    def own_copy(self, t, chip):
        return pltpu.make_async_copy(
            self.part(t, chip, self.c), self.own.at[t % OWN, chip], self.sems[0].at[t % OWN, chip]
        )

    def sib_copy(self, t, chip):
        k = t % LAND
        return remote(
            self.part(t, chip, 1 - self.c), self.sibr.at[k, chip],
            self.sems[1].at[k, chip], self.sems[2].at[k, chip], self.sib,
        )

    def p2_copy(self, t, j):
        k = t % LAND
        return remote(
            self.own.at[t % OWN, (self.qg, self.qd)[j]], self.p2r.at[k, j],
            self.sems[3].at[k, j], self.sems[4].at[k, j], self.pg,
        )

    def p1_copy(self, t):
        k = t % LAND
        return remote(
            self.own.at[t % OWN, self.qf], self.p1r.at[k], self.sems[5].at[k], self.sems[6].at[k], self.pf
        )

    def z_copy(self, t, j):
        k = t % LAND
        return remote(
            self.own.at[t % OWN, self.q, lax.rem(self.z + j + 1, 4)], self.zr.at[k, j],
            self.sems[7].at[k, j], self.sems[8].at[k, j], self.zpeers[j],
        )

    def put_out(self, t):
        layer, col = self.where(t)
        k = t % LAND
        return pltpu.make_async_copy(self.fin.at[k], self.out_ref.at[layer, :, pl.ds(col, CHUNK)], self.fsem.at[k])

    def add(self, dst, src):
        @pl.loop(0, 4)
        def _(i):
            dst[i] = dst[i] + src[i]

    def step(self, name, t):
        own = self.own.at[t % OWN]
        k = t % LAND
        if name == "a":
            for chip in range(4):
                self.sib_copy(t, chip).start()
                self.own_copy(t, chip).start()
        elif name == "b":
            for chip in range(4):
                self.sib_copy(t, chip).wait()
                self.own_copy(t, chip).wait()

            @pl.loop(0, 4)
            def _(chip):
                self.add(own.at[chip], self.sibr.at[k, chip])

            for j in range(2):
                self.p2_copy(t, j).start()
        elif name == "c":
            for j in range(2):
                self.p2_copy(t, j).wait()
            self.add(own.at[self.q], self.p2r.at[k, 0])
            self.add(own.at[self.qf], self.p2r.at[k, 1])
            self.p1_copy(t).start()
        elif name == "d":
            self.p1_copy(t).wait()
            self.add(own.at[self.q], self.p1r.at[k])
            for j in range(3):
                self.z_copy(t, j).start()
        elif name == "e":
            for j in range(3):
                self.z_copy(t, j).wait()
            total = own[self.q, self.z].astype(F32)
            for j in range(3):
                total = total + self.zr[k, j].astype(F32)
            if t >= LAND:
                self.put_out(t - LAND).wait()
            self.fin[k] = total
            self.put_out(t).start()

    def run(self, plan):
        for at in range(0, len(plan), 2):
            self.step(plan[at], int(plan[at + 1]))


BACK = {
    "mid1": "a0",
    "in1": "b0a1",
    "ffn1": "",
    "wo1": "c0b1a2",
    "heads1": ["d0", "c1b2a3", "e0d1", "c2b3", "e1d2"],
    "psent1": "c3",
    "end1": "e2d3a4",
    "mid0": "b4a5e3",
    "in0": "",
    "ffn0": "c4b5a6",
    "wo0": "d4",
    "heads0": ["c5b6a7e4", "d5", "c6b7a8e5", "d6", "c7b8e6"],
    "psent0": "d7c8",
    "end0": ["a9e7", "d8b9", "", "c9", "e8d9", "e9"],
}


def backward_kernel(dx_ref, last_ref, xs_ref, xms_ref, os_ref, hdns_ref, gps_ref, qs_ref, ks_ref, vs_ref, ohs_ref, lses_ref,
                    vec_ref, segr_ref, segc_ref, w_ref,
                    hout_ref, gin_ref, gv_ref, gout_ref, g_ref,
                    wbuf, x_s, xm_s, o_s, hdn_s, gp_s, q_s, k_s, v_s, oh_s, lse_s,
                    gbuf, at_s, dy, dyt, da2, dosend, dorecv, dos, kt, dqt, dk, dv, delta, psend, precv,
                    own, sibr, p2r, p1r, zr, fin, dxo_ref, vgot,
                    wsem, lsem, gsem, ss, rs, oss, ors, fsem, mv_s, mv_r, vs_sem, vr_sem, *net_sems):
    y, x, c, z = where_am_i()
    me, peer_of = attention_peers(y, x, c, z)
    net = Scatter(g_ref, gout_ref, own, sibr, p2r, p1r, zr, fin, fsem, net_sems)

    def load_w(layer, i):
        return pltpu.make_async_copy(w_ref.at[layer, :, :, pl.ds(i * CHUNK, CHUNK)], wbuf.at[HELD[layer, i]], wsem.at[i])

    saved = {
        "x": (xs_ref, x_s), "xm": (xms_ref, xm_s), "o": (os_ref, o_s), "hdn": (hdns_ref, hdn_s), "gp": (gps_ref, gp_s),
        "q": (qs_ref, q_s), "k": (ks_ref, k_s), "v": (vs_ref, v_s), "oh": (ohs_ref, oh_s), "lse": (lses_ref, lse_s),
    }

    def load(name, layer):
        src, dst = saved[name]
        return pltpu.make_async_copy(src.at[layer], dst, lsem.at[SAVED.index(name)])

    def fetch(layer, names):
        for name in names:
            if isinstance(name, int):
                load_w(layer, name).start()
            else:
                load(name, layer).start()

    def arrive(layer, *names):
        for name in names:
            if isinstance(name, int):
                load_w(layer, name).wait()
            else:
                load(name, layer).wait()

    fetch(1, ["xm", "hdn", "gp", 3, 1, 4, 2, "k", "q", "v", "oh", "lse", "o", "x"])
    zx = z + 1 - 2 * lax.rem(z, 2)
    greet(net.zpeers + [net.pf, net.pg, net.sib, (row_of(y, x, 1 - c), zx), swap_partner(y, x, c, z)])
    move_tokens(last_ref, hout_ref, mv_s.at[0], mv_r.at[0], 0)
    dxo_ref[...] = dx_ref[...]

    ends = [net.sib, (row_of(y, 1 - x, c), z), (row_of(1 - y, x, c), z), (row_of(y, x, c), zx),
            (row_of(y, x, c), lax.rem(z + 2, 4))]

    def vector_hop(k):
        return remote(gv_ref, vgot.at[k], vs_sem.at[k], vr_sem.at[k], ends[k])

    for layer in reversed(range(LAYERS)):
        vl = vec_ref.at[pl.ds(layer, 1), :]
        gl = gv_ref.at[pl.ds(layer, 1), :]
        dy[...] = dxo_ref[...].astype(BF16)
        dyf = dy[...].astype(F32)
        dyt[...] = dyf.T.astype(BF16)
        gl[0:1, 4480:5120] = col_sum(dyf)
        arrive(layer, "xm")
        n2, spread2 = norm_parts(xm_s[...])
        g2 = piece(vl, 3200)
        at_s[...] = (n2 * g2 + piece(vl, 3840)).T.astype(BF16)
        da2[...] = jnp.zeros_like(da2)
        arrive(layer, "hdn", "gp")

        def put(slot, i, col):
            return pltpu.make_async_copy(gbuf.at[slot], g_ref.at[layer, i, :, pl.ds(col, CHUNK)], gsem.at[slot])

        for half in range(2):
            arrive(layer, 3 + half, 1 + half)

            @pl.loop(0, 4)
            def _(i):
                if half:
                    @pl.when(i == 2)
                    def _():
                        net.run(BACK["in%d" % layer])

                to = pl.multiple_of(i * 1280 + half * CHUNK, CHUNK)

                gdown = dot(dyt[...], hdn_s[:, pl.ds(to, CHUNK)]).astype(BF16)

                @pl.when(i > 0)
                def _():
                    put(0, 0, 0).wait()

                gbuf[0] = gdown
                put(0, i, 1920 + half * CHUNK).start()
                dh = dot(dy[...], wbuf[HELD[layer, 3 + half], i])
                du = (dh * gp_s[:, pl.ds(to, CHUNK)].astype(F32)).astype(BF16)
                gl[0:1, pl.ds(5120 + to, CHUNK)] = col_sum(du.astype(F32))
                gup = dot(at_s[...], du).astype(BF16)

                @pl.when(i > 0)
                def _():
                    put(1, 0, 0).wait()

                gbuf[1] = gup
                put(1, i, 640 + half * CHUNK).start()
                da2[...] += dot_nt(du, wbuf[HELD[layer, 1 + half], i])

            put(0, 0, 0).wait()
            put(1, 0, 0).wait()
            if half == 0:
                fetch(layer, [0])
            elif layer:
                fetch(layer - 1, [3, 1, 4])
            net.run(BACK["ffn%d" % layer if half else "mid%d" % layer])

        da2v = da2[...]
        gl[0:1, 3200:3840] = col_sum(da2v * n2)
        gl[0:1, 3840:4480] = col_sum(da2v)
        dxm = dxo_ref[...] + norm_back(da2v, n2, spread2, g2)
        dxo_ref[...] = dxm
        if layer:
            fetch(layer - 1, ["hdn", "gp", "xm"])
        dy1f = dxm.astype(BF16).astype(F32)
        dy[...] = dxm.astype(BF16)
        gl[0:1, 2560:3200] = col_sum(dy1f)
        arrive(layer, 0)
        wa = wbuf.at[HELD[layer, 0]]
        zpad = jnp.zeros((320, 96), F32)
        dof = None
        for i in range(4):
            dpad = jnp.concatenate([zpad, dy1f[:, HW * i : HW * (i + 1)]], axis=1).astype(BF16)
            term = dot_nt(dpad, wa[i, :, 384:640])
            dof = term if dof is None else dof + term
        for b in range(4):
            dosend[b] = fold(dof[:, HW * b : HW * (b + 1)])
        copies = exchange(me, peer_of, dosend, dorecv, oss.at[layer], ors.at[layer])
        dorecv[me] = dosend[me]
        arrive(layer, "k", "q", "v", "oh", "lse")
        kt[...] = k_s[...].astype(F32).T.astype(BF16)
        dk[...] = jnp.zeros_like(dk)
        dv[...] = jnp.zeros_like(dv)
        net.run(BACK["wo%d" % layer])
        for cp in copies:
            cp.wait()
        for b in range(4):
            for j in range(4):
                dos[320 * b + 80 * j : 320 * b + 80 * (j + 1), :] = (
                    dorecv[b, :, HW * j : HW * (j + 1)].astype(F32).astype(BF16)
                )
        lane = lax.broadcasted_iota(jnp.int32, (8, HW), 1)
        head = lax.broadcasted_iota(jnp.int32, (8, HW), 0)
        pick = jnp.where((lane >= head * HDIM) & (lane < (head + 1) * HDIM), 1.0, 0.0).astype(F32)
        delta[...] = lax.dot_general(
            pick, dos[...].astype(F32) * oh_s[...].astype(F32), NT,
            precision=lax.Precision.HIGHEST, preferred_element_type=F32,
        )

        @pl.loop(0, HEADS)
        def _(h):
            for i, plan in enumerate(BACK["heads%d" % layer]):
                if plan:
                    @pl.when(h == i)
                    def _():
                        net.run(plan)

            @pl.loop(0, 5)
            def _(step):
                at = pl.multiple_of(step * QB, QB)
                zero = jnp.zeros((), BF16)
                mask = head_mask(h, QB)
                qm = jnp.where(mask, q_s[pl.ds(at, QB), :], zero)
                dm = jnp.where(mask, dos[pl.ds(at, QB), :], zero)
                s = dot_nt(k_s[...], qm) * SCALE
                s = jnp.where(segc_ref[...] == segr_ref[0:1, pl.ds(at, QB)], s, negative)
                p = jnp.exp(s - lse_s[pl.ds(h, 1), pl.ds(at, QB)])
                dp = dot_nt(v_s[...], dm)
                ds = (p * (dp - delta[pl.ds(h, 1), pl.ds(at, QB)])).astype(BF16)
                dv[...] += dot(p.astype(BF16), dm)
                dk[...] += dot(ds, qm)
                rows = pl.ds(pl.multiple_of(h * HDIM, HDIM), HDIM)
                dqt[rows, pl.ds(at, QB)] = dot(kt[rows, :], ds)

        if layer:
            fetch(layer - 1, ["k", "q", "v", "oh", "lse"])
        dq = dqt[...].T * SCALE
        zpad = jnp.zeros((320, 32), F32)
        for b in range(4):
            rows = slice(320 * b, 320 * (b + 1))
            psend[b] = jnp.concatenate([dq[rows], dk[rows, :] * SCALE, dv[rows, :], zpad], axis=1).astype(BF16)
        copies = exchange(me, peer_of, psend, precv, ss.at[layer], rs.at[layer])
        precv[me] = psend[me]
        arrive(layer, "x", "o")
        n1, spread1 = norm_parts(x_s[...])
        g1 = piece(vl, 0)
        at_s[...] = (n1 * g1 + piece(vl, 640)).T.astype(BF16)
        otr = o_s[...].astype(F32).T.astype(BF16)
        gos = [dot(otr, dy[...].astype(F32)[:, HW * i : HW * (i + 1)].astype(BF16)) for i in range(4)]
        if layer:
            fetch(layer - 1, ["x", "o"])
        net.run(BACK["psent%d" % layer])
        for cp in copies:
            cp.wait()
        got = [precv[b].astype(F32) for b in range(4)]
        gl[0:1, 1280:1920] = jnp.concatenate([col_sum(got[b][:, 0:HW]) for b in range(4)], axis=1)
        gl[0:1, 1920:2560] = jnp.concatenate([col_sum(got[b][:, 2 * HW : 3 * HW]) for b in range(4)], axis=1)
        blocks = [got[b % 4][:, (b // 4) * HW : (b // 4 + 1) * HW] for b in range(12)]
        da = None
        for i in range(4):
            dpi = jnp.concatenate(blocks[3 * i : 3 * i + 3] + [zpad], axis=1).astype(BF16)
            if i > 1:
                put(i % 2, 0, 0).wait()
            gbuf[i % 2] = jnp.concatenate([dot(at_s[...], dpi)[:, 0:480], gos[i]], axis=1).astype(BF16)
            put(i % 2, i, 0).start()
            term = dot_nt(dpi, wa[i, :, 0:512])
            da = term if da is None else da + term
        if layer:
            fetch(layer - 1, [2])
        gl[0:1, 0:640] = col_sum(da * n1)
        gl[0:1, 640:1280] = col_sum(da)
        dxo_ref[...] = dxo_ref[...] + norm_back(da, n1, spread1, g1)
        put(0, 0, 0).wait()
        put(1, 0, 0).wait()
        if layer:
            net.run(BACK["end%d" % layer])
    move_tokens(dxo_ref, gin_ref, mv_s.at[1], mv_r.at[1], 0)
    for k, plan in enumerate(BACK["end0"]):
        if k:
            vector_hop(k - 1).wait()
            gv_ref[...] += vgot[k - 1]
        if k < 5:
            vector_hop(k).start()
        net.run(plan)
    for t in range(NCH - LAND, NCH):
        net.put_out(t).wait()
    move_tokens(last_ref, hout_ref, mv_s.at[0], mv_r.at[0], 1)
    move_tokens(dxo_ref, gin_ref, mv_s.at[1], mv_r.at[1], 1)


def backward_all(dx, last, kept, vec, segr, segc, weights):
    dma = pltpu.SemaphoreType.DMA
    sds = jax.ShapeDtypeStruct
    vmem = pltpu.VMEM
    return pl.pallas_call(
        backward_kernel,
        name="backward",
        out_shape=(
            sds((320, 640), F32), sds((320, 640), F32), sds((LAYERS, 10240), F32), sds((LAYERS, 80, 3200), F32),
            sds((LAYERS, 4, 640, 3200), BF16),
        ),
        in_specs=[VM] + [ANY] * 11 + [VM, VM, VM, ANY],
        out_specs=(ANY, ANY, VM, ANY, ANY),
        scratch_shapes=[
            vmem((4, 4, 640, CHUNK), BF16),
            vmem((320, 640), F32), vmem((320, 640), F32), vmem((320, 640), BF16),
            vmem((320, 5120), BF16), vmem((320, 5120), BF16),
            vmem((1280, HW), BF16), vmem((1280, HW), BF16), vmem((1280, HW), BF16), vmem((1280, HW), BF16),
            vmem((8, 1280), F32),
            vmem((2, 640, CHUNK), BF16), vmem((640, 320), BF16),
            vmem((320, 640), BF16), vmem((640, 320), BF16), vmem((320, 640), F32),
            vmem((4, 80, 640), BF16), vmem((4, 80, 640), BF16), vmem((1280, HW), BF16),
            vmem((HW, 1280), BF16), vmem((HW, 1280), F32),
            vmem((1280, HW), F32), vmem((1280, HW), F32), vmem((8, 1280), F32),
            vmem((4, 320, 512), BF16), vmem((4, 320, 512), BF16),
            vmem((OWN, 4, 4, 80, CHUNK), BF16), vmem((LAND, 4, 4, 80, CHUNK), BF16),
            vmem((LAND, 2, 4, 80, CHUNK), BF16), vmem((LAND, 4, 80, CHUNK), BF16), vmem((LAND, 3, 80, CHUNK), BF16),
            vmem((LAND, 80, CHUNK), F32), vmem((320, 640), F32), vmem((5, LAYERS, 10240), F32),
            dma((5,)), dma((len(SAVED),)), dma((2,)),
            dma((LAYERS, 4)), dma((LAYERS, 4)), dma((LAYERS, 4)), dma((LAYERS, 4)), dma((LAND,)),
            dma((2,)), dma((2,)), dma((5,)), dma((5,)),
            dma((OWN, 4)), dma((LAND, 4)), dma((LAND, 4)), dma((LAND, 2)), dma((LAND, 2)),
            dma((LAND,)), dma((LAND,)), dma((LAND, 3)), dma((LAND, 3)),
        ],
        compiler_params=pltpu.CompilerParams(
            collective_id=1, has_side_effects=True, vmem_limit_bytes=60 << 20
        ),
    )(dx, last, *kept, vec, segr, segc, weights)


def per_device_fast(
    hidden_in, cotangent, segment_ids, w_qkv, w_out, w_up, w_down, vectors,
    m_qkv, v_qkv, m_out, v_out, m_up, v_up, m_down, v_down, m_vectors, v_vectors,
):
    depth = w_qkv.shape[0]
    shards = jnp.concatenate(
        [w_qkv.astype(BF16), w_out.astype(BF16), w_up.astype(BF16), w_down.astype(BF16).transpose(0, 2, 1)], axis=2
    )
    weights, x, dx, segr, segc, *kept = forward_all(hidden_in, cotangent, segment_ids, vectors, shards)
    hidden_out, grad_in, grad_vectors, grad_all, _ = backward_all(dx, x, kept, vectors, segr, segc, weights)
    gradients = (
        grad_all[:, :, 0:480], grad_all[:, :, 480:640], grad_all[:, :, 640:1920],
        grad_all[:, :, 1920:3200].transpose(0, 2, 1),
    )
    masters = (w_qkv, w_out, w_up, w_down)
    firsts = (m_qkv, m_out, m_up, m_down)
    seconds = (v_qkv, v_out, v_up, v_down)
    updates = [
        adam_direction(masters[kind], gradients[kind], firsts[kind], seconds[kind], 0.01) for kind in range(4)
    ]
    partial_sums = jnp.stack(
        [jnp.stack(matrix_sums(masters[kind], updates[kind][2]), axis=1) for kind in range(4)], axis=1
    )
    flat = jnp.pad(partial_sums.reshape(1, -1), ((0, 7), (0, 128 - partial_sums.size)))
    total_sums = total_over_devices(flat, 3)[0, : partial_sums.size].reshape(partial_sums.shape)
    lamb_norms = jnp.sqrt(total_sums)
    trust_ratio = lamb_norms[:, :, 0] / lamb_norms[:, :, 1]
    new_masters = [
        masters[kind] - 0.5 * trust_ratio[:, kind, None, None] * updates[kind][2] for kind in range(4)
    ]
    vec_first, vec_second, new_vectors = vector_update(vectors, grad_vectors, m_vectors, v_vectors)
    moments = [part for kind in range(4) for part in updates[kind][:2]]
    return (
        hidden_out, grad_in, *gradients, grad_vectors, *moments, vec_first, vec_second,
        *new_masters, new_vectors, *[w.astype(BF16) for w in new_masters], lamb_norms,
    )


def solution(mesh):
    fast = mesh.shape["row"] == 8 and mesh.shape["col"] == 4
    per_device = per_device_fast if fast else per_device_any
    return jax.shard_map(
        per_device,
        mesh=mesh,
        in_specs=(
            P(("row", "col"), None),
            P(("row", "col"), None),
            P("row", None),
            P(None, "row", "col"),
            P(None, "row", "col"),
            P(None, "row", "col"),
            P(None, "col", "row"),
            P(),
            P(None, "row", "col"),
            P(None, "row", "col"),
            P(None, "row", "col"),
            P(None, "row", "col"),
            P(None, "row", "col"),
            P(None, "row", "col"),
            P(None, "col", "row"),
            P(None, "col", "row"),
            P(),
            P(),
        ),
        out_specs=(
            P(("row", "col"), None),
            P(("row", "col"), None),
            P(None, "row", "col"),
            P(None, "row", "col"),
            P(None, "row", "col"),
            P(None, "col", "row"),
            P(),
            P(None, "row", "col"),
            P(None, "row", "col"),
            P(None, "row", "col"),
            P(None, "row", "col"),
            P(None, "row", "col"),
            P(None, "row", "col"),
            P(None, "col", "row"),
            P(None, "col", "row"),
            P(),
            P(),
            P(None, "row", "col"),
            P(None, "row", "col"),
            P(None, "row", "col"),
            P(None, "col", "row"),
            P(),
            P(None, "row", "col"),
            P(None, "row", "col"),
            P(None, "row", "col"),
            P(None, "col", "row"),
            P(),
        ),
        check_vma=False,
    )
```

```python
import functools
from functools import partial

import jax
import jax.numpy as jnp
from jax import lax
from jax.experimental import pallas as pl
from jax.experimental.pallas import tpu as pltpu
from jax.sharding import PartitionSpec as P

D = 640
HDIM = 32
FF = 5120
STEP = 5


head_groups = 4
negative = -1e30


def layer_norm(values_in, norm_gain, norm_bias):
    average = jnp.mean(values_in, axis=-1, keepdims=True)
    centered = values_in - average
    variance = jnp.mean(centered * centered, axis=-1, keepdims=True)
    return centered * lax.rsqrt(variance + 1e-05) * norm_gain + norm_bias


def to_groups(matrix):
    tokens = matrix.shape[0]
    return matrix.reshape(tokens, head_groups, -1, HDIM).transpose(1, 2, 0, 3)


def from_groups(blocks):
    return blocks.transpose(2, 0, 1, 3).reshape(blocks.shape[2], -1)


def contract_rows(left, right):
    return lax.dot_general(
        left, right, (((0,), (0,)), ((), ())), preferred_element_type=jnp.float32
    )


def contract_cols(left, right):
    return lax.dot_general(
        left, right, (((1,), (1,)), ((), ())), preferred_element_type=jnp.float32
    )


def column_total(matrix):
    return jnp.sum(matrix.astype(jnp.float32), axis=0)


def masked_scores(query_block, key_block, allowed):
    scores = jnp.einsum(
        "hqd,hkd->hqk", query_block, key_block, preferred_element_type=jnp.float32
    ) * HDIM ** (-0.5)
    return jnp.where(allowed[None, :, :], scores, negative)


def attend(queries, all_kv, allowed, kept_lse):
    features = queries.shape[1]
    tokens = queries.shape[0]
    q_groups = to_groups(queries)
    k_groups = to_groups(all_kv[:, :features])
    v_groups = to_groups(all_kv[:, features:])
    if kept_lse is None:

        def first_group(members):
            q_block, k_block, v_block = members
            scores = masked_scores(q_block, k_block, allowed)
            row_max = jnp.max(scores, axis=-1)
            log_total = row_max + jnp.log(jnp.sum(jnp.exp(scores - row_max[..., None]), axis=-1))
            softmax = jnp.exp(scores - log_total[..., None]).astype(jnp.bfloat16)
            return (
                jnp.einsum("hqk,hkd->hqd", softmax, v_block, preferred_element_type=jnp.float32),
                log_total,
            )

        attended, log_total = lax.map(first_group, (q_groups, k_groups, v_groups))
    else:
        log_total = kept_lse.reshape(head_groups, -1, tokens)

        def again_group(members):
            q_block, k_block, v_block, lse_block = members
            softmax = jnp.exp(
                masked_scores(q_block, k_block, allowed) - lse_block[..., None]
            ).astype(jnp.bfloat16)
            return jnp.einsum("hqk,hkd->hqd", softmax, v_block, preferred_element_type=jnp.float32)

        attended = lax.map(again_group, (q_groups, k_groups, v_groups, log_total))
    return (from_groups(attended).astype(jnp.bfloat16), log_total.reshape(-1, tokens))


def attention_back(queries, all_kv, grad_mixed, kept_lse, allowed):
    features = queries.shape[1]
    tokens = queries.shape[0]
    inv_root = HDIM ** (-0.5)
    q_groups = to_groups(queries)
    k_groups = to_groups(all_kv[:, :features])
    v_groups = to_groups(all_kv[:, features:])
    g_groups = to_groups(grad_mixed)
    lse_groups = kept_lse.reshape(head_groups, -1, tokens)

    def one_group(members):
        q_block, k_block, v_block, g_block, lse_block = members
        softmax = jnp.exp(masked_scores(q_block, k_block, allowed) - lse_block[..., None])
        grad_probs = jnp.einsum(
            "hqd,hkd->hqk", g_block, v_block, preferred_element_type=jnp.float32
        )
        row_dot = jnp.sum(softmax * grad_probs, axis=-1, keepdims=True)
        grad_scores = (softmax * (grad_probs - row_dot)).astype(jnp.bfloat16)
        grad_q = (
            jnp.einsum("hqk,hkd->hqd", grad_scores, k_block, preferred_element_type=jnp.float32)
            * inv_root
        )
        grad_k = (
            jnp.einsum("hqk,hqd->hkd", grad_scores, q_block, preferred_element_type=jnp.float32)
            * inv_root
        )
        grad_v = jnp.einsum(
            "hqk,hqd->hkd",
            softmax.astype(jnp.bfloat16),
            g_block,
            preferred_element_type=jnp.float32,
        )
        return (grad_q, grad_k, grad_v)

    grad_q, grad_k, grad_v = lax.map(
        one_group, (q_groups, k_groups, v_groups, g_groups, lse_groups)
    )
    return (
        from_groups(grad_q),
        jnp.concatenate([from_groups(grad_k), from_groups(grad_v)], axis=1),
    )


def layer_forward(state_in, weights, vector, allowed, kept_lse):
    w_qkv_full, w_out_full, w_up_part, w_down_part = weights
    features = state_in.shape[1]
    normed = layer_norm(state_in, vector[0:features], vector[features : 2 * features]).astype(
        jnp.bfloat16
    )
    projected = jnp.dot(normed, w_qkv_full, preferred_element_type=jnp.float32)
    queries = (projected[:, :features] + vector[2 * features : 3 * features]).astype(jnp.bfloat16)
    kv_bias = jnp.concatenate(
        [jnp.zeros((features,), jnp.float32), vector[3 * features : 4 * features]]
    )
    own_kv = (projected[:, features:] + kv_bias).astype(jnp.bfloat16)
    all_kv = lax.all_gather(own_kv, "col", axis=0, tiled=True)
    attended, log_total = attend(queries, all_kv, allowed, kept_lse)
    middle = state_in + (
        jnp.dot(attended, w_out_full, preferred_element_type=jnp.float32)
        + vector[4 * features : 5 * features]
    )
    normed_ffn = layer_norm(
        middle, vector[5 * features : 6 * features], vector[6 * features : 7 * features]
    ).astype(jnp.bfloat16)
    before = (
        jnp.dot(normed_ffn, w_up_part, preferred_element_type=jnp.float32) + vector[8 * features :]
    )
    hidden = jax.nn.gelu(before, approximate=False).astype(jnp.bfloat16)
    branch = jnp.dot(hidden, w_down_part, preferred_element_type=jnp.float32)
    state_out = middle + (branch + vector[7 * features : 8 * features])
    kept_vals = (normed, queries, all_kv, log_total, attended, middle, normed_ffn, before, hidden)
    return (state_out, kept_vals)


def layer_backward(grad_state, state_in, kept_vals, weights, vector, allowed):
    w_qkv_full, w_out_full, w_up_part, w_down_part = weights
    normed, queries, all_kv, log_total, attended, middle, ffn_rows, before, hidden = kept_vals
    features = state_in.shape[1]
    grad_branch = grad_state.astype(jnp.bfloat16)
    gelu_vjp = jax.vjp(partial(jax.nn.gelu, approximate=False), before)[1]
    grad_down = contract_rows(hidden, grad_branch)
    grad_before = gelu_vjp(contract_cols(grad_branch, w_down_part))[0].astype(jnp.bfloat16)
    grad_up = contract_rows(ffn_rows, grad_before)
    grad_up_bias = column_total(grad_before)
    grad_normed_ffn = contract_cols(grad_before, w_up_part)
    norm_two = jax.vjp(
        layer_norm, middle, vector[5 * features : 6 * features], vector[6 * features : 7 * features]
    )[1]
    grad_middle_norm, grad_gain_two, grad_bias_two = norm_two(grad_normed_ffn)
    grad_middle = grad_state + grad_middle_norm
    grad_attn_out = grad_middle.astype(jnp.bfloat16)
    grad_out_w = contract_rows(attended, grad_attn_out)
    grad_mixed = contract_cols(grad_attn_out, w_out_full).astype(jnp.bfloat16)
    grad_queries, kv_terms = attention_back(queries, all_kv, grad_mixed, log_total, allowed)
    grad_kv = lax.psum_scatter(
        kv_terms.astype(jnp.bfloat16), "col", scatter_dimension=0, tiled=True
    )
    grad_queries = grad_queries.astype(jnp.bfloat16)
    grad_proj = jnp.concatenate([grad_queries, grad_kv], axis=1)
    grad_qkv_w = contract_rows(normed, grad_proj)
    grad_normed = contract_cols(grad_proj, w_qkv_full)
    norm_one = jax.vjp(layer_norm, state_in, vector[0:features], vector[features : 2 * features])[1]
    grad_input_norm, grad_gain_one, grad_bias_one = norm_one(grad_normed)
    grad_input = grad_middle + grad_input_norm
    grad_vector = jnp.concatenate(
        [
            grad_gain_one,
            grad_bias_one,
            column_total(grad_queries),
            column_total(grad_kv[:, features:]),
            column_total(grad_attn_out),
            grad_gain_two,
            grad_bias_two,
            column_total(grad_branch),
            grad_up_bias,
        ]
    )
    return (grad_input, (grad_qkv_w, grad_out_w, grad_up, grad_down), grad_vector)


def adam_direction(weight, gradient, first_mom, second_mom, decay_rate):
    first_new = 0.9 * first_mom + 0.1 * gradient
    second_new = 0.999 * second_mom + 0.001 * gradient * gradient
    direction = (
        first_new / (1.0 - 0.9**STEP) / (jnp.sqrt(second_new / (1.0 - 0.999**STEP)) + 1e-06)
        + decay_rate * weight
    )
    return (first_new, second_new, direction)


def matrix_sums(weight, direction):
    return (jnp.sum(weight * weight, axis=(1, 2)), jnp.sum(direction * direction, axis=(1, 2)))


def vector_update(vector, gradient, first_mom, second_mom):
    first_new, second_new, direction = adam_direction(vector, gradient, first_mom, second_mom, 0.0)
    depth_count = vector.shape[0]
    head_part = 8 * D

    def ratio_of(weight_part, step_part):
        return jnp.sqrt(jnp.sum(weight_part * weight_part, axis=-1, keepdims=True)) / jnp.sqrt(
            jnp.sum(step_part * step_part, axis=-1, keepdims=True)
        )

    lead_ratio = ratio_of(
        vector[:, :head_part].reshape(depth_count, 8, D),
        direction[:, :head_part].reshape(depth_count, 8, D),
    )
    tail_ratio = ratio_of(vector[:, head_part:], direction[:, head_part:])
    trust_ratio = jnp.concatenate(
        [
            jnp.broadcast_to(lead_ratio, (depth_count, 8, D)).reshape(depth_count, head_part),
            jnp.broadcast_to(tail_ratio, (depth_count, FF)),
        ],
        axis=1,
    )
    return (first_new, second_new, vector - 0.5 * trust_ratio * direction)


def per_device_any(
    hidden_in,
    cotangent,
    segment_ids,
    w_qkv,
    w_out,
    w_up,
    w_down,
    vectors,
    m_qkv,
    v_qkv,
    m_out,
    v_out,
    m_up,
    v_up,
    m_down,
    v_down,
    m_vectors,
    v_vectors,
):
    tokens = hidden_in.shape[0]
    depth_count = w_qkv.shape[0]
    group_ids = segment_ids[0]
    own_ids = lax.dynamic_slice_in_dim(group_ids, lax.axis_index("col") * tokens, tokens)
    allowed = own_ids[:, None] == group_ids[None, :]

    def gather_weights(layer_at):
        qkv_raw = w_qkv[layer_at].astype(jnp.bfloat16)
        out_raw = w_out[layer_at].astype(jnp.bfloat16)
        up_raw = w_up[layer_at].astype(jnp.bfloat16)
        down_raw = w_down[layer_at].astype(jnp.bfloat16)
        qkv_cols, out_cols, up_cols, down_cols = (
            lax.all_gather(qkv_raw, "col", axis=1, tiled=True),
            lax.all_gather(out_raw, "col", axis=1, tiled=True),
            lax.all_gather(up_raw, "col", axis=1, tiled=True),
            lax.all_gather(down_raw, "col", axis=0, tiled=True),
        )
        return (
            lax.all_gather(qkv_cols, "row", axis=0, tiled=True),
            lax.all_gather(out_cols, "row", axis=0, tiled=True),
            lax.all_gather(up_cols, "row", axis=0, tiled=True),
            lax.all_gather(down_cols, "row", axis=1, tiled=True),
        )

    current = hidden_in.astype(jnp.float32)
    layer_inputs = []
    kept_runs = []
    kept_weights = []
    for layer_at in range(depth_count):
        weights = gather_weights(layer_at)
        layer_inputs.append(current)
        current, kept_vals = layer_forward(current, weights, vectors[layer_at], allowed, None)
        kept_runs.append(kept_vals)
        kept_weights.append(weights)
    grad_current = cotangent
    grads_by_layer = [None] * depth_count
    vector_grads = [None] * depth_count
    for layer_at in reversed(range(depth_count)):
        weights = gather_weights(layer_at)
        unused_out, kept_vals = layer_forward(
            layer_inputs[layer_at], weights, vectors[layer_at], allowed, kept_runs[layer_at][3]
        )
        grad_current, matrix_grads, vector_grad = layer_backward(
            grad_current, layer_inputs[layer_at], kept_vals, weights, vectors[layer_at], allowed
        )
        rows_done = (
            lax.psum_scatter(
                matrix_grads[0].astype(jnp.bfloat16), "row", scatter_dimension=0, tiled=True
            ).astype(jnp.float32),
            lax.psum_scatter(
                matrix_grads[1].astype(jnp.bfloat16), "row", scatter_dimension=0, tiled=True
            ).astype(jnp.float32),
            lax.psum_scatter(
                matrix_grads[2].astype(jnp.bfloat16), "row", scatter_dimension=0, tiled=True
            ).astype(jnp.float32),
            lax.psum_scatter(
                matrix_grads[3].astype(jnp.bfloat16), "row", scatter_dimension=1, tiled=True
            ).astype(jnp.float32),
        )
        shards = (
            lax.psum_scatter(
                rows_done[0].astype(jnp.bfloat16), "col", scatter_dimension=1, tiled=True
            ).astype(jnp.float32),
            lax.psum_scatter(
                rows_done[1].astype(jnp.bfloat16), "col", scatter_dimension=1, tiled=True
            ).astype(jnp.float32),
            lax.psum_scatter(
                rows_done[2].astype(jnp.bfloat16), "col", scatter_dimension=1, tiled=True
            ).astype(jnp.float32),
            lax.psum_scatter(
                rows_done[3].astype(jnp.bfloat16), "col", scatter_dimension=0, tiled=True
            ).astype(jnp.float32),
        )
        grads_by_layer[layer_at] = shards
        vector_grads[layer_at] = vector_grad
    masters = (w_qkv, w_out, w_up, w_down)
    firsts = (m_qkv, m_out, m_up, m_down)
    seconds = (v_qkv, v_out, v_up, v_down)
    gradients = tuple(
        (
            jnp.stack([grads_by_layer[layer_at][kind] for layer_at in range(depth_count)])
            for kind in range(4)
        )
    )
    updates = [
        adam_direction(masters[kind], gradients[kind], firsts[kind], seconds[kind], 0.01)
        for kind in range(4)
    ]
    partial_sums = jnp.stack(
        [jnp.stack(matrix_sums(masters[kind], updates[kind][2]), axis=1) for kind in range(4)],
        axis=1,
    )
    grad_vectors, total_sums = lax.psum((jnp.stack(vector_grads), partial_sums), ("row", "col"))
    lamb_norms = jnp.sqrt(total_sums)
    trust_ratio = lamb_norms[:, :, 0] / lamb_norms[:, :, 1]
    new_masters = [
        masters[kind] - 0.5 * trust_ratio[:, kind, None, None] * updates[kind][2]
        for kind in range(4)
    ]
    vec_first, vec_second, new_vectors = vector_update(vectors, grad_vectors, m_vectors, v_vectors)
    return (
        current,
        grad_current,
        gradients[0],
        gradients[1],
        gradients[2],
        gradients[3],
        grad_vectors,
        updates[0][0],
        updates[0][1],
        updates[1][0],
        updates[1][1],
        updates[2][0],
        updates[2][1],
        updates[3][0],
        updates[3][1],
        vec_first,
        vec_second,
        new_masters[0],
        new_masters[1],
        new_masters[2],
        new_masters[3],
        new_vectors,
        new_masters[0].astype(jnp.bfloat16),
        new_masters[1].astype(jnp.bfloat16),
        new_masters[2].astype(jnp.bfloat16),
        new_masters[3].astype(jnp.bfloat16),
        lamb_norms,
    )


MESH = pl.DeviceIdType.MESH
F32 = jnp.float32
BF16 = jnp.bfloat16
NT = (((1,), (1,)), ((), ()))
CHUNK = 640
VM = pl.BlockSpec(memory_space=pltpu.VMEM)
ANY = pl.BlockSpec(memory_space=pl.ANY)
SCALE = HDIM ** (-0.5)
SCALE2 = SCALE * 1.4426950408889634
HEADS = 5
HW = HEADS * HDIM


def where_am_i():
    r = lax.axis_index("row")
    z = lax.axis_index("col")
    return r // 4, (r // 2) % 2, r % 2, z


def row_of(y, x, c):
    return (y * 2 + x) * 2 + c


def trade_partners(y, x, c, z):
    yf = y + (1 - c) * (1 - 2 * y)
    xf = x + c * (1 - 2 * x)
    yg = y + c * (1 - 2 * y)
    xg = x + (1 - c) * (1 - 2 * x)
    return (yf, xf), (yg, xg), (1 - y, 1 - x)


def greet(peers):
    barrier = pltpu.get_barrier_semaphore()
    for peer in peers:
        pl.semaphore_signal(barrier, inc=1, device_id=peer, device_id_type=MESH)
    pl.semaphore_wait(barrier, len(peers))


def remote(src, dst, send_sem, recv_sem, peer):
    return pltpu.make_async_remote_copy(
        src_ref=src, dst_ref=dst, send_sem=send_sem, recv_sem=recv_sem,
        device_id=peer, device_id_type=MESH,
    )


def rows_at(row):
    return pl.ds(pl.multiple_of(row * 80, 80), 80)


def total_kernel(x_ref, o_ref, rows, cols, rs_send, rs_recv, cs_send, cs_recv):
    y, x, c, z = where_am_i()
    r = row_of(y, x, c)
    row_peers = [(lax.rem(r + k, 8), z) for k in range(1, 8)]
    col_peers = [(r, lax.rem(z + k, 4)) for k in range(1, 4)]
    greet(row_peers + col_peers)
    rows[r] = x_ref[...]
    copies = [
        remote(x_ref, rows.at[r], rs_send.at[k], rs_recv.at[k], peer) for k, peer in enumerate(row_peers)
    ]
    for cp in copies:
        cp.start()
    for cp in copies:
        cp.wait()
    total = rows[0]
    for k in range(1, 8):
        total = total + rows[k]
    cols[z] = total
    copies = [
        remote(cols.at[z], cols.at[z], cs_send.at[k], cs_recv.at[k], peer) for k, peer in enumerate(col_peers)
    ]
    for cp in copies:
        cp.start()
    for cp in copies:
        cp.wait()
    o_ref[...] = cols[0] + cols[1] + cols[2] + cols[3]


def total_over_devices(x, cid):
    dma = pltpu.SemaphoreType.DMA
    return pl.pallas_call(
        total_kernel,
        name="total",
        out_shape=jax.ShapeDtypeStruct(x.shape, F32),
        in_specs=[VM],
        out_specs=VM,
        scratch_shapes=[
            pltpu.VMEM((8,) + x.shape, F32), pltpu.VMEM((4,) + x.shape, F32),
            dma((7,)), dma((7,)), dma((3,)), dma((3,)),
        ],
        compiler_params=pltpu.CompilerParams(collective_id=cid, has_side_effects=True),
    )(x)


def attention_peers(y, x, c, z):
    return c * 2 + z % 2, lambda b: (row_of(y, x, b // 2), (z // 2) * 2 + b % 2)


def norm_parts(values):
    average = jnp.mean(values, axis=-1, keepdims=True)
    centered = values - average
    variance = jnp.mean(centered * centered, axis=-1, keepdims=True)
    spread = lax.rsqrt(variance + 1e-05)
    return centered * spread, spread


def dot(a, b):
    return jnp.dot(a, b, preferred_element_type=F32)


def dot_nt(a, b):
    return lax.dot_general(a, b, NT, preferred_element_type=F32)


def piece(vec_ref, at, count=640):
    return vec_ref[0:1, at : at + count]


def exchange(me, peer_of, sbuf, rbuf, ss, rs):
    y, x, c, z = where_am_i()
    out = []
    for k in (1, 2, 3):
        b = lax.rem(me + k, 4)
        out.append(remote(sbuf.at[b], rbuf.at[me], ss.at[k], rs.at[k], peer_of(b)))
    for cp in out:
        cp.start()
    return out


def head_mask(h, rows):
    lane = lax.broadcasted_iota(jnp.int32, (rows, HW), 1)
    return (lane >= h * HDIM) & (lane < (h + 1) * HDIM)


def fold(values, n):
    rows = 320 // n
    return jnp.concatenate([values[rows * j : rows * (j + 1)] for j in range(n)], axis=1)


GROUPS = ((0, 2, 2), (2, 3, 4))


def group_shapes():
    return [(4, 320 // n, n * 3 * heads * HDIM) for _, heads, n in GROUPS]


def pack_group(group, parts):
    first, heads, n = GROUPS[group]
    cut = slice(first * HDIM, (first + heads) * HDIM)
    return fold(jnp.concatenate([part[:, cut] for part in parts], axis=1), n).astype(BF16)


def unpack_group(group, block, kind):
    _, heads, n = GROUPS[group]
    w = heads * HDIM
    return jnp.concatenate(
        [block[:, (3 * j + kind) * w : (3 * j + kind + 1) * w].astype(F32) for j in range(n)], axis=0
    )


QB = 256
LAYERS = 2
NCH = LAYERS * 5


class Steps:
    def run(self, plan):
        for at in range(0, len(plan), 2):
            self.step(plan[at], int(plan[at + 1]))

    def run_at(self, plans, index):
        for at, plan in enumerate(plans):
            if plan:
                @pl.when(index == at)
                def _():
                    self.run(plan)


class Gather(Steps):
    def __init__(self, s_ref, w_ref, wbuf, zs, zr, ps, pr, own_sem, load_sem):
        y, x, c, z = where_am_i()
        self.s_ref, self.w_ref, self.wbuf = s_ref, w_ref, wbuf
        self.sems = zs, zr, ps, pr, own_sem, load_sem
        (yf, xf), (yg, xg), (yd, xd) = trade_partners(y, x, c, z)
        self.z, self.r = z, row_of(y, x, c)
        self.rf, self.rg, self.rd = row_of(yf, xf, c), row_of(yg, xg, c), row_of(yd, xd, c)
        self.zpeers = [(self.r, lax.rem(z + k, 4)) for k in (1, 2, 3)]
        self.pf, self.pg, self.sib = (self.rf, z), (self.rg, z), (row_of(y, x, 1 - c), z)

    def cols(self, t):
        return t // 5, pl.ds((t % 5) * CHUNK, CHUNK)

    def zcopy(self, t, k):
        layer, cs = self.cols(t)
        zs, zr = self.sems[:2]
        return remote(
            self.s_ref.at[layer, :, cs], self.w_ref.at[layer, self.z, rows_at(self.r), cs],
            zs.at[t, k], zr.at[t, k], self.zpeers[k],
        )

    def own(self, t):
        layer, cs = self.cols(t)
        return pltpu.make_async_copy(
            self.s_ref.at[layer, :, cs], self.w_ref.at[layer, self.z, rows_at(self.r), cs], self.sems[4].at[t]
        )

    def hop(self, t, which):
        layer, cs = self.cols(t)
        row, peer = (
            (self.r, self.pf), (self.r, self.pg), (self.rf, self.pg),
            (self.r, self.sib), (self.rf, self.sib), (self.rg, self.sib), (self.rd, self.sib),
        )[which]
        block = self.w_ref.at[layer, :, rows_at(row), cs]
        return remote(block, block, self.sems[2].at[t, which], self.sems[3].at[t, which], peer)

    def load(self, t):
        layer, cs = self.cols(t)
        return pltpu.make_async_copy(self.w_ref.at[layer, :, :, cs], self.wbuf.at[t % 5], self.sems[5].at[t])

    def step(self, name, t):
        if name == "Z":
            for k in range(3):
                self.zcopy(t, k).start()
            self.own(t).start()
        elif name == "z":
            for k in range(3):
                self.zcopy(t, k).wait()
            self.own(t).wait()
            for which in (0, 1, 3):
                self.hop(t, which).start()
        elif name == "f":
            self.hop(t, 0).wait()
            for which in (2, 4):
                self.hop(t, which).start()
        elif name == "g":
            self.hop(t, 1).wait()
            self.hop(t, 2).wait()
            for which in (5, 6):
                self.hop(t, which).start()
        elif name == "s":
            for which in (3, 4, 5, 6):
                self.hop(t, which).wait()
        elif name == "L":
            self.load(t).start()
        elif name == "l":
            self.load(t).wait()


PLAN = {
    "start": "Z0",
    "first": "z0Z1Z2f0z1Z3g0z2Z4s0L0l0",
    "sent0": "f1z3Z5",
    "heads0": ["f2g1z4Z6", "s1L1", "f3g2z5Z7", "s2L2", ""],
    "osent0": "f4g3z6Z8",
    "up0": ["l1s3L3", "", "", "f5g4z7Z9", "l2", "", "s4L4", ""],
    "down0": ["l3", "l4"],
    "qkv1": "f6g5z8s5L5l5",
    "sent1": "f7g6z9",
    "heads1": ["f8g7s6L6", "", "s7L7", "f9g8", "s8L8"],
    "osent1": "g9",
    "up1": ["l6s9", "", "", "", "l7L9", "", "", ""],
    "down1": ["l8", "l9"],
}


def swap_partner(y, x, c, z):
    return row_of(y, x, 1 - c), lax.rem(z + 2, 4)


def move_tokens(src, dst, send, recv, then):
    y, x, c, z = where_am_i()
    goes = c != z // 2
    copy = remote(src, dst, send, recv, swap_partner(y, x, c, z))
    stay = pltpu.make_async_copy(src, dst, send)

    @pl.when(goes)
    def _():
        copy.wait() if then else copy.start()

    @pl.when(jnp.logical_not(goes))
    def _():
        stay.wait() if then else stay.start()


SAVED = ("x", "xm", "o", "hdn", "gp", "q", "k", "v", "oh", "lse")


def forward_kernel(hid_ref, cot_ref, seg_ref, vec_ref, s_ref,
                   w_ref, xo_ref, dx_ref, segr_ref, segc_ref,
                   x_out, xm_out, o_out, hdn_out, gp_out, q_out, k_out, v_out, oh_out, lse_out,
                   wbuf, hid, xcur, xm_s, o_s, hdn_s, gp_s, q_s, k_s, v_s, oh_s, lse_s,
                   abuf, ubuf, pbuf, segbuf, sbuf0, sbuf1, rbuf0, rbuf1, osbuf, orbuf, vt, ot,
                   zs, zr, ps, pr, own_sem, load_sem, ss, rs, oss, ors, save_sem, mv_s, mv_r):
    y, x, c, z = where_am_i()
    me, peer_of = attention_peers(y, x, c, z)
    sbufs, rbufs = (sbuf0, sbuf1), (rbuf0, rbuf1)
    net = Gather(s_ref, w_ref, wbuf, zs, zr, ps, pr, own_sem, load_sem)
    zx = z + 1 - 2 * lax.rem(z, 2)
    greet(net.zpeers + [net.pf, net.pg, net.sib, (row_of(y, x, 1 - c), zx), swap_partner(y, x, c, z)])
    move_tokens(hid_ref, hid, mv_s.at[0], mv_r.at[0], 0)
    seg_copy = remote(seg_ref, segbuf.at[1], mv_s.at[1], mv_r.at[1], net.sib)
    seg_copy.start()
    net.run(PLAN["start"])
    move_tokens(hid_ref, hid, mv_s.at[0], mv_r.at[0], 1)
    seg_copy.wait()
    segbuf[0] = seg_ref[...]
    segr_ref[...] = jnp.where(c == z // 2, segbuf[0], segbuf[1])
    segc_ref[...] = jnp.broadcast_to(segr_ref[...].astype(F32), (8, 1280)).T[:, 0:1].astype(jnp.int32)
    xcur[...] = hid[...].astype(F32)

    kept = dict(zip(SAVED, (
        (xcur, x_out), (xm_s, xm_out), (o_s, o_out), (hdn_s, hdn_out), (gp_s, gp_out),
        (q_s, q_out), (k_s, k_out), (v_s, v_out), (oh_s, oh_out), (lse_s, lse_out))))

    def save(name, layer):
        src, dst = kept[name]
        return pltpu.make_async_copy(src, dst.at[layer], save_sem.at[layer, SAVED.index(name)])

    def before(name, layer):
        if layer:
            save(name, layer - 1).wait()

    for layer in range(LAYERS):
        vl = vec_ref.at[pl.ds(layer, 1), :]
        wa, wb, wc = wbuf.at[0], wbuf.at[pl.ds(1, 2)], wbuf.at[pl.ds(3, 2)]
        save("x", layer).start()
        n1, _ = norm_parts(xcur[...])
        a = (n1 * piece(vl, 0) + piece(vl, 640)).astype(BF16)
        net.run(PLAN["qkv1" if layer else "first"])
        abuf[...] = a

        for i in range(4):
            pbuf[i] = dot(abuf[...], wa[i, :, 0:512])

        blocks = [pbuf[b // 3, :, (b % 3) * HW : (b % 3 + 1) * HW] for b in range(12)]
        for b in range(4):
            q = blocks[b] + vl[0:1, 1280 + HW * b : 1280 + HW * (b + 1)]
            v = blocks[8 + b] + vl[0:1, 1920 + HW * b : 1920 + HW * (b + 1)]
            for g in range(2):
                sbufs[g][b] = pack_group(g, (q, blocks[4 + b], v))
        copies = exchange(me, peer_of, sbufs[0], rbufs[0], ss.at[layer, 0], rs.at[layer, 0])
        for name in ("q", "k", "v", "oh", "lse"):
            before(name, layer)
        if layer == 0:
            k_s[...] = jnp.zeros_like(k_s)
        net.run(PLAN["sent%d" % layer])
        lse_s[...] = jnp.zeros_like(lse_s)

        for g, (first, heads, _) in enumerate(GROUPS):
            rbufs[g][me] = sbufs[g][me]
            for cp in copies:
                cp.wait()
            if g == 0:
                copies = exchange(me, peer_of, sbufs[1], rbufs[1], ss.at[layer, 1], rs.at[layer, 1])
            cut = slice(first * HDIM, (first + heads) * HDIM)
            for b in range(4):
                rows = slice(320 * b, 320 * (b + 1))
                for kind, ref in enumerate((q_s, k_s, v_s)):
                    ref[rows, cut] = unpack_group(g, rbufs[g][b], kind).astype(BF16)
            wide = 128 if g == 0 else HW
            vt[cut, :] = v_s[:, 0:wide].astype(F32).T[cut, :].astype(BF16)
            if g == 1:
                for name in ("q", "k", "v"):
                    save(name, layer).start()

            @pl.loop(first, first + heads)
            def _(h):
                net.run_at(PLAN["heads%d" % layer][first : first + heads], h - first)

                @pl.loop(0, 5, unroll=5)
                def _(step):
                    at = pl.multiple_of(step * QB, QB)
                    qm = jnp.where(head_mask(h, QB), q_s[pl.ds(at, QB), :], jnp.zeros((), BF16))
                    s = dot_nt(k_s[...], qm)
                    s = jnp.where(segc_ref[...] == segr_ref[0:1, pl.ds(at, QB)], s, negative)
                    top = jnp.max(s, axis=0, keepdims=True)
                    p = jnp.exp2(s * SCALE2 - top * SCALE2)
                    total = jnp.sum(p, axis=0, keepdims=True)
                    rows = pl.ds(pl.multiple_of(h * HDIM, HDIM), HDIM)
                    ot[rows, pl.ds(at, QB)] = dot(vt[rows, :], p.astype(BF16)) / total
                    lse_s[pl.ds(h, 1), pl.ds(at, QB)] = top * SCALE2 + jnp.log2(total)

        save("lse", layer).start()
        oh_s[...] = ot[...].T.astype(BF16)
        save("oh", layer).start()
        for b in range(4):
            osbuf[b] = fold(oh_s[320 * b : 320 * (b + 1), :].astype(F32), 4).astype(BF16)
        copies = exchange(me, peer_of, osbuf, orbuf, oss.at[layer], ors.at[layer])
        orbuf[me] = osbuf[me]
        for name in ("o", "xm", "hdn", "gp"):
            before(name, layer)
        net.run(PLAN["osent%d" % layer])
        for cp in copies:
            cp.wait()
        for j in range(4):
            o_s[80 * j : 80 * (j + 1), :] = jnp.concatenate(
                [orbuf[b, :, HW * j : HW * (j + 1)].astype(F32) for b in range(4)], axis=1
            ).astype(BF16)
        save("o", layer).start()

        for i in range(4):
            pbuf[i, :, 0:256] = dot(o_s[...], wa[i, :, 384:640])

        yv = jnp.concatenate([pbuf[i, :, 96:256] for i in range(4)], axis=1)
        xm = xcur[...] + (yv + piece(vl, 2560))
        xm_s[...] = xm
        save("xm", layer).start()
        n2, _ = norm_parts(xm)
        abuf[...] = (n2 * piece(vl, 3200) + piece(vl, 3840)).astype(BF16)
        if layer == 0:
            move_tokens(cot_ref, dx_ref, mv_s.at[2], mv_r.at[2], 0)

        for half in range(2):
            @pl.loop(0, 4)
            def _(i):
                net.run_at(PLAN["up%d" % layer][4 * half : 4 * half + 4], i)

                to = pl.multiple_of(i * 1280 + half * 640, 640)
                ubuf[...] = dot(abuf[...], wb[half, i]) + vl[0:1, pl.ds(5120 + to, 640)]

                @pl.loop(0, 10)
                def _(j):
                    rows = pl.ds(pl.multiple_of(j * 32, 32), 32)
                    u = ubuf[rows, :]
                    cdf = 0.5 * (1.0 + lax.erf(u * (0.5**0.5)))
                    hdn_s[rows, pl.ds(to, 640)] = (u * cdf).astype(BF16)
                    gp_s[rows, pl.ds(to, 640)] = (
                        cdf + u * (jnp.exp(-0.5 * u * u) * 0.3989422804014327)
                    ).astype(BF16)

        save("hdn", layer).start()
        save("gp", layer).start()
        save("x", layer).wait()
        xcur[...] = xm_s[...] + piece(vl, 4480)
        for half in range(2):
            net.run(PLAN["down%d" % layer][half])

            @pl.loop(0, 4)
            def _(i):
                to = pl.multiple_of(i * 1280 + half * 640, 640)
                xcur[...] += dot_nt(hdn_s[:, pl.ds(to, 640)], wc[half, i])


    xo_ref[...] = xcur[...]
    for name in SAVED[1:]:
        save(name, LAYERS - 1).wait()
    move_tokens(cot_ref, dx_ref, mv_s.at[2], mv_r.at[2], 1)


def forward_all(hidden, cotangent, segments, vectors, shards):
    dma = pltpu.SemaphoreType.DMA
    sds = jax.ShapeDtypeStruct
    vmem = pltpu.VMEM
    return pl.pallas_call(
        forward_kernel,
        name="forward",
        out_shape=(
            sds((LAYERS, 4, 640, 3200), BF16), sds((320, 640), F32), sds((320, 640), F32),
            sds((1, 1280), jnp.int32), sds((1280, 1), jnp.int32),
            sds((LAYERS, 320, 640), F32), sds((LAYERS, 320, 640), F32), sds((LAYERS, 320, 640), BF16),
            sds((LAYERS, 320, 5120), BF16), sds((LAYERS, 320, 5120), BF16),
            sds((LAYERS, 1280, HW), BF16), sds((LAYERS, 1280, HW), BF16), sds((LAYERS, 1280, HW), BF16),
            sds((LAYERS, 1280, HW), BF16), sds((LAYERS, 8, 1280), F32),
        ),
        in_specs=[ANY, ANY, VM, VM, ANY],
        out_specs=(ANY, VM, ANY, VM, VM) + (ANY,) * 10,
        scratch_shapes=[
            vmem((5, 4, 640, CHUNK), BF16), vmem((320, 640), BF16), vmem((320, 640), F32),
            vmem((320, 640), F32), vmem((320, 640), BF16), vmem((320, 5120), BF16), vmem((320, 5120), BF16),
            vmem((1280, HW), BF16), vmem((1280, HW), BF16), vmem((1280, HW), BF16), vmem((1280, HW), BF16),
            vmem((8, 1280), F32),
            vmem((320, 640), BF16), vmem((320, 640), F32), vmem((4, 320, 512), F32), vmem((2, 1, 1280), jnp.int32),
            *[vmem(shape, BF16) for shape in group_shapes() * 2],
            vmem((4, 80, 640), BF16), vmem((4, 80, 640), BF16),
            vmem((HW, 1280), BF16), vmem((HW, 1280), F32),
            dma((NCH, 3)), dma((NCH, 3)), dma((NCH, 7)), dma((NCH, 7)), dma((NCH,)), dma((NCH,)),
            dma((LAYERS, 2, 4)), dma((LAYERS, 2, 4)), dma((LAYERS, 4)), dma((LAYERS, 4)),
            dma((LAYERS, len(SAVED))), dma((3,)), dma((3,)),
        ],
        compiler_params=pltpu.CompilerParams(
            collective_id=0, has_side_effects=True, vmem_limit_bytes=56 << 20
        ),
    )(hidden, cotangent, segments, vectors, shards)


def norm_back(dy, n, spread, gain):
    dn = dy * gain
    mean1 = jnp.mean(dn, axis=-1, keepdims=True)
    mean2 = jnp.mean(dn * n, axis=-1, keepdims=True)
    return spread * (dn - mean1 - n * mean2)


def col_sum(values):
    return jnp.sum(values, axis=0, keepdims=True)


ORDER = (3, 1, 4, 2, 0)
OWN, LAND = 4, 2
HELD = {(1, 3): 0, (1, 1): 1, (1, 4): 2, (1, 2): 3, (1, 0): 0, (0, 3): 1, (0, 1): 2, (0, 4): 3, (0, 2): 0, (0, 0): 1}


class Scatter(Steps):
    def __init__(self, g_ref, out_ref, own, sibr, p2r, p1r, zr, fin, fsem, sems):
        y, x, c, z = where_am_i()
        (yf, xf), (yg, xg), (yd, xd) = trade_partners(y, x, c, z)
        self.c, self.z = c, z
        self.q, self.qf, self.qg, self.qd = y * 2 + x, yf * 2 + xf, yg * 2 + xg, yd * 2 + xd
        r = row_of(y, x, c)
        self.zpeers = [(r, lax.rem(z + k, 4)) for k in (1, 2, 3)]
        self.pf, self.pg = (self.qf * 2 + c, z), (self.qg * 2 + c, z)
        self.sib = (row_of(y, x, 1 - c), z)
        self.g_ref, self.out_ref = g_ref, out_ref
        self.own, self.sibr, self.p2r, self.p1r, self.zr = own, sibr, p2r, p1r, zr
        self.fin, self.fsem, self.sems = fin, fsem, sems

    def where(self, t):
        return LAYERS - 1 - t // 5, ORDER[t % 5] * CHUNK

    def part(self, t, chip, core):
        layer, col = self.where(t)
        return self.g_ref.at[layer, :, rows_at(chip * 2 + core), pl.ds(col, CHUNK)]

    def own_copy(self, t, chip):
        return pltpu.make_async_copy(
            self.part(t, chip, self.c), self.own.at[t % OWN, chip], self.sems[0].at[t % OWN, chip]
        )

    def sib_copy(self, t, chip):
        k = t % LAND
        return remote(
            self.part(t, chip, 1 - self.c), self.sibr.at[k, chip],
            self.sems[1].at[k, chip], self.sems[2].at[k, chip], self.sib,
        )

    def p2_copy(self, t, j):
        k = t % LAND
        return remote(
            self.own.at[t % OWN, (self.qg, self.qd)[j]], self.p2r.at[k, j],
            self.sems[3].at[k, j], self.sems[4].at[k, j], self.pg,
        )

    def p1_copy(self, t):
        k = t % LAND
        return remote(
            self.own.at[t % OWN, self.qf], self.p1r.at[k], self.sems[5].at[k], self.sems[6].at[k], self.pf
        )

    def z_copy(self, t, j):
        k = t % LAND
        return remote(
            self.own.at[t % OWN, self.q, lax.rem(self.z + j + 1, 4)], self.zr.at[k, j],
            self.sems[7].at[k, j], self.sems[8].at[k, j], self.zpeers[j],
        )

    def put_out(self, t):
        layer, col = self.where(t)
        k = t % LAND
        return pltpu.make_async_copy(self.fin.at[k], self.out_ref.at[layer, :, pl.ds(col, CHUNK)], self.fsem.at[k])

    def add(self, dst, src):
        @pl.loop(0, 4)
        def _(i):
            dst[i] = dst[i] + src[i]

    def step(self, name, t):
        own = self.own.at[t % OWN]
        k = t % LAND
        if name == "a":
            for chip in range(4):
                self.sib_copy(t, chip).start()
                self.own_copy(t, chip).start()
        elif name == "b":
            for chip in range(4):
                self.sib_copy(t, chip).wait()
                self.own_copy(t, chip).wait()

            @pl.loop(0, 4)
            def _(chip):
                self.add(own.at[chip], self.sibr.at[k, chip])

            for j in range(2):
                self.p2_copy(t, j).start()
        elif name == "c":
            for j in range(2):
                self.p2_copy(t, j).wait()
            self.add(own.at[self.q], self.p2r.at[k, 0])
            self.add(own.at[self.qf], self.p2r.at[k, 1])
            self.p1_copy(t).start()
        elif name == "d":
            self.p1_copy(t).wait()
            self.add(own.at[self.q], self.p1r.at[k])
            for j in range(3):
                self.z_copy(t, j).start()
        elif name == "e":
            for j in range(3):
                self.z_copy(t, j).wait()
            total = own[self.q, self.z].astype(F32)
            for j in range(3):
                total = total + self.zr[k, j].astype(F32)
            if t >= LAND:
                self.put_out(t - LAND).wait()
            self.fin[k] = total
            self.put_out(t).start()


BACK = {
    "f1": ["", "", "", "", "a0", "", "", "b0a1"],
    "ffn1": "",
    "wo1": "c0b1a2",
    "heads1": ["", "", "d0", "c1", "e0b2d1a3"],
    "psent1": "c2e1b3d2",
    "end1": "c3",
    "f0": ["", "e2d3a4", "", "b4", "a5", "", "", ""],
    "ffn0": "c4b5",
    "wo0": "e3a6d4",
    "heads0": ["c5b6a7", "", "e4d5c6", "", "e5b7d6a8"],
    "psent0": "c7e6b8d7",
    "end0": ["a9", "c8b9", "e7", "d8c9", "e8", "d9e9"],
}


def backward_kernel(dx_ref, last_ref, xs_ref, xms_ref, os_ref, hdns_ref, gps_ref, qs_ref, ks_ref, vs_ref, ohs_ref, lses_ref,
                    vec_ref, segr_ref, segc_ref, w_ref,
                    hout_ref, gin_ref, gv_ref, gout_ref, g_ref,
                    wbuf, x_s, xm_s, o_s, hdn_s, gp_s, q_s, k_s, v_s, oh_s, lse_s,
                    gbuf, at_s, dy, dyt, da2, dosend, dorecv, dos, kt, dqt, dk, dv, delta, psend0, psend1, precv0, precv1, dp4,
                    own, sibr, p2r, p1r, zr, fin, dxo_ref, vgot, dpad,
                    wsem, lsem, gsem, ss, rs, oss, ors, fsem, mv_s, mv_r, vs_sem, vr_sem, *net_sems):
    y, x, c, z = where_am_i()
    me, peer_of = attention_peers(y, x, c, z)
    psends, precvs = (psend0, psend1), (precv0, precv1)
    net = Scatter(g_ref, gout_ref, own, sibr, p2r, p1r, zr, fin, fsem, net_sems)

    def load_w(layer, i):
        return pltpu.make_async_copy(w_ref.at[layer, :, :, pl.ds(i * CHUNK, CHUNK)], wbuf.at[HELD[layer, i]], wsem.at[i])

    saved = {
        "x": (xs_ref, x_s), "xm": (xms_ref, xm_s), "o": (os_ref, o_s), "hdn": (hdns_ref, hdn_s), "gp": (gps_ref, gp_s),
        "q": (qs_ref, q_s), "k": (ks_ref, k_s), "v": (vs_ref, v_s), "oh": (ohs_ref, oh_s), "lse": (lses_ref, lse_s),
    }

    def load(name, layer):
        src, dst = saved[name]
        return pltpu.make_async_copy(src.at[layer], dst, lsem.at[SAVED.index(name)])

    def fetch(layer, names):
        for name in names:
            if isinstance(name, int):
                load_w(layer, name).start()
            else:
                load(name, layer).start()

    def arrive(layer, *names):
        for name in names:
            if isinstance(name, int):
                load_w(layer, name).wait()
            else:
                load(name, layer).wait()

    fetch(1, ["xm", "hdn", "gp", 3, 1, 4, 2, "k", "q", "v", "oh", "lse", "o", "x"])
    zx = z + 1 - 2 * lax.rem(z, 2)
    greet(net.zpeers + [net.pf, net.pg, net.sib, (row_of(y, x, 1 - c), zx), swap_partner(y, x, c, z)])
    move_tokens(last_ref, hout_ref, mv_s.at[0], mv_r.at[0], 0)
    dxo_ref[...] = dx_ref[...]

    ends = [net.sib, (row_of(y, 1 - x, c), z), (row_of(1 - y, x, c), z), (row_of(y, x, c), zx),
            (row_of(y, x, c), lax.rem(z + 2, 4))]

    def vector_hop(k):
        return remote(gv_ref, vgot.at[k], vs_sem.at[k], vr_sem.at[k], ends[k])

    for layer in reversed(range(LAYERS)):
        vl = vec_ref.at[pl.ds(layer, 1), :]
        gl = gv_ref.at[pl.ds(layer, 1), :]
        dy[...] = dxo_ref[...].astype(BF16)
        dyf = dy[...].astype(F32)
        dyt[...] = dyf.T.astype(BF16)
        gl[0:1, 4480:5120] = col_sum(dyf)
        arrive(layer, "xm")
        n2, spread2 = norm_parts(xm_s[...])
        g2 = piece(vl, 3200)
        at_s[...] = (n2 * g2 + piece(vl, 3840)).T.astype(BF16)
        da2[...] = jnp.zeros_like(da2)
        arrive(layer, "hdn", "gp")

        def put(slot, i, col):
            return pltpu.make_async_copy(gbuf.at[slot], g_ref.at[layer, i, :, pl.ds(col, CHUNK)], gsem.at[slot])

        for half in range(2):
            arrive(layer, 3 + half, 1 + half)

            @pl.loop(0, 4)
            def _(i):
                net.run_at(BACK["f%d" % layer][4 * half : 4 * half + 4], i)
                to = pl.multiple_of(i * 1280 + half * CHUNK, CHUNK)

                gdown = dot(dyt[...], hdn_s[:, pl.ds(to, CHUNK)]).astype(BF16)

                @pl.when(i > 0)
                def _():
                    put(0, 0, 0).wait()

                gbuf[0] = gdown
                put(0, i, 1920 + half * CHUNK).start()
                dh = dot(dy[...], wbuf[HELD[layer, 3 + half], i])
                du = (dh * gp_s[:, pl.ds(to, CHUNK)].astype(F32)).astype(BF16)
                gl[0:1, pl.ds(5120 + to, CHUNK)] = col_sum(du.astype(F32))
                gup = dot(at_s[...], du).astype(BF16)

                @pl.when(i > 0)
                def _():
                    put(1, 0, 0).wait()

                gbuf[1] = gup
                put(1, i, 640 + half * CHUNK).start()
                da2[...] += dot_nt(du, wbuf[HELD[layer, 1 + half], i])

            put(0, 0, 0).wait()
            put(1, 0, 0).wait()
            if half == 0:
                fetch(layer, [0])
            elif layer:
                fetch(layer - 1, [3, 1, 4])
            if half:
                net.run(BACK["ffn%d" % layer])

        da2v = da2[...]
        gl[0:1, 3200:3840] = col_sum(da2v * n2)
        gl[0:1, 3840:4480] = col_sum(da2v)
        dxm = dxo_ref[...] + norm_back(da2v, n2, spread2, g2)
        dxo_ref[...] = dxm
        if layer:
            fetch(layer - 1, ["hdn", "gp", "xm"])
        dy1f = dxm.astype(BF16).astype(F32)
        dy[...] = dxm.astype(BF16)
        gl[0:1, 2560:3200] = col_sum(dy1f)
        arrive(layer, 0)
        wa = wbuf.at[HELD[layer, 0]]
        zpad = jnp.zeros((320, 96), F32)
        for i in range(4):
            dpad[i] = jnp.concatenate([zpad, dy1f[:, HW * i : HW * (i + 1)]], axis=1).astype(BF16)
        da2[...] = jnp.zeros_like(da2)

        for i in range(4):
            da2[...] += dot_nt(dpad[i], wa[i, :, 384:640])

        for b in range(4):
            dosend[b] = fold(da2[:, HW * b : HW * (b + 1)], 4).astype(BF16)
        copies = exchange(me, peer_of, dosend, dorecv, oss.at[layer], ors.at[layer])
        dorecv[me] = dosend[me]
        arrive(layer, "k", "q", "v", "oh", "lse")
        kt[...] = k_s[...].astype(F32).T.astype(BF16)
        dk[...] = jnp.zeros_like(dk)
        dv[...] = jnp.zeros_like(dv)
        net.run(BACK["wo%d" % layer])
        for cp in copies:
            cp.wait()
        for b in range(4):
            for j in range(4):
                dos[320 * b + 80 * j : 320 * b + 80 * (j + 1), :] = (
                    dorecv[b, :, HW * j : HW * (j + 1)].astype(F32).astype(BF16)
                )
        lane = lax.broadcasted_iota(jnp.int32, (8, HW), 1)
        head = lax.broadcasted_iota(jnp.int32, (8, HW), 0)
        pick = jnp.where((lane >= head * HDIM) & (lane < (head + 1) * HDIM), 1.0, 0.0).astype(F32)
        delta[...] = lax.dot_general(
            pick, dos[...].astype(F32) * oh_s[...].astype(F32), NT,
            precision=lax.Precision.HIGHEST, preferred_element_type=F32,
        )

        groups = {}
        for g in (1, 0):
            first, heads, _ = GROUPS[g]
            plans = BACK["heads%d" % layer][0:3] if g else BACK["heads%d" % layer][3:5]

            @pl.loop(first, first + heads)
            def _(h):
                net.run_at(plans, h - first)

                @pl.loop(0, 5, unroll=5)
                def _(step):
                    at = pl.multiple_of(step * QB, QB)
                    zero = jnp.zeros((), BF16)
                    mask = head_mask(h, QB)
                    qm = jnp.where(mask, q_s[pl.ds(at, QB), :], zero)
                    dm = jnp.where(mask, dos[pl.ds(at, QB), :], zero)
                    s = dot_nt(k_s[...], qm)
                    s = jnp.where(segc_ref[...] == segr_ref[0:1, pl.ds(at, QB)], s, negative)
                    p = jnp.exp2(s * SCALE2 - lse_s[pl.ds(h, 1), pl.ds(at, QB)])
                    dp = dot_nt(v_s[...], dm)
                    ds = (p * (dp - delta[pl.ds(h, 1), pl.ds(at, QB)])).astype(BF16)
                    dv[...] += dot(p.astype(BF16), dm)
                    dk[...] += dot(ds, qm)
                    rows = pl.ds(pl.multiple_of(h * HDIM, HDIM), HDIM)
                    dqt[rows, pl.ds(at, QB)] = dot(kt[rows, :], ds)

            if layer and g == 0:
                fetch(layer - 1, ["k", "q", "v", "oh", "lse"])
            dq = dqt[...].T * SCALE
            for b in range(4):
                rows = slice(320 * b, 320 * (b + 1))
                psends[g][b] = pack_group(g, (dq[rows], dk[rows, :] * SCALE, dv[rows, :]))
            groups[g] = exchange(me, peer_of, psends[g], precvs[g], ss.at[layer, g], rs.at[layer, g])
            precvs[g][me] = psends[g][me]
        copies = groups[1] + groups[0]
        zpad = jnp.zeros((320, 32), F32)
        arrive(layer, "x", "o")
        n1, spread1 = norm_parts(x_s[...])
        g1 = piece(vl, 0)
        at_s[...] = (n1 * g1 + piece(vl, 640)).T.astype(BF16)
        dyt[...] = o_s[...].astype(F32).T.astype(BF16)
        if layer:
            fetch(layer - 1, ["x", "o"])
        net.run(BACK["psent%d" % layer])
        for cp in copies:
            cp.wait()
        blocks = []
        for kind in range(3):
            own_kind = [
                jnp.concatenate([unpack_group(g, precvs[g][b], kind) for g in range(2)], axis=1) for b in range(4)
            ]
            if kind != 1:
                at = 1280 if kind == 0 else 1920
                gl[0:1, at : at + 640] = jnp.concatenate([col_sum(part) for part in own_kind], axis=1)
            blocks += own_kind
        for i in range(4):
            dp4[i] = jnp.concatenate(blocks[3 * i : 3 * i + 3] + [zpad], axis=1).astype(BF16)
        da2[...] = jnp.zeros_like(da2)

        for i in range(4):
            slot = i % 2
            part = dot(at_s[...], dp4[i])
            rest = dot(dyt[...], dpad[i])
            if i > 1:
                put(slot, 0, 0).wait()

            gbuf[slot, :, 0:384] = part[:, 0:384].astype(BF16)
            gbuf[slot, :, 384:512] = (part[:, 384:512] + rest[:, 0:128]).astype(BF16)
            gbuf[slot, :, 512:640] = rest[:, 128:256].astype(BF16)
            put(slot, i, 0).start()
            da2[...] += dot_nt(dp4[i], wa[i, :, 0:512])

        da = da2[...]
        if layer:
            fetch(layer - 1, [2])
        gl[0:1, 0:640] = col_sum(da * n1)
        gl[0:1, 640:1280] = col_sum(da)
        dxo_ref[...] = dxo_ref[...] + norm_back(da, n1, spread1, g1)
        put(0, 0, 0).wait()
        put(1, 0, 0).wait()
        if layer:
            net.run(BACK["end%d" % layer])
    move_tokens(dxo_ref, gin_ref, mv_s.at[1], mv_r.at[1], 0)
    for k, plan in enumerate(BACK["end0"]):
        if k:
            vector_hop(k - 1).wait()
            gv_ref[...] += vgot[k - 1]
        if k < 5:
            vector_hop(k).start()
        net.run(plan)
    for t in range(NCH - LAND, NCH):
        net.put_out(t).wait()
    move_tokens(last_ref, hout_ref, mv_s.at[0], mv_r.at[0], 1)
    move_tokens(dxo_ref, gin_ref, mv_s.at[1], mv_r.at[1], 1)


def backward_all(dx, last, kept, vec, segr, segc, weights):
    dma = pltpu.SemaphoreType.DMA
    sds = jax.ShapeDtypeStruct
    vmem = pltpu.VMEM
    return pl.pallas_call(
        backward_kernel,
        name="backward",
        out_shape=(
            sds((320, 640), F32), sds((320, 640), F32), sds((LAYERS, 10240), F32), sds((LAYERS, 80, 3200), F32),
            sds((LAYERS, 4, 640, 3200), BF16),
        ),
        in_specs=[VM] + [ANY] * 11 + [VM, VM, VM, ANY],
        out_specs=(ANY, ANY, VM, ANY, ANY),
        scratch_shapes=[
            vmem((4, 4, 640, CHUNK), BF16),
            vmem((320, 640), F32), vmem((320, 640), F32), vmem((320, 640), BF16),
            vmem((320, 5120), BF16), vmem((320, 5120), BF16),
            vmem((1280, HW), BF16), vmem((1280, HW), BF16), vmem((1280, HW), BF16), vmem((1280, HW), BF16),
            vmem((8, 1280), F32),
            vmem((2, 640, CHUNK), BF16), vmem((640, 320), BF16),
            vmem((320, 640), BF16), vmem((640, 320), BF16), vmem((320, 640), F32),
            vmem((4, 80, 640), BF16), vmem((4, 80, 640), BF16), vmem((1280, HW), BF16),
            vmem((HW, 1280), BF16), vmem((HW, 1280), F32),
            vmem((1280, HW), F32), vmem((1280, HW), F32), vmem((8, 1280), F32),
            *[vmem(shape, BF16) for shape in group_shapes() * 2], vmem((4, 320, 512), BF16),
            vmem((OWN, 4, 4, 80, CHUNK), BF16), vmem((LAND, 4, 4, 80, CHUNK), BF16),
            vmem((LAND, 2, 4, 80, CHUNK), BF16), vmem((LAND, 4, 80, CHUNK), BF16), vmem((LAND, 3, 80, CHUNK), BF16),
            vmem((LAND, 80, CHUNK), F32), vmem((320, 640), F32), vmem((5, LAYERS, 10240), F32),
            vmem((4, 320, 256), BF16),
            dma((5,)), dma((len(SAVED),)), dma((2,)),
            dma((LAYERS, 2, 4)), dma((LAYERS, 2, 4)), dma((LAYERS, 4)), dma((LAYERS, 4)), dma((LAND,)),
            dma((2,)), dma((2,)), dma((5,)), dma((5,)),
            dma((OWN, 4)), dma((LAND, 4)), dma((LAND, 4)), dma((LAND, 2)), dma((LAND, 2)),
            dma((LAND,)), dma((LAND,)), dma((LAND, 3)), dma((LAND, 3)),
        ],
        compiler_params=pltpu.CompilerParams(
            collective_id=1, has_side_effects=True, vmem_limit_bytes=60 << 20
        ),
    )(dx, last, *kept, vec, segr, segc, weights)


def per_device_fast(
    hidden_in, cotangent, segment_ids, w_qkv, w_out, w_up, w_down, vectors,
    m_qkv, v_qkv, m_out, v_out, m_up, v_up, m_down, v_down, m_vectors, v_vectors,
):
    depth = w_qkv.shape[0]
    shards = jnp.concatenate(
        [w_qkv.astype(BF16), w_out.astype(BF16), w_up.astype(BF16), w_down.astype(BF16).transpose(0, 2, 1)], axis=2
    )
    weights, x, dx, segr, segc, *kept = forward_all(hidden_in, cotangent, segment_ids, vectors, shards)
    hidden_out, grad_in, grad_vectors, grad_all, _ = backward_all(dx, x, kept, vectors, segr, segc, weights)
    gradients = (
        grad_all[:, :, 0:480], grad_all[:, :, 480:640], grad_all[:, :, 640:1920],
        grad_all[:, :, 1920:3200].transpose(0, 2, 1),
    )
    masters = (w_qkv, w_out, w_up, w_down)
    firsts = (m_qkv, m_out, m_up, m_down)
    seconds = (v_qkv, v_out, v_up, v_down)
    updates = [
        adam_direction(masters[kind], gradients[kind], firsts[kind], seconds[kind], 0.01) for kind in range(4)
    ]
    partial_sums = jnp.stack(
        [jnp.stack(matrix_sums(masters[kind], updates[kind][2]), axis=1) for kind in range(4)], axis=1
    )
    flat = jnp.pad(partial_sums.reshape(1, -1), ((0, 7), (0, 128 - partial_sums.size)))
    total_sums = total_over_devices(flat, 3)[0, : partial_sums.size].reshape(partial_sums.shape)
    lamb_norms = jnp.sqrt(total_sums)
    trust_ratio = lamb_norms[:, :, 0] / lamb_norms[:, :, 1]
    new_masters = [
        masters[kind] - 0.5 * trust_ratio[:, kind, None, None] * updates[kind][2] for kind in range(4)
    ]
    vec_first, vec_second, new_vectors = vector_update(vectors, grad_vectors, m_vectors, v_vectors)
    moments = [part for kind in range(4) for part in updates[kind][:2]]
    return (
        hidden_out, grad_in, *gradients, grad_vectors, *moments, vec_first, vec_second,
        *new_masters, new_vectors, *[w.astype(BF16) for w in new_masters], lamb_norms,
    )


def solution(mesh):
    fast = mesh.shape["row"] == 8 and mesh.shape["col"] == 4
    per_device = per_device_fast if fast else per_device_any
    return jax.shard_map(
        per_device,
        mesh=mesh,
        in_specs=(
            P(("row", "col"), None),
            P(("row", "col"), None),
            P("row", None),
            P(None, "row", "col"),
            P(None, "row", "col"),
            P(None, "row", "col"),
            P(None, "col", "row"),
            P(),
            P(None, "row", "col"),
            P(None, "row", "col"),
            P(None, "row", "col"),
            P(None, "row", "col"),
            P(None, "row", "col"),
            P(None, "row", "col"),
            P(None, "col", "row"),
            P(None, "col", "row"),
            P(),
            P(),
        ),
        out_specs=(
            P(("row", "col"), None),
            P(("row", "col"), None),
            P(None, "row", "col"),
            P(None, "row", "col"),
            P(None, "row", "col"),
            P(None, "col", "row"),
            P(),
            P(None, "row", "col"),
            P(None, "row", "col"),
            P(None, "row", "col"),
            P(None, "row", "col"),
            P(None, "row", "col"),
            P(None, "row", "col"),
            P(None, "col", "row"),
            P(None, "col", "row"),
            P(),
            P(),
            P(None, "row", "col"),
            P(None, "row", "col"),
            P(None, "row", "col"),
            P(None, "col", "row"),
            P(),
            P(None, "row", "col"),
            P(None, "row", "col"),
            P(None, "row", "col"),
            P(None, "col", "row"),
            P(),
        ),
        check_vma=False,
    )
```

```python
import functools
from functools import partial

import jax
import jax.numpy as jnp
from jax import lax
from jax.experimental import pallas as pl
from jax.experimental.pallas import tpu as pltpu
from jax.sharding import PartitionSpec as P

D = 640
HDIM = 32
FF = 5120
STEP = 5


head_groups = 4
negative = -1e30


def layer_norm(values_in, norm_gain, norm_bias):
    average = jnp.mean(values_in, axis=-1, keepdims=True)
    centered = values_in - average
    variance = jnp.mean(centered * centered, axis=-1, keepdims=True)
    return centered * lax.rsqrt(variance + 1e-05) * norm_gain + norm_bias


def to_groups(matrix):
    tokens = matrix.shape[0]
    return matrix.reshape(tokens, head_groups, -1, HDIM).transpose(1, 2, 0, 3)


def from_groups(blocks):
    return blocks.transpose(2, 0, 1, 3).reshape(blocks.shape[2], -1)


def contract_rows(left, right):
    return lax.dot_general(
        left, right, (((0,), (0,)), ((), ())), preferred_element_type=jnp.float32
    )


def contract_cols(left, right):
    return lax.dot_general(
        left, right, (((1,), (1,)), ((), ())), preferred_element_type=jnp.float32
    )


def column_total(matrix):
    return jnp.sum(matrix.astype(jnp.float32), axis=0)


def masked_scores(query_block, key_block, allowed):
    scores = jnp.einsum(
        "hqd,hkd->hqk", query_block, key_block, preferred_element_type=jnp.float32
    ) * HDIM ** (-0.5)
    return jnp.where(allowed[None, :, :], scores, negative)


def attend(queries, all_kv, allowed, kept_lse):
    features = queries.shape[1]
    tokens = queries.shape[0]
    q_groups = to_groups(queries)
    k_groups = to_groups(all_kv[:, :features])
    v_groups = to_groups(all_kv[:, features:])
    if kept_lse is None:

        def first_group(members):
            q_block, k_block, v_block = members
            scores = masked_scores(q_block, k_block, allowed)
            row_max = jnp.max(scores, axis=-1)
            log_total = row_max + jnp.log(jnp.sum(jnp.exp(scores - row_max[..., None]), axis=-1))
            softmax = jnp.exp(scores - log_total[..., None]).astype(jnp.bfloat16)
            return (
                jnp.einsum("hqk,hkd->hqd", softmax, v_block, preferred_element_type=jnp.float32),
                log_total,
            )

        attended, log_total = lax.map(first_group, (q_groups, k_groups, v_groups))
    else:
        log_total = kept_lse.reshape(head_groups, -1, tokens)

        def again_group(members):
            q_block, k_block, v_block, lse_block = members
            softmax = jnp.exp(
                masked_scores(q_block, k_block, allowed) - lse_block[..., None]
            ).astype(jnp.bfloat16)
            return jnp.einsum("hqk,hkd->hqd", softmax, v_block, preferred_element_type=jnp.float32)

        attended = lax.map(again_group, (q_groups, k_groups, v_groups, log_total))
    return (from_groups(attended).astype(jnp.bfloat16), log_total.reshape(-1, tokens))


def attention_back(queries, all_kv, grad_mixed, kept_lse, allowed):
    features = queries.shape[1]
    tokens = queries.shape[0]
    inv_root = HDIM ** (-0.5)
    q_groups = to_groups(queries)
    k_groups = to_groups(all_kv[:, :features])
    v_groups = to_groups(all_kv[:, features:])
    g_groups = to_groups(grad_mixed)
    lse_groups = kept_lse.reshape(head_groups, -1, tokens)

    def one_group(members):
        q_block, k_block, v_block, g_block, lse_block = members
        softmax = jnp.exp(masked_scores(q_block, k_block, allowed) - lse_block[..., None])
        grad_probs = jnp.einsum(
            "hqd,hkd->hqk", g_block, v_block, preferred_element_type=jnp.float32
        )
        row_dot = jnp.sum(softmax * grad_probs, axis=-1, keepdims=True)
        grad_scores = (softmax * (grad_probs - row_dot)).astype(jnp.bfloat16)
        grad_q = (
            jnp.einsum("hqk,hkd->hqd", grad_scores, k_block, preferred_element_type=jnp.float32)
            * inv_root
        )
        grad_k = (
            jnp.einsum("hqk,hqd->hkd", grad_scores, q_block, preferred_element_type=jnp.float32)
            * inv_root
        )
        grad_v = jnp.einsum(
            "hqk,hqd->hkd",
            softmax.astype(jnp.bfloat16),
            g_block,
            preferred_element_type=jnp.float32,
        )
        return (grad_q, grad_k, grad_v)

    grad_q, grad_k, grad_v = lax.map(
        one_group, (q_groups, k_groups, v_groups, g_groups, lse_groups)
    )
    return (
        from_groups(grad_q),
        jnp.concatenate([from_groups(grad_k), from_groups(grad_v)], axis=1),
    )


def layer_forward(state_in, weights, vector, allowed, kept_lse):
    w_qkv_full, w_out_full, w_up_part, w_down_part = weights
    features = state_in.shape[1]
    normed = layer_norm(state_in, vector[0:features], vector[features : 2 * features]).astype(
        jnp.bfloat16
    )
    projected = jnp.dot(normed, w_qkv_full, preferred_element_type=jnp.float32)
    queries = (projected[:, :features] + vector[2 * features : 3 * features]).astype(jnp.bfloat16)
    kv_bias = jnp.concatenate(
        [jnp.zeros((features,), jnp.float32), vector[3 * features : 4 * features]]
    )
    own_kv = (projected[:, features:] + kv_bias).astype(jnp.bfloat16)
    all_kv = lax.all_gather(own_kv, "col", axis=0, tiled=True)
    attended, log_total = attend(queries, all_kv, allowed, kept_lse)
    middle = state_in + (
        jnp.dot(attended, w_out_full, preferred_element_type=jnp.float32)
        + vector[4 * features : 5 * features]
    )
    normed_ffn = layer_norm(
        middle, vector[5 * features : 6 * features], vector[6 * features : 7 * features]
    ).astype(jnp.bfloat16)
    before = (
        jnp.dot(normed_ffn, w_up_part, preferred_element_type=jnp.float32) + vector[8 * features :]
    )
    hidden = jax.nn.gelu(before, approximate=False).astype(jnp.bfloat16)
    branch = jnp.dot(hidden, w_down_part, preferred_element_type=jnp.float32)
    state_out = middle + (branch + vector[7 * features : 8 * features])
    kept_vals = (normed, queries, all_kv, log_total, attended, middle, normed_ffn, before, hidden)
    return (state_out, kept_vals)


def layer_backward(grad_state, state_in, kept_vals, weights, vector, allowed):
    w_qkv_full, w_out_full, w_up_part, w_down_part = weights
    normed, queries, all_kv, log_total, attended, middle, ffn_rows, before, hidden = kept_vals
    features = state_in.shape[1]
    grad_branch = grad_state.astype(jnp.bfloat16)
    gelu_vjp = jax.vjp(partial(jax.nn.gelu, approximate=False), before)[1]
    grad_down = contract_rows(hidden, grad_branch)
    grad_before = gelu_vjp(contract_cols(grad_branch, w_down_part))[0].astype(jnp.bfloat16)
    grad_up = contract_rows(ffn_rows, grad_before)
    grad_up_bias = column_total(grad_before)
    grad_normed_ffn = contract_cols(grad_before, w_up_part)
    norm_two = jax.vjp(
        layer_norm, middle, vector[5 * features : 6 * features], vector[6 * features : 7 * features]
    )[1]
    grad_middle_norm, grad_gain_two, grad_bias_two = norm_two(grad_normed_ffn)
    grad_middle = grad_state + grad_middle_norm
    grad_attn_out = grad_middle.astype(jnp.bfloat16)
    grad_out_w = contract_rows(attended, grad_attn_out)
    grad_mixed = contract_cols(grad_attn_out, w_out_full).astype(jnp.bfloat16)
    grad_queries, kv_terms = attention_back(queries, all_kv, grad_mixed, log_total, allowed)
    grad_kv = lax.psum_scatter(
        kv_terms.astype(jnp.bfloat16), "col", scatter_dimension=0, tiled=True
    )
    grad_queries = grad_queries.astype(jnp.bfloat16)
    grad_proj = jnp.concatenate([grad_queries, grad_kv], axis=1)
    grad_qkv_w = contract_rows(normed, grad_proj)
    grad_normed = contract_cols(grad_proj, w_qkv_full)
    norm_one = jax.vjp(layer_norm, state_in, vector[0:features], vector[features : 2 * features])[1]
    grad_input_norm, grad_gain_one, grad_bias_one = norm_one(grad_normed)
    grad_input = grad_middle + grad_input_norm
    grad_vector = jnp.concatenate(
        [
            grad_gain_one,
            grad_bias_one,
            column_total(grad_queries),
            column_total(grad_kv[:, features:]),
            column_total(grad_attn_out),
            grad_gain_two,
            grad_bias_two,
            column_total(grad_branch),
            grad_up_bias,
        ]
    )
    return (grad_input, (grad_qkv_w, grad_out_w, grad_up, grad_down), grad_vector)


def adam_direction(weight, gradient, first_mom, second_mom, decay_rate):
    first_new = 0.9 * first_mom + 0.1 * gradient
    second_new = 0.999 * second_mom + 0.001 * gradient * gradient
    direction = (
        first_new / (1.0 - 0.9**STEP) / (jnp.sqrt(second_new / (1.0 - 0.999**STEP)) + 1e-06)
        + decay_rate * weight
    )
    return (first_new, second_new, direction)


def matrix_sums(weight, direction):
    return (jnp.sum(weight * weight, axis=(1, 2)), jnp.sum(direction * direction, axis=(1, 2)))


def vector_update(vector, gradient, first_mom, second_mom):
    first_new, second_new, direction = adam_direction(vector, gradient, first_mom, second_mom, 0.0)
    depth_count = vector.shape[0]
    head_part = 8 * D

    def ratio_of(weight_part, step_part):
        return jnp.sqrt(jnp.sum(weight_part * weight_part, axis=-1, keepdims=True)) / jnp.sqrt(
            jnp.sum(step_part * step_part, axis=-1, keepdims=True)
        )

    lead_ratio = ratio_of(
        vector[:, :head_part].reshape(depth_count, 8, D),
        direction[:, :head_part].reshape(depth_count, 8, D),
    )
    tail_ratio = ratio_of(vector[:, head_part:], direction[:, head_part:])
    trust_ratio = jnp.concatenate(
        [
            jnp.broadcast_to(lead_ratio, (depth_count, 8, D)).reshape(depth_count, head_part),
            jnp.broadcast_to(tail_ratio, (depth_count, FF)),
        ],
        axis=1,
    )
    return (first_new, second_new, vector - 0.5 * trust_ratio * direction)


def per_device_any(
    hidden_in,
    cotangent,
    segment_ids,
    w_qkv,
    w_out,
    w_up,
    w_down,
    vectors,
    m_qkv,
    v_qkv,
    m_out,
    v_out,
    m_up,
    v_up,
    m_down,
    v_down,
    m_vectors,
    v_vectors,
):
    tokens = hidden_in.shape[0]
    depth_count = w_qkv.shape[0]
    group_ids = segment_ids[0]
    own_ids = lax.dynamic_slice_in_dim(group_ids, lax.axis_index("col") * tokens, tokens)
    allowed = own_ids[:, None] == group_ids[None, :]

    def gather_weights(layer_at):
        qkv_raw = w_qkv[layer_at].astype(jnp.bfloat16)
        out_raw = w_out[layer_at].astype(jnp.bfloat16)
        up_raw = w_up[layer_at].astype(jnp.bfloat16)
        down_raw = w_down[layer_at].astype(jnp.bfloat16)
        qkv_cols, out_cols, up_cols, down_cols = (
            lax.all_gather(qkv_raw, "col", axis=1, tiled=True),
            lax.all_gather(out_raw, "col", axis=1, tiled=True),
            lax.all_gather(up_raw, "col", axis=1, tiled=True),
            lax.all_gather(down_raw, "col", axis=0, tiled=True),
        )
        return (
            lax.all_gather(qkv_cols, "row", axis=0, tiled=True),
            lax.all_gather(out_cols, "row", axis=0, tiled=True),
            lax.all_gather(up_cols, "row", axis=0, tiled=True),
            lax.all_gather(down_cols, "row", axis=1, tiled=True),
        )

    current = hidden_in.astype(jnp.float32)
    layer_inputs = []
    kept_runs = []
    kept_weights = []
    for layer_at in range(depth_count):
        weights = gather_weights(layer_at)
        layer_inputs.append(current)
        current, kept_vals = layer_forward(current, weights, vectors[layer_at], allowed, None)
        kept_runs.append(kept_vals)
        kept_weights.append(weights)
    grad_current = cotangent
    grads_by_layer = [None] * depth_count
    vector_grads = [None] * depth_count
    for layer_at in reversed(range(depth_count)):
        weights = gather_weights(layer_at)
        unused_out, kept_vals = layer_forward(
            layer_inputs[layer_at], weights, vectors[layer_at], allowed, kept_runs[layer_at][3]
        )
        grad_current, matrix_grads, vector_grad = layer_backward(
            grad_current, layer_inputs[layer_at], kept_vals, weights, vectors[layer_at], allowed
        )
        rows_done = (
            lax.psum_scatter(
                matrix_grads[0].astype(jnp.bfloat16), "row", scatter_dimension=0, tiled=True
            ).astype(jnp.float32),
            lax.psum_scatter(
                matrix_grads[1].astype(jnp.bfloat16), "row", scatter_dimension=0, tiled=True
            ).astype(jnp.float32),
            lax.psum_scatter(
                matrix_grads[2].astype(jnp.bfloat16), "row", scatter_dimension=0, tiled=True
            ).astype(jnp.float32),
            lax.psum_scatter(
                matrix_grads[3].astype(jnp.bfloat16), "row", scatter_dimension=1, tiled=True
            ).astype(jnp.float32),
        )
        shards = (
            lax.psum_scatter(
                rows_done[0].astype(jnp.bfloat16), "col", scatter_dimension=1, tiled=True
            ).astype(jnp.float32),
            lax.psum_scatter(
                rows_done[1].astype(jnp.bfloat16), "col", scatter_dimension=1, tiled=True
            ).astype(jnp.float32),
            lax.psum_scatter(
                rows_done[2].astype(jnp.bfloat16), "col", scatter_dimension=1, tiled=True
            ).astype(jnp.float32),
            lax.psum_scatter(
                rows_done[3].astype(jnp.bfloat16), "col", scatter_dimension=0, tiled=True
            ).astype(jnp.float32),
        )
        grads_by_layer[layer_at] = shards
        vector_grads[layer_at] = vector_grad
    masters = (w_qkv, w_out, w_up, w_down)
    firsts = (m_qkv, m_out, m_up, m_down)
    seconds = (v_qkv, v_out, v_up, v_down)
    gradients = tuple(
        (
            jnp.stack([grads_by_layer[layer_at][kind] for layer_at in range(depth_count)])
            for kind in range(4)
        )
    )
    updates = [
        adam_direction(masters[kind], gradients[kind], firsts[kind], seconds[kind], 0.01)
        for kind in range(4)
    ]
    partial_sums = jnp.stack(
        [jnp.stack(matrix_sums(masters[kind], updates[kind][2]), axis=1) for kind in range(4)],
        axis=1,
    )
    grad_vectors, total_sums = lax.psum((jnp.stack(vector_grads), partial_sums), ("row", "col"))
    lamb_norms = jnp.sqrt(total_sums)
    trust_ratio = lamb_norms[:, :, 0] / lamb_norms[:, :, 1]
    new_masters = [
        masters[kind] - 0.5 * trust_ratio[:, kind, None, None] * updates[kind][2]
        for kind in range(4)
    ]
    vec_first, vec_second, new_vectors = vector_update(vectors, grad_vectors, m_vectors, v_vectors)
    return (
        current,
        grad_current,
        gradients[0],
        gradients[1],
        gradients[2],
        gradients[3],
        grad_vectors,
        updates[0][0],
        updates[0][1],
        updates[1][0],
        updates[1][1],
        updates[2][0],
        updates[2][1],
        updates[3][0],
        updates[3][1],
        vec_first,
        vec_second,
        new_masters[0],
        new_masters[1],
        new_masters[2],
        new_masters[3],
        new_vectors,
        new_masters[0].astype(jnp.bfloat16),
        new_masters[1].astype(jnp.bfloat16),
        new_masters[2].astype(jnp.bfloat16),
        new_masters[3].astype(jnp.bfloat16),
        lamb_norms,
    )


MESH = pl.DeviceIdType.MESH
F32 = jnp.float32
BF16 = jnp.bfloat16
NT = (((1,), (1,)), ((), ()))
CHUNK = 640
VM = pl.BlockSpec(memory_space=pltpu.VMEM)
ANY = pl.BlockSpec(memory_space=pl.ANY)
SCALE = HDIM ** (-0.5)
SCALE2 = SCALE * 1.4426950408889634
HEADS = 5
HW = HEADS * HDIM


def where_am_i():
    r = lax.axis_index("row")
    z = lax.axis_index("col")
    return r // 4, (r // 2) % 2, r % 2, z


def row_of(y, x, c):
    return (y * 2 + x) * 2 + c


def trade_partners(y, x, c, z):
    yf = y + (1 - c) * (1 - 2 * y)
    xf = x + c * (1 - 2 * x)
    yg = y + c * (1 - 2 * y)
    xg = x + (1 - c) * (1 - 2 * x)
    return (yf, xf), (yg, xg), (1 - y, 1 - x)


def greet(peers):
    barrier = pltpu.get_barrier_semaphore()
    for peer in peers:
        pl.semaphore_signal(barrier, inc=1, device_id=peer, device_id_type=MESH)
    pl.semaphore_wait(barrier, len(peers))


def remote(src, dst, send_sem, recv_sem, peer):
    return pltpu.make_async_remote_copy(
        src_ref=src, dst_ref=dst, send_sem=send_sem, recv_sem=recv_sem,
        device_id=peer, device_id_type=MESH,
    )


def total_kernel(x_ref, o_ref, rows, cols, rs_send, rs_recv, cs_send, cs_recv):
    y, x, c, z = where_am_i()
    r = row_of(y, x, c)
    row_peers = [(lax.rem(r + k, 8), z) for k in range(1, 8)]
    col_peers = [(r, lax.rem(z + k, 4)) for k in range(1, 4)]
    greet(row_peers + col_peers)
    rows[r] = x_ref[...]
    copies = [
        remote(x_ref, rows.at[r], rs_send.at[k], rs_recv.at[k], peer) for k, peer in enumerate(row_peers)
    ]
    for cp in copies:
        cp.start()
    for cp in copies:
        cp.wait()
    total = rows[0]
    for k in range(1, 8):
        total = total + rows[k]
    cols[z] = total
    copies = [
        remote(cols.at[z], cols.at[z], cs_send.at[k], cs_recv.at[k], peer) for k, peer in enumerate(col_peers)
    ]
    for cp in copies:
        cp.start()
    for cp in copies:
        cp.wait()
    o_ref[...] = cols[0] + cols[1] + cols[2] + cols[3]


def total_over_devices(x, cid):
    dma = pltpu.SemaphoreType.DMA
    return pl.pallas_call(
        total_kernel,
        name="total",
        out_shape=jax.ShapeDtypeStruct(x.shape, F32),
        in_specs=[VM],
        out_specs=VM,
        scratch_shapes=[
            pltpu.VMEM((8,) + x.shape, F32), pltpu.VMEM((4,) + x.shape, F32),
            dma((7,)), dma((7,)), dma((3,)), dma((3,)),
        ],
        compiler_params=pltpu.CompilerParams(collective_id=cid, has_side_effects=True),
    )(x)


def attention_peers(y, x, c, z):
    return c * 2 + z % 2, lambda b: (row_of(y, x, b // 2), (z // 2) * 2 + b % 2)


def norm_parts(values):
    average = jnp.mean(values, axis=-1, keepdims=True)
    centered = values - average
    variance = jnp.mean(centered * centered, axis=-1, keepdims=True)
    spread = lax.rsqrt(variance + 1e-05)
    return centered * spread, spread


def dot(a, b):
    return jnp.dot(a, b, preferred_element_type=F32)


def dot_nt(a, b):
    return lax.dot_general(a, b, NT, preferred_element_type=F32)


def piece(vec_ref, at, count=640):
    return vec_ref[0:1, at : at + count]


def exchange(me, peer_of, sbuf, rbuf, ss, rs):
    y, x, c, z = where_am_i()
    out = []
    for k in (1, 2, 3):
        b = lax.rem(me + k, 4)
        out.append(remote(sbuf.at[b], rbuf.at[me], ss.at[k], rs.at[k], peer_of(b)))
    for cp in out:
        cp.start()
    return out


def head_mask(h, rows):
    lane = lax.broadcasted_iota(jnp.int32, (rows, HW), 1)
    return (lane >= h * HDIM) & (lane < (h + 1) * HDIM)


def fold(values, n):
    rows = 320 // n
    return jnp.concatenate([values[rows * j : rows * (j + 1)] for j in range(n)], axis=1)


GROUPS = ((0, 2, 2), (2, 3, 4))


def group_shapes():
    return [(4, 320 // n, n * 3 * heads * HDIM) for _, heads, n in GROUPS]


def pack_group(group, parts):
    first, heads, n = GROUPS[group]
    cut = slice(first * HDIM, (first + heads) * HDIM)
    return fold(jnp.concatenate([part[:, cut] for part in parts], axis=1), n).astype(BF16)


def unpack_group(group, block, kind):
    _, heads, n = GROUPS[group]
    w = heads * HDIM
    return jnp.concatenate(
        [block[:, (3 * j + kind) * w : (3 * j + kind + 1) * w].astype(F32) for j in range(n)], axis=0
    )


QB = 256
LAYERS = 2
NCH = LAYERS * 5
PIECES = ((0, 0, 256), (0, 256, 256), (0, 512, 768)) + tuple(
    (layer, col, CHUNK) for layer in range(LAYERS) for col in range(0, 3200, CHUNK) if layer or col >= 1280
)


class Steps:
    def run(self, plan):
        for at in range(0, len(plan), 2):
            self.step(plan[at], int(plan[at + 1], 16))

    def run_at(self, plans, index):
        for at, plan in enumerate(plans):
            if plan:
                @pl.when(index == at)
                def _():
                    self.run(plan)


class Gather(Steps):
    def __init__(self, s_ref, w_ref, wbuf, zs, zr, ps, pr, own_sem, load_sem):
        y, x, c, z = where_am_i()
        self.s_ref, self.w_ref, self.wbuf = s_ref, w_ref, wbuf
        self.sems = zs, zr, ps, pr, own_sem, load_sem
        (yf, xf), (yg, xg), (yd, xd) = trade_partners(y, x, c, z)
        self.z, self.r = z, row_of(y, x, c)
        self.c, self.q, self.qf = c, y * 2 + x, yf * 2 + xf
        self.zpeers = [(self.r, lax.rem(z + k, 4)) for k in (1, 2, 3)]
        self.pf, self.pg, self.sib = (row_of(yf, xf, c), z), (row_of(yg, xg, c), z), (row_of(y, x, 1 - c), z)

    def cols(self, t):
        layer, col, width = PIECES[t]
        return layer, pl.ds(col, width)

    def zcopy(self, t, k):
        layer, cs = self.cols(t)
        zs, zr = self.sems[:2]
        return remote(
            self.s_ref.at[layer, :, cs], self.w_ref.at[layer, self.z, self.q, self.c, :, cs],
            zs.at[t, k], zr.at[t, k], self.zpeers[k],
        )

    def own(self, t):
        layer, cs = self.cols(t)
        return pltpu.make_async_copy(
            self.s_ref.at[layer, :, cs], self.w_ref.at[layer, self.z, self.q, self.c, :, cs], self.sems[4].at[t]
        )

    def hop(self, t, which):
        layer, cs = self.cols(t)
        chip, peer = (
            (self.q, self.pf), (self.q, self.pg), (self.qf, self.pg), (slice(None), self.sib)
        )[which]
        block = self.w_ref.at[layer, :, chip, self.c, :, cs]
        return remote(block, block, self.sems[2].at[t, which], self.sems[3].at[t, which], peer)

    def load(self, t):
        layer, cs = self.cols(t)
        return pltpu.make_async_copy(self.w_ref.at[layer, :, :, :, :, cs], self.wbuf.at[:, :, :, :, cs], self.sems[5].at[t])

    def step(self, name, t):
        if name == "Z":
            for k in range(3):
                self.zcopy(t, k).start()
            self.own(t).start()
        elif name == "z":
            for k in range(3):
                self.zcopy(t, k).wait()
            self.own(t).wait()
            for which in (0, 1):
                self.hop(t, which).start()
        elif name == "f":
            self.hop(t, 0).wait()
            self.hop(t, 2).start()
        elif name == "g":
            self.hop(t, 1).wait()
            self.hop(t, 2).wait()
            self.hop(t, 3).start()
        elif name == "s":
            self.hop(t, 3).wait()
        elif name == "L":
            self.load(t).start()
        elif name == "l":
            self.load(t).wait()


PLAN = {
    "start": "Z0",
    "first": "z0Z1f0z1Z2g0f1Z3g1s0L0s1L1z2Z4l0l1",
    "sent0": "z3Z5f2z4Z6",
    "heads0": ["f3z5Z7", "g2s2L2", "f4z6Z8", "g3s3L3", "f5"],
    "osent0": "l2g4z7Z9",
    "up0": ["s4L4", "", "f6z8Za", "g5", "l3", "", "s5L5", "z9f7"],
    "down0": ["l4", "l5"],
    "qkv1": "g6s6L6l6",
    "sent1": "f8g7za",
    "heads1": ["f9g8s7L7", "", "s8L8", "fag9", "s9L9"],
    "osent1": "ga",
    "up1": ["l7sa", "", "", "", "l8La", "", "", ""],
    "down1": ["l9", "la"],
}


def swap_partner(y, x, c, z):
    return row_of(y, x, 1 - c), lax.rem(z + 2, 4)


def move_tokens(src, dst, send, recv, then):
    y, x, c, z = where_am_i()
    goes = c != z // 2
    copy = remote(src, dst, send, recv, swap_partner(y, x, c, z))
    stay = pltpu.make_async_copy(src, dst, send)

    @pl.when(goes)
    def _():
        copy.wait() if then else copy.start()

    @pl.when(jnp.logical_not(goes))
    def _():
        stay.wait() if then else stay.start()


SAVED = ("x", "xm", "o", "hdn", "gp", "q", "k", "v", "oh", "lse")


def forward_kernel(hid_ref, cot_ref, seg_ref, vec_ref, s_ref,
                   w_ref, xo_ref, dx_ref, segr_ref, segc_ref,
                   x_out, xm_out, o_out, hdn_out, gp_out, q_out, k_out, v_out, oh_out, lse_out,
                   wbuf, hid, xcur, xm_s, o_s, hdn_s, gp_s, q_s, k_s, v_s, oh_s, lse_s,
                   abuf, ubuf, pbuf, segbuf, sbuf0, sbuf1, rbuf0, rbuf1, osbuf, orbuf, vt, ot,
                   zs, zr, ps, pr, own_sem, load_sem, ss, rs, oss, ors, save_sem, mv_s, mv_r):
    y, x, c, z = where_am_i()
    me, peer_of = attention_peers(y, x, c, z)
    sbufs, rbufs = (sbuf0, sbuf1), (rbuf0, rbuf1)
    net = Gather(s_ref, w_ref, wbuf, zs, zr, ps, pr, own_sem, load_sem)
    zx = z + 1 - 2 * lax.rem(z, 2)
    greet(net.zpeers + [net.pf, net.pg, net.sib, (row_of(y, x, 1 - c), zx), swap_partner(y, x, c, z)])
    move_tokens(hid_ref, hid, mv_s.at[0], mv_r.at[0], 0)
    seg_copy = remote(seg_ref, segbuf.at[1], mv_s.at[1], mv_r.at[1], net.sib)
    seg_copy.start()
    net.run(PLAN["start"])
    move_tokens(hid_ref, hid, mv_s.at[0], mv_r.at[0], 1)
    seg_copy.wait()
    segbuf[0] = seg_ref[...]
    segr_ref[...] = jnp.where(c == z // 2, segbuf[0], segbuf[1])
    segc_ref[...] = jnp.broadcast_to(segr_ref[...].astype(F32), (8, 1280)).T[:, 0:1].astype(jnp.int32)
    xcur[...] = hid[...].astype(F32)

    kept = dict(zip(SAVED, (
        (xcur, x_out), (xm_s, xm_out), (o_s, o_out), (hdn_s, hdn_out), (gp_s, gp_out),
        (q_s, q_out), (k_s, k_out), (v_s, v_out), (oh_s, oh_out), (lse_s, lse_out))))

    def save(name, layer):
        src, dst = kept[name]
        return pltpu.make_async_copy(src, dst.at[layer], save_sem.at[layer, SAVED.index(name)])

    def held(i, col, width):
        return wbuf[i, :, :, :, col : col + width].reshape(640, width)

    def before(name, layer):
        if layer:
            save(name, layer - 1).wait()

    for layer in range(LAYERS):
        vl = vec_ref.at[pl.ds(layer, 1), :]
        save("x", layer).start()
        n1, _ = norm_parts(xcur[...])
        a = (n1 * piece(vl, 0) + piece(vl, 640)).astype(BF16)
        net.run(PLAN["qkv1" if layer else "first"])
        abuf[...] = a

        for i in range(4):
            pbuf[i] = dot(abuf[...], held(i, 0, 512))

        blocks = [pbuf[b // 3, :, (b % 3) * HW : (b % 3 + 1) * HW] for b in range(12)]
        for b in range(4):
            q = blocks[b] + vl[0:1, 1280 + HW * b : 1280 + HW * (b + 1)]
            v = blocks[8 + b] + vl[0:1, 1920 + HW * b : 1920 + HW * (b + 1)]
            for g in range(2):
                sbufs[g][b] = pack_group(g, (q, blocks[4 + b], v))
        copies = exchange(me, peer_of, sbufs[0], rbufs[0], ss.at[layer, 0], rs.at[layer, 0])
        for name in ("q", "k", "v", "oh", "lse"):
            before(name, layer)
        if layer == 0:
            k_s[...] = jnp.zeros_like(k_s)
        net.run(PLAN["sent%d" % layer])
        lse_s[...] = jnp.zeros_like(lse_s)

        for g, (first, heads, _) in enumerate(GROUPS):
            rbufs[g][me] = sbufs[g][me]
            for cp in copies:
                cp.wait()
            if g == 0:
                copies = exchange(me, peer_of, sbufs[1], rbufs[1], ss.at[layer, 1], rs.at[layer, 1])
            cut = slice(first * HDIM, (first + heads) * HDIM)
            for b in range(4):
                rows = slice(320 * b, 320 * (b + 1))
                for kind, ref in enumerate((q_s, k_s, v_s)):
                    ref[rows, cut] = unpack_group(g, rbufs[g][b], kind).astype(BF16)
            wide = 128 if g == 0 else HW
            vt[cut, :] = v_s[:, 0:wide].astype(F32).T[cut, :].astype(BF16)
            if g == 1:
                for name in ("q", "k", "v"):
                    save(name, layer).start()

            @pl.loop(first, first + heads)
            def _(h):
                net.run_at(PLAN["heads%d" % layer][first : first + heads], h - first)

                @pl.loop(0, 5, unroll=5)
                def _(step):
                    at = pl.multiple_of(step * QB, QB)
                    qm = jnp.where(head_mask(h, QB), q_s[pl.ds(at, QB), :], jnp.zeros((), BF16))
                    s = dot_nt(k_s[...], qm)
                    s = jnp.where(segc_ref[...] == segr_ref[0:1, pl.ds(at, QB)], s, negative)
                    top = jnp.max(s, axis=0, keepdims=True)
                    p = jnp.exp2(s * SCALE2 - top * SCALE2)
                    total = jnp.sum(p, axis=0, keepdims=True)
                    rows = pl.ds(pl.multiple_of(h * HDIM, HDIM), HDIM)
                    ot[rows, pl.ds(at, QB)] = dot(vt[rows, :], p.astype(BF16)) / total
                    lse_s[pl.ds(h, 1), pl.ds(at, QB)] = top * SCALE2 + jnp.log2(total)

        save("lse", layer).start()
        oh_s[...] = ot[...].T.astype(BF16)
        save("oh", layer).start()
        for b in range(4):
            osbuf[b] = fold(oh_s[320 * b : 320 * (b + 1), :].astype(F32), 4).astype(BF16)
        copies = exchange(me, peer_of, osbuf, orbuf, oss.at[layer], ors.at[layer])
        orbuf[me] = osbuf[me]
        for name in ("o", "xm", "hdn", "gp"):
            before(name, layer)
        net.run(PLAN["osent%d" % layer])
        for cp in copies:
            cp.wait()
        for j in range(4):
            o_s[80 * j : 80 * (j + 1), :] = jnp.concatenate(
                [orbuf[b, :, HW * j : HW * (j + 1)].astype(F32) for b in range(4)], axis=1
            ).astype(BF16)
        save("o", layer).start()

        for i in range(4):
            pbuf[i, :, 0:256] = dot(o_s[...], held(i, 384, 256))

        yv = jnp.concatenate([pbuf[i, :, 96:256] for i in range(4)], axis=1)
        xm = xcur[...] + (yv + piece(vl, 2560))
        xm_s[...] = xm
        save("xm", layer).start()
        n2, _ = norm_parts(xm)
        abuf[...] = (n2 * piece(vl, 3200) + piece(vl, 3840)).astype(BF16)
        if layer == 0:
            move_tokens(cot_ref, dx_ref, mv_s.at[2], mv_r.at[2], 0)

        for half in range(2):
            @pl.loop(0, 4)
            def _(i):
                net.run_at(PLAN["up%d" % layer][4 * half : 4 * half + 4], i)

                to = pl.multiple_of(i * 1280 + half * 640, 640)
                ubuf[...] = dot(abuf[...], held(i, 640 * (half + 1), 640)) + vl[0:1, pl.ds(5120 + to, 640)]

                @pl.loop(0, 10)
                def _(j):
                    rows = pl.ds(pl.multiple_of(j * 32, 32), 32)
                    u = ubuf[rows, :]
                    cdf = 0.5 * (1.0 + lax.erf(u * (0.5**0.5)))
                    hdn_s[rows, pl.ds(to, 640)] = (u * cdf).astype(BF16)
                    gp_s[rows, pl.ds(to, 640)] = (
                        cdf + u * (jnp.exp(-0.5 * u * u) * 0.3989422804014327)
                    ).astype(BF16)

        save("hdn", layer).start()
        save("gp", layer).start()
        save("x", layer).wait()
        xcur[...] = xm_s[...] + piece(vl, 4480)
        for half in range(2):
            net.run(PLAN["down%d" % layer][half])

            @pl.loop(0, 4)
            def _(i):
                to = pl.multiple_of(i * 1280 + half * 640, 640)
                xcur[...] += dot_nt(hdn_s[:, pl.ds(to, 640)], held(i, 640 * (half + 3), 640))


    xo_ref[...] = xcur[...]
    for name in SAVED[1:]:
        save(name, LAYERS - 1).wait()
    move_tokens(cot_ref, dx_ref, mv_s.at[2], mv_r.at[2], 1)


def forward_all(hidden, cotangent, segments, vectors, shards):
    dma = pltpu.SemaphoreType.DMA
    sds = jax.ShapeDtypeStruct
    vmem = pltpu.VMEM
    return pl.pallas_call(
        forward_kernel,
        name="forward",
        out_shape=(
            sds((LAYERS, 4, 4, 2, 80, 3200), BF16), sds((320, 640), F32), sds((320, 640), F32),
            sds((1, 1280), jnp.int32), sds((1280, 1), jnp.int32),
            sds((LAYERS, 320, 640), F32), sds((LAYERS, 320, 640), F32), sds((LAYERS, 320, 640), BF16),
            sds((LAYERS, 320, 5120), BF16), sds((LAYERS, 320, 5120), BF16),
            sds((LAYERS, 1280, HW), BF16), sds((LAYERS, 1280, HW), BF16), sds((LAYERS, 1280, HW), BF16),
            sds((LAYERS, 1280, HW), BF16), sds((LAYERS, 8, 1280), F32),
        ),
        in_specs=[ANY, ANY, VM, VM, ANY],
        out_specs=(ANY, VM, ANY, VM, VM) + (ANY,) * 10,
        scratch_shapes=[
            vmem((4, 4, 2, 80, 3200), BF16), vmem((320, 640), BF16), vmem((320, 640), F32),
            vmem((320, 640), F32), vmem((320, 640), BF16), vmem((320, 5120), BF16), vmem((320, 5120), BF16),
            vmem((1280, HW), BF16), vmem((1280, HW), BF16), vmem((1280, HW), BF16), vmem((1280, HW), BF16),
            vmem((8, 1280), F32),
            vmem((320, 640), BF16), vmem((320, 640), F32), vmem((4, 320, 512), F32), vmem((2, 1, 1280), jnp.int32),
            *[vmem(shape, BF16) for shape in group_shapes() * 2],
            vmem((4, 80, 640), BF16), vmem((4, 80, 640), BF16),
            vmem((HW, 1280), BF16), vmem((HW, 1280), F32),
            *[dma((len(PIECES),) + shape) for shape in ((3,), (3,), (4,), (4,), (), ())],
            dma((LAYERS, 2, 4)), dma((LAYERS, 2, 4)), dma((LAYERS, 4)), dma((LAYERS, 4)),
            dma((LAYERS, len(SAVED))), dma((3,)), dma((3,)),
        ],
        compiler_params=pltpu.CompilerParams(
            collective_id=0, has_side_effects=True, vmem_limit_bytes=56 << 20
        ),
    )(hidden, cotangent, segments, vectors, shards)


def norm_back(dy, n, spread, gain):
    dn = dy * gain
    mean1 = jnp.mean(dn, axis=-1, keepdims=True)
    mean2 = jnp.mean(dn * n, axis=-1, keepdims=True)
    return spread * (dn - mean1 - n * mean2)


def col_sum(values):
    return jnp.sum(values, axis=0, keepdims=True)


ORDER = (3, 1, 4, 2, 0)
OWN, LAND = 4, 2
HELD = {(1, 3): 0, (1, 1): 1, (1, 4): 2, (1, 2): 3, (1, 0): 0, (0, 3): 1, (0, 1): 2, (0, 4): 3, (0, 2): 0, (0, 0): 1}


class Scatter(Steps):
    def __init__(self, g_ref, out_ref, own, sibr, p2r, p1r, zr, fin, fsem, sems):
        y, x, c, z = where_am_i()
        (yf, xf), (yg, xg), (yd, xd) = trade_partners(y, x, c, z)
        self.c, self.z = c, z
        self.q, self.qf, self.qg, self.qd = y * 2 + x, yf * 2 + xf, yg * 2 + xg, yd * 2 + xd
        r = row_of(y, x, c)
        self.zpeers = [(r, lax.rem(z + k, 4)) for k in (1, 2, 3)]
        self.pf, self.pg = (self.qf * 2 + c, z), (self.qg * 2 + c, z)
        self.sib = (row_of(y, x, 1 - c), z)
        self.g_ref, self.out_ref = g_ref, out_ref
        self.own, self.sibr, self.p2r, self.p1r, self.zr = own, sibr, p2r, p1r, zr
        self.fin, self.fsem, self.sems = fin, fsem, sems

    def where(self, t):
        return LAYERS - 1 - t // 5, ORDER[t % 5] * CHUNK

    def part(self, t, core):
        layer, col = self.where(t)
        return self.g_ref.at[layer, :, :, core, :, pl.ds(col, CHUNK)]

    def own_copy(self, t):
        return pltpu.make_async_copy(self.part(t, self.c), self.own.at[t % OWN], self.sems[0].at[t % OWN])

    def sib_copy(self, t):
        k = t % LAND
        return remote(
            self.part(t, 1 - self.c), self.sibr.at[k], self.sems[1].at[k], self.sems[2].at[k], self.sib
        )

    def p2_copy(self, t, j):
        k = t % LAND
        return remote(
            self.own.at[t % OWN, :, (self.qg, self.qd)[j]], self.p2r.at[k, j],
            self.sems[3].at[k, j], self.sems[4].at[k, j], self.pg,
        )

    def p1_copy(self, t):
        k = t % LAND
        return remote(
            self.own.at[t % OWN, :, self.qf], self.p1r.at[k], self.sems[5].at[k], self.sems[6].at[k], self.pf
        )

    def z_copy(self, t, j):
        k = t % LAND
        return remote(
            self.own.at[t % OWN, lax.rem(self.z + j + 1, 4), self.q], self.zr.at[k, j],
            self.sems[7].at[k, j], self.sems[8].at[k, j], self.zpeers[j],
        )

    def put_out(self, t):
        layer, col = self.where(t)
        k = t % LAND
        return pltpu.make_async_copy(self.fin.at[k], self.out_ref.at[layer, :, pl.ds(col, CHUNK)], self.fsem.at[k])

    def add(self, dst, src):
        @pl.loop(0, 4)
        def _(i):
            dst[i] = dst[i] + src[i]

    def step(self, name, t):
        own = self.own.at[t % OWN]
        k = t % LAND
        if name == "a":
            self.sib_copy(t).start()
            self.own_copy(t).start()
        elif name == "b":
            self.sib_copy(t).wait()
            self.own_copy(t).wait()
            self.add(own, self.sibr.at[k])

            for j in range(2):
                self.p2_copy(t, j).start()
        elif name == "c":
            for j in range(2):
                self.p2_copy(t, j).wait()
            self.add(own.at[:, self.q], self.p2r.at[k, 0])
            self.add(own.at[:, self.qf], self.p2r.at[k, 1])
            self.p1_copy(t).start()
        elif name == "d":
            self.p1_copy(t).wait()
            self.add(own.at[:, self.q], self.p1r.at[k])
            for j in range(3):
                self.z_copy(t, j).start()
        elif name == "e":
            for j in range(3):
                self.z_copy(t, j).wait()
            total = own[self.z, self.q].astype(F32)
            for j in range(3):
                total = total + self.zr[k, j].astype(F32)
            if t >= LAND:
                self.put_out(t - LAND).wait()
            self.fin[k] = total
            self.put_out(t).start()


BACK = {
    "f1": ["", "", "", "", "a0", "", "b0", "a1"],
    "ffn1": "",
    "wo1": "c0b1a2",
    "heads1": ["", "", "d0", "c1b2", ""],
    "psent1": "a3e0d1c2b3",
    "end1": "a4",
    "f0": ["e1d2c3", "b4", "", "", "e2d3a5", "c4", "", "b5e3d4"],
    "ffn0": "",
    "wo0": "a6c5e4b6a7",
    "heads0": ["", "d5", "c6b7", "", "e5d6a8c7"],
    "psent0": "b8e6",
    "end0": ["a9", "d7c8", "b9e7", "d8", "c9e8", "d9e9"],
}


def backward_kernel(dx_ref, last_ref, xs_ref, xms_ref, os_ref, hdns_ref, gps_ref, qs_ref, ks_ref, vs_ref, ohs_ref, lses_ref,
                    vec_ref, segr_ref, segc_ref, w_ref,
                    hout_ref, gin_ref, gv_ref, gout_ref, g_ref,
                    wbuf, x_s, xm_s, o_s, hdn_s, gp_s, q_s, k_s, v_s, oh_s, lse_s,
                    gbuf, at_s, dy, dyt, da2, dosend, dorecv, dos, kt, dqt, dk, dv, delta, psend0, psend1, precv0, precv1, dp4,
                    own, sibr, p2r, p1r, zr, fin, dxo_ref, vgot, dpad,
                    wsem, lsem, gsem, ss, rs, oss, ors, fsem, mv_s, mv_r, vs_sem, vr_sem, *net_sems):
    y, x, c, z = where_am_i()
    me, peer_of = attention_peers(y, x, c, z)
    psends, precvs = (psend0, psend1), (precv0, precv1)
    net = Scatter(g_ref, gout_ref, own, sibr, p2r, p1r, zr, fin, fsem, net_sems)

    def load_w(layer, i):
        return pltpu.make_async_copy(w_ref.at[layer, :, :, pl.ds(i * CHUNK, CHUNK)], wbuf.at[HELD[layer, i]], wsem.at[i])

    saved = {
        "x": (xs_ref, x_s), "xm": (xms_ref, xm_s), "o": (os_ref, o_s), "hdn": (hdns_ref, hdn_s), "gp": (gps_ref, gp_s),
        "q": (qs_ref, q_s), "k": (ks_ref, k_s), "v": (vs_ref, v_s), "oh": (ohs_ref, oh_s), "lse": (lses_ref, lse_s),
    }

    def load(name, layer):
        src, dst = saved[name]
        return pltpu.make_async_copy(src.at[layer], dst, lsem.at[SAVED.index(name)])

    def fetch(layer, names):
        for name in names:
            if isinstance(name, int):
                load_w(layer, name).start()
            else:
                load(name, layer).start()

    def arrive(layer, *names):
        for name in names:
            if isinstance(name, int):
                load_w(layer, name).wait()
            else:
                load(name, layer).wait()

    fetch(1, ["xm", "hdn", "gp", 3, 1, 4, 2, "k", "q", "v", "oh", "lse", "o", "x"])
    zx = z + 1 - 2 * lax.rem(z, 2)
    greet(net.zpeers + [net.pf, net.pg, net.sib, (row_of(y, x, 1 - c), zx), swap_partner(y, x, c, z)])
    move_tokens(last_ref, hout_ref, mv_s.at[0], mv_r.at[0], 0)
    dxo_ref[...] = dx_ref[...]

    ends = [net.sib, (row_of(y, 1 - x, c), z), (row_of(1 - y, x, c), z), (row_of(y, x, c), zx),
            (row_of(y, x, c), lax.rem(z + 2, 4))]

    def vector_hop(k):
        return remote(gv_ref, vgot.at[k], vs_sem.at[k], vr_sem.at[k], ends[k])

    for layer in reversed(range(LAYERS)):
        vl = vec_ref.at[pl.ds(layer, 1), :]
        gl = gv_ref.at[pl.ds(layer, 1), :]
        dy[...] = dxo_ref[...].astype(BF16)
        dyf = dy[...].astype(F32)
        dyt[...] = dyf.T.astype(BF16)
        gl[0:1, 4480:5120] = col_sum(dyf)
        arrive(layer, "xm")
        n2, spread2 = norm_parts(xm_s[...])
        g2 = piece(vl, 3200)
        at_s[...] = (n2 * g2 + piece(vl, 3840)).T.astype(BF16)
        da2[...] = jnp.zeros_like(da2)
        arrive(layer, "hdn", "gp")

        def put(slot, i, col):
            return pltpu.make_async_copy(gbuf.at[slot], g_ref.at[layer, i, :, :, :, pl.ds(col, CHUNK)], gsem.at[slot])

        for half in range(2):
            arrive(layer, 3 + half, 1 + half)

            @pl.loop(0, 4)
            def _(i):
                net.run_at(BACK["f%d" % layer][4 * half : 4 * half + 4], i)
                to = pl.multiple_of(i * 1280 + half * CHUNK, CHUNK)

                gdown = dot(dyt[...], hdn_s[:, pl.ds(to, CHUNK)]).astype(BF16)

                @pl.when(i > 0)
                def _():
                    put(0, 0, 0).wait()

                gbuf[0] = gdown.reshape(4, 2, 80, CHUNK)
                put(0, i, 1920 + half * CHUNK).start()
                dh = dot(dy[...], wbuf[HELD[layer, 3 + half], i])
                du = (dh * gp_s[:, pl.ds(to, CHUNK)].astype(F32)).astype(BF16)
                gl[0:1, pl.ds(5120 + to, CHUNK)] = col_sum(du.astype(F32))
                gup = dot(at_s[...], du).astype(BF16)

                @pl.when(i > 0)
                def _():
                    put(1, 0, 0).wait()

                gbuf[1] = gup.reshape(4, 2, 80, CHUNK)
                put(1, i, 640 + half * CHUNK).start()
                da2[...] += dot_nt(du, wbuf[HELD[layer, 1 + half], i])

            put(0, 0, 0).wait()
            put(1, 0, 0).wait()
            if half == 0:
                fetch(layer, [0])
            elif layer:
                fetch(layer - 1, [3, 1, 4])
            if half:
                net.run(BACK["ffn%d" % layer])

        da2v = da2[...]
        gl[0:1, 3200:3840] = col_sum(da2v * n2)
        gl[0:1, 3840:4480] = col_sum(da2v)
        dxm = dxo_ref[...] + norm_back(da2v, n2, spread2, g2)
        dxo_ref[...] = dxm
        if layer:
            fetch(layer - 1, ["hdn", "gp", "xm"])
        dy1f = dxm.astype(BF16).astype(F32)
        dy[...] = dxm.astype(BF16)
        gl[0:1, 2560:3200] = col_sum(dy1f)
        arrive(layer, 0)
        wa = wbuf.at[HELD[layer, 0]]
        zpad = jnp.zeros((320, 96), F32)
        for i in range(4):
            dpad[i] = jnp.concatenate([zpad, dy1f[:, HW * i : HW * (i + 1)]], axis=1).astype(BF16)
        da2[...] = jnp.zeros_like(da2)

        for i in range(4):
            da2[...] += dot_nt(dpad[i], wa[i, :, 384:640])

        for b in range(4):
            dosend[b] = fold(da2[:, HW * b : HW * (b + 1)], 4).astype(BF16)
        copies = exchange(me, peer_of, dosend, dorecv, oss.at[layer], ors.at[layer])
        dorecv[me] = dosend[me]
        arrive(layer, "k", "q", "v", "oh", "lse")
        kt[...] = k_s[...].astype(F32).T.astype(BF16)
        dk[...] = jnp.zeros_like(dk)
        dv[...] = jnp.zeros_like(dv)
        net.run(BACK["wo%d" % layer])
        for cp in copies:
            cp.wait()
        for b in range(4):
            for j in range(4):
                dos[320 * b + 80 * j : 320 * b + 80 * (j + 1), :] = (
                    dorecv[b, :, HW * j : HW * (j + 1)].astype(F32).astype(BF16)
                )
        lane = lax.broadcasted_iota(jnp.int32, (8, HW), 1)
        head = lax.broadcasted_iota(jnp.int32, (8, HW), 0)
        pick = jnp.where((lane >= head * HDIM) & (lane < (head + 1) * HDIM), 1.0, 0.0).astype(F32)
        delta[...] = lax.dot_general(
            pick, dos[...].astype(F32) * oh_s[...].astype(F32), NT,
            precision=lax.Precision.HIGHEST, preferred_element_type=F32,
        )

        groups = {}
        for g in (1, 0):
            first, heads, _ = GROUPS[g]
            plans = BACK["heads%d" % layer][0:3] if g else BACK["heads%d" % layer][3:5]

            @pl.loop(first, first + heads)
            def _(h):
                net.run_at(plans, h - first)

                @pl.loop(0, 5, unroll=5)
                def _(step):
                    at = pl.multiple_of(step * QB, QB)
                    zero = jnp.zeros((), BF16)
                    mask = head_mask(h, QB)
                    qm = jnp.where(mask, q_s[pl.ds(at, QB), :], zero)
                    dm = jnp.where(mask, dos[pl.ds(at, QB), :], zero)
                    s = dot_nt(k_s[...], qm)
                    s = jnp.where(segc_ref[...] == segr_ref[0:1, pl.ds(at, QB)], s, negative)
                    p = jnp.exp2(s * SCALE2 - lse_s[pl.ds(h, 1), pl.ds(at, QB)])
                    dp = dot_nt(v_s[...], dm)
                    ds = (p * (dp - delta[pl.ds(h, 1), pl.ds(at, QB)])).astype(BF16)
                    dv[...] += dot(p.astype(BF16), dm)
                    dk[...] += dot(ds, qm)
                    rows = pl.ds(pl.multiple_of(h * HDIM, HDIM), HDIM)
                    dqt[rows, pl.ds(at, QB)] = dot(kt[rows, :], ds)

            if layer and g == 0:
                fetch(layer - 1, ["k", "q", "v", "oh", "lse"])
            dq = dqt[...].T * SCALE
            for b in range(4):
                rows = slice(320 * b, 320 * (b + 1))
                psends[g][b] = pack_group(g, (dq[rows], dk[rows, :] * SCALE, dv[rows, :]))
            groups[g] = exchange(me, peer_of, psends[g], precvs[g], ss.at[layer, g], rs.at[layer, g])
            precvs[g][me] = psends[g][me]
        copies = groups[1] + groups[0]
        zpad = jnp.zeros((320, 32), F32)
        arrive(layer, "x", "o")
        n1, spread1 = norm_parts(x_s[...])
        g1 = piece(vl, 0)
        at_s[...] = (n1 * g1 + piece(vl, 640)).T.astype(BF16)
        dyt[...] = o_s[...].astype(F32).T.astype(BF16)
        if layer:
            fetch(layer - 1, ["x", "o"])
        net.run(BACK["psent%d" % layer])
        for cp in copies:
            cp.wait()
        blocks = []
        for kind in range(3):
            own_kind = [
                jnp.concatenate([unpack_group(g, precvs[g][b], kind) for g in range(2)], axis=1) for b in range(4)
            ]
            if kind != 1:
                at = 1280 if kind == 0 else 1920
                gl[0:1, at : at + 640] = jnp.concatenate([col_sum(part) for part in own_kind], axis=1)
            blocks += own_kind
        for i in range(4):
            dp4[i] = jnp.concatenate(blocks[3 * i : 3 * i + 3] + [zpad], axis=1).astype(BF16)
        da2[...] = jnp.zeros_like(da2)

        for i in range(4):
            slot = i % 2
            part = dot(at_s[...], dp4[i])
            rest = dot(dyt[...], dpad[i])
            if i > 1:
                put(slot, 0, 0).wait()

            gbuf[slot, :, :, :, 0:384] = part[:, 0:384].astype(BF16).reshape(4, 2, 80, 384)
            gbuf[slot, :, :, :, 384:512] = (part[:, 384:512] + rest[:, 0:128]).astype(BF16).reshape(4, 2, 80, 128)
            gbuf[slot, :, :, :, 512:640] = rest[:, 128:256].astype(BF16).reshape(4, 2, 80, 128)
            put(slot, i, 0).start()
            da2[...] += dot_nt(dp4[i], wa[i, :, 0:512])

        da = da2[...]
        if layer:
            fetch(layer - 1, [2])
        gl[0:1, 0:640] = col_sum(da * n1)
        gl[0:1, 640:1280] = col_sum(da)
        dxo_ref[...] = dxo_ref[...] + norm_back(da, n1, spread1, g1)
        put(0, 0, 0).wait()
        put(1, 0, 0).wait()
        if layer:
            net.run(BACK["end%d" % layer])
    move_tokens(dxo_ref, gin_ref, mv_s.at[1], mv_r.at[1], 0)
    for k, plan in enumerate(BACK["end0"]):
        if k:
            vector_hop(k - 1).wait()
            gv_ref[...] += vgot[k - 1]
        if k < 5:
            vector_hop(k).start()
        net.run(plan)
    for t in range(NCH - LAND, NCH):
        net.put_out(t).wait()
    move_tokens(last_ref, hout_ref, mv_s.at[0], mv_r.at[0], 1)
    move_tokens(dxo_ref, gin_ref, mv_s.at[1], mv_r.at[1], 1)


def backward_all(dx, last, kept, vec, segr, segc, weights):
    dma = pltpu.SemaphoreType.DMA
    sds = jax.ShapeDtypeStruct
    vmem = pltpu.VMEM
    return pl.pallas_call(
        backward_kernel,
        name="backward",
        out_shape=(
            sds((320, 640), F32), sds((320, 640), F32), sds((LAYERS, 10240), F32), sds((LAYERS, 80, 3200), F32),
            sds((LAYERS, 4, 4, 2, 80, 3200), BF16),
        ),
        in_specs=[VM] + [ANY] * 11 + [VM, VM, VM, ANY],
        out_specs=(ANY, ANY, VM, ANY, ANY),
        scratch_shapes=[
            vmem((4, 4, 640, CHUNK), BF16),
            vmem((320, 640), F32), vmem((320, 640), F32), vmem((320, 640), BF16),
            vmem((320, 5120), BF16), vmem((320, 5120), BF16),
            vmem((1280, HW), BF16), vmem((1280, HW), BF16), vmem((1280, HW), BF16), vmem((1280, HW), BF16),
            vmem((8, 1280), F32),
            vmem((2, 4, 2, 80, CHUNK), BF16), vmem((640, 320), BF16),
            vmem((320, 640), BF16), vmem((640, 320), BF16), vmem((320, 640), F32),
            vmem((4, 80, 640), BF16), vmem((4, 80, 640), BF16), vmem((1280, HW), BF16),
            vmem((HW, 1280), BF16), vmem((HW, 1280), F32),
            vmem((1280, HW), F32), vmem((1280, HW), F32), vmem((8, 1280), F32),
            *[vmem(shape, BF16) for shape in group_shapes() * 2], vmem((4, 320, 512), BF16),
            vmem((OWN, 4, 4, 80, CHUNK), BF16), vmem((LAND, 4, 4, 80, CHUNK), BF16),
            vmem((LAND, 2, 4, 80, CHUNK), BF16), vmem((LAND, 4, 80, CHUNK), BF16), vmem((LAND, 3, 80, CHUNK), BF16),
            vmem((LAND, 80, CHUNK), F32), vmem((320, 640), F32), vmem((5, LAYERS, 10240), F32),
            vmem((4, 320, 256), BF16),
            dma((5,)), dma((len(SAVED),)), dma((2,)),
            dma((LAYERS, 2, 4)), dma((LAYERS, 2, 4)), dma((LAYERS, 4)), dma((LAYERS, 4)), dma((LAND,)),
            dma((2,)), dma((2,)), dma((5,)), dma((5,)),
            dma((OWN,)), dma((LAND,)), dma((LAND,)), dma((LAND, 2)), dma((LAND, 2)),
            dma((LAND,)), dma((LAND,)), dma((LAND, 3)), dma((LAND, 3)),
        ],
        compiler_params=pltpu.CompilerParams(
            collective_id=1, has_side_effects=True, vmem_limit_bytes=60 << 20
        ),
    )(dx, last, *kept, vec, segr, segc, weights)


def per_device_fast(
    hidden_in, cotangent, segment_ids, w_qkv, w_out, w_up, w_down, vectors,
    m_qkv, v_qkv, m_out, v_out, m_up, v_up, m_down, v_down, m_vectors, v_vectors,
):
    depth = w_qkv.shape[0]
    shards = jnp.concatenate(
        [w_qkv.astype(BF16), w_out.astype(BF16), w_up.astype(BF16), w_down.astype(BF16).transpose(0, 2, 1)], axis=2
    )
    weights, x, dx, segr, segc, *kept = forward_all(hidden_in, cotangent, segment_ids, vectors, shards)
    hidden_out, grad_in, grad_vectors, grad_all, _ = backward_all(
        dx, x, kept, vectors, segr, segc, weights.reshape(depth, 4, 640, 3200)
    )
    gradients = (
        grad_all[:, :, 0:480], grad_all[:, :, 480:640], grad_all[:, :, 640:1920],
        grad_all[:, :, 1920:3200].transpose(0, 2, 1),
    )
    masters = (w_qkv, w_out, w_up, w_down)
    firsts = (m_qkv, m_out, m_up, m_down)
    seconds = (v_qkv, v_out, v_up, v_down)
    updates = [
        adam_direction(masters[kind], gradients[kind], firsts[kind], seconds[kind], 0.01) for kind in range(4)
    ]
    partial_sums = jnp.stack(
        [jnp.stack(matrix_sums(masters[kind], updates[kind][2]), axis=1) for kind in range(4)], axis=1
    )
    flat = jnp.pad(partial_sums.reshape(1, -1), ((0, 7), (0, 128 - partial_sums.size)))
    total_sums = total_over_devices(flat, 3)[0, : partial_sums.size].reshape(partial_sums.shape)
    lamb_norms = jnp.sqrt(total_sums)
    trust_ratio = lamb_norms[:, :, 0] / lamb_norms[:, :, 1]
    new_masters = [
        masters[kind] - 0.5 * trust_ratio[:, kind, None, None] * updates[kind][2] for kind in range(4)
    ]
    vec_first, vec_second, new_vectors = vector_update(vectors, grad_vectors, m_vectors, v_vectors)
    moments = [part for kind in range(4) for part in updates[kind][:2]]
    return (
        hidden_out, grad_in, *gradients, grad_vectors, *moments, vec_first, vec_second,
        *new_masters, new_vectors, *[w.astype(BF16) for w in new_masters], lamb_norms,
    )


def solution(mesh):
    fast = mesh.shape["row"] == 8 and mesh.shape["col"] == 4
    per_device = per_device_fast if fast else per_device_any
    return jax.shard_map(
        per_device,
        mesh=mesh,
        in_specs=(
            P(("row", "col"), None),
            P(("row", "col"), None),
            P("row", None),
            P(None, "row", "col"),
            P(None, "row", "col"),
            P(None, "row", "col"),
            P(None, "col", "row"),
            P(),
            P(None, "row", "col"),
            P(None, "row", "col"),
            P(None, "row", "col"),
            P(None, "row", "col"),
            P(None, "row", "col"),
            P(None, "row", "col"),
            P(None, "col", "row"),
            P(None, "col", "row"),
            P(),
            P(),
        ),
        out_specs=(
            P(("row", "col"), None),
            P(("row", "col"), None),
            P(None, "row", "col"),
            P(None, "row", "col"),
            P(None, "row", "col"),
            P(None, "col", "row"),
            P(),
            P(None, "row", "col"),
            P(None, "row", "col"),
            P(None, "row", "col"),
            P(None, "row", "col"),
            P(None, "row", "col"),
            P(None, "row", "col"),
            P(None, "col", "row"),
            P(None, "col", "row"),
            P(),
            P(),
            P(None, "row", "col"),
            P(None, "row", "col"),
            P(None, "row", "col"),
            P(None, "col", "row"),
            P(),
            P(None, "row", "col"),
            P(None, "row", "col"),
            P(None, "row", "col"),
            P(None, "col", "row"),
            P(),
        ),
        check_vma=False,
    )
```

```python
import functools
from functools import partial

import jax
import jax.numpy as jnp
from jax import lax
from jax.experimental import pallas as pl
from jax.experimental.pallas import tpu as pltpu
from jax.sharding import PartitionSpec as P

D = 640
HDIM = 32
FF = 5120
STEP = 5


head_groups = 4
negative = -1e30


def layer_norm(values_in, norm_gain, norm_bias):
    average = jnp.mean(values_in, axis=-1, keepdims=True)
    centered = values_in - average
    variance = jnp.mean(centered * centered, axis=-1, keepdims=True)
    return centered * lax.rsqrt(variance + 1e-05) * norm_gain + norm_bias


def to_groups(matrix):
    tokens = matrix.shape[0]
    return matrix.reshape(tokens, head_groups, -1, HDIM).transpose(1, 2, 0, 3)


def from_groups(blocks):
    return blocks.transpose(2, 0, 1, 3).reshape(blocks.shape[2], -1)


def contract_rows(left, right):
    return lax.dot_general(
        left, right, (((0,), (0,)), ((), ())), preferred_element_type=jnp.float32
    )


def contract_cols(left, right):
    return lax.dot_general(
        left, right, (((1,), (1,)), ((), ())), preferred_element_type=jnp.float32
    )


def column_total(matrix):
    return jnp.sum(matrix.astype(jnp.float32), axis=0)


def masked_scores(query_block, key_block, allowed):
    scores = jnp.einsum(
        "hqd,hkd->hqk", query_block, key_block, preferred_element_type=jnp.float32
    ) * HDIM ** (-0.5)
    return jnp.where(allowed[None, :, :], scores, negative)


def attend(queries, all_kv, allowed, kept_lse):
    features = queries.shape[1]
    tokens = queries.shape[0]
    q_groups = to_groups(queries)
    k_groups = to_groups(all_kv[:, :features])
    v_groups = to_groups(all_kv[:, features:])
    if kept_lse is None:

        def first_group(members):
            q_block, k_block, v_block = members
            scores = masked_scores(q_block, k_block, allowed)
            row_max = jnp.max(scores, axis=-1)
            log_total = row_max + jnp.log(jnp.sum(jnp.exp(scores - row_max[..., None]), axis=-1))
            softmax = jnp.exp(scores - log_total[..., None]).astype(jnp.bfloat16)
            return (
                jnp.einsum("hqk,hkd->hqd", softmax, v_block, preferred_element_type=jnp.float32),
                log_total,
            )

        attended, log_total = lax.map(first_group, (q_groups, k_groups, v_groups))
    else:
        log_total = kept_lse.reshape(head_groups, -1, tokens)

        def again_group(members):
            q_block, k_block, v_block, lse_block = members
            softmax = jnp.exp(
                masked_scores(q_block, k_block, allowed) - lse_block[..., None]
            ).astype(jnp.bfloat16)
            return jnp.einsum("hqk,hkd->hqd", softmax, v_block, preferred_element_type=jnp.float32)

        attended = lax.map(again_group, (q_groups, k_groups, v_groups, log_total))
    return (from_groups(attended).astype(jnp.bfloat16), log_total.reshape(-1, tokens))


def attention_back(queries, all_kv, grad_mixed, kept_lse, allowed):
    features = queries.shape[1]
    tokens = queries.shape[0]
    inv_root = HDIM ** (-0.5)
    q_groups = to_groups(queries)
    k_groups = to_groups(all_kv[:, :features])
    v_groups = to_groups(all_kv[:, features:])
    g_groups = to_groups(grad_mixed)
    lse_groups = kept_lse.reshape(head_groups, -1, tokens)

    def one_group(members):
        q_block, k_block, v_block, g_block, lse_block = members
        softmax = jnp.exp(masked_scores(q_block, k_block, allowed) - lse_block[..., None])
        grad_probs = jnp.einsum(
            "hqd,hkd->hqk", g_block, v_block, preferred_element_type=jnp.float32
        )
        row_dot = jnp.sum(softmax * grad_probs, axis=-1, keepdims=True)
        grad_scores = (softmax * (grad_probs - row_dot)).astype(jnp.bfloat16)
        grad_q = (
            jnp.einsum("hqk,hkd->hqd", grad_scores, k_block, preferred_element_type=jnp.float32)
            * inv_root
        )
        grad_k = (
            jnp.einsum("hqk,hqd->hkd", grad_scores, q_block, preferred_element_type=jnp.float32)
            * inv_root
        )
        grad_v = jnp.einsum(
            "hqk,hqd->hkd",
            softmax.astype(jnp.bfloat16),
            g_block,
            preferred_element_type=jnp.float32,
        )
        return (grad_q, grad_k, grad_v)

    grad_q, grad_k, grad_v = lax.map(
        one_group, (q_groups, k_groups, v_groups, g_groups, lse_groups)
    )
    return (
        from_groups(grad_q),
        jnp.concatenate([from_groups(grad_k), from_groups(grad_v)], axis=1),
    )


def layer_forward(state_in, weights, vector, allowed, kept_lse):
    w_qkv_full, w_out_full, w_up_part, w_down_part = weights
    features = state_in.shape[1]
    normed = layer_norm(state_in, vector[0:features], vector[features : 2 * features]).astype(
        jnp.bfloat16
    )
    projected = jnp.dot(normed, w_qkv_full, preferred_element_type=jnp.float32)
    queries = (projected[:, :features] + vector[2 * features : 3 * features]).astype(jnp.bfloat16)
    kv_bias = jnp.concatenate(
        [jnp.zeros((features,), jnp.float32), vector[3 * features : 4 * features]]
    )
    own_kv = (projected[:, features:] + kv_bias).astype(jnp.bfloat16)
    all_kv = lax.all_gather(own_kv, "col", axis=0, tiled=True)
    attended, log_total = attend(queries, all_kv, allowed, kept_lse)
    middle = state_in + (
        jnp.dot(attended, w_out_full, preferred_element_type=jnp.float32)
        + vector[4 * features : 5 * features]
    )
    normed_ffn = layer_norm(
        middle, vector[5 * features : 6 * features], vector[6 * features : 7 * features]
    ).astype(jnp.bfloat16)
    before = (
        jnp.dot(normed_ffn, w_up_part, preferred_element_type=jnp.float32) + vector[8 * features :]
    )
    hidden = jax.nn.gelu(before, approximate=False).astype(jnp.bfloat16)
    branch = jnp.dot(hidden, w_down_part, preferred_element_type=jnp.float32)
    state_out = middle + (branch + vector[7 * features : 8 * features])
    kept_vals = (normed, queries, all_kv, log_total, attended, middle, normed_ffn, before, hidden)
    return (state_out, kept_vals)


def layer_backward(grad_state, state_in, kept_vals, weights, vector, allowed):
    w_qkv_full, w_out_full, w_up_part, w_down_part = weights
    normed, queries, all_kv, log_total, attended, middle, ffn_rows, before, hidden = kept_vals
    features = state_in.shape[1]
    grad_branch = grad_state.astype(jnp.bfloat16)
    gelu_vjp = jax.vjp(partial(jax.nn.gelu, approximate=False), before)[1]
    grad_down = contract_rows(hidden, grad_branch)
    grad_before = gelu_vjp(contract_cols(grad_branch, w_down_part))[0].astype(jnp.bfloat16)
    grad_up = contract_rows(ffn_rows, grad_before)
    grad_up_bias = column_total(grad_before)
    grad_normed_ffn = contract_cols(grad_before, w_up_part)
    norm_two = jax.vjp(
        layer_norm, middle, vector[5 * features : 6 * features], vector[6 * features : 7 * features]
    )[1]
    grad_middle_norm, grad_gain_two, grad_bias_two = norm_two(grad_normed_ffn)
    grad_middle = grad_state + grad_middle_norm
    grad_attn_out = grad_middle.astype(jnp.bfloat16)
    grad_out_w = contract_rows(attended, grad_attn_out)
    grad_mixed = contract_cols(grad_attn_out, w_out_full).astype(jnp.bfloat16)
    grad_queries, kv_terms = attention_back(queries, all_kv, grad_mixed, log_total, allowed)
    grad_kv = lax.psum_scatter(
        kv_terms.astype(jnp.bfloat16), "col", scatter_dimension=0, tiled=True
    )
    grad_queries = grad_queries.astype(jnp.bfloat16)
    grad_proj = jnp.concatenate([grad_queries, grad_kv], axis=1)
    grad_qkv_w = contract_rows(normed, grad_proj)
    grad_normed = contract_cols(grad_proj, w_qkv_full)
    norm_one = jax.vjp(layer_norm, state_in, vector[0:features], vector[features : 2 * features])[1]
    grad_input_norm, grad_gain_one, grad_bias_one = norm_one(grad_normed)
    grad_input = grad_middle + grad_input_norm
    grad_vector = jnp.concatenate(
        [
            grad_gain_one,
            grad_bias_one,
            column_total(grad_queries),
            column_total(grad_kv[:, features:]),
            column_total(grad_attn_out),
            grad_gain_two,
            grad_bias_two,
            column_total(grad_branch),
            grad_up_bias,
        ]
    )
    return (grad_input, (grad_qkv_w, grad_out_w, grad_up, grad_down), grad_vector)


def adam_direction(weight, gradient, first_mom, second_mom, decay_rate):
    first_new = 0.9 * first_mom + 0.1 * gradient
    second_new = 0.999 * second_mom + 0.001 * gradient * gradient
    direction = (
        first_new / (1.0 - 0.9**STEP) / (jnp.sqrt(second_new / (1.0 - 0.999**STEP)) + 1e-06)
        + decay_rate * weight
    )
    return (first_new, second_new, direction)


def matrix_sums(weight, direction):
    return (jnp.sum(weight * weight, axis=(1, 2)), jnp.sum(direction * direction, axis=(1, 2)))


def vector_update(vector, gradient, first_mom, second_mom):
    first_new, second_new, direction = adam_direction(vector, gradient, first_mom, second_mom, 0.0)
    depth_count = vector.shape[0]
    head_part = 8 * D

    def ratio_of(weight_part, step_part):
        return jnp.sqrt(jnp.sum(weight_part * weight_part, axis=-1, keepdims=True)) / jnp.sqrt(
            jnp.sum(step_part * step_part, axis=-1, keepdims=True)
        )

    lead_ratio = ratio_of(
        vector[:, :head_part].reshape(depth_count, 8, D),
        direction[:, :head_part].reshape(depth_count, 8, D),
    )
    tail_ratio = ratio_of(vector[:, head_part:], direction[:, head_part:])
    trust_ratio = jnp.concatenate(
        [
            jnp.broadcast_to(lead_ratio, (depth_count, 8, D)).reshape(depth_count, head_part),
            jnp.broadcast_to(tail_ratio, (depth_count, FF)),
        ],
        axis=1,
    )
    return (first_new, second_new, vector - 0.5 * trust_ratio * direction)


def per_device_any(
    hidden_in,
    cotangent,
    segment_ids,
    w_qkv,
    w_out,
    w_up,
    w_down,
    vectors,
    m_qkv,
    v_qkv,
    m_out,
    v_out,
    m_up,
    v_up,
    m_down,
    v_down,
    m_vectors,
    v_vectors,
):
    tokens = hidden_in.shape[0]
    depth_count = w_qkv.shape[0]
    group_ids = segment_ids[0]
    own_ids = lax.dynamic_slice_in_dim(group_ids, lax.axis_index("col") * tokens, tokens)
    allowed = own_ids[:, None] == group_ids[None, :]

    def gather_weights(layer_at):
        qkv_raw = w_qkv[layer_at].astype(jnp.bfloat16)
        out_raw = w_out[layer_at].astype(jnp.bfloat16)
        up_raw = w_up[layer_at].astype(jnp.bfloat16)
        down_raw = w_down[layer_at].astype(jnp.bfloat16)
        qkv_cols, out_cols, up_cols, down_cols = (
            lax.all_gather(qkv_raw, "col", axis=1, tiled=True),
            lax.all_gather(out_raw, "col", axis=1, tiled=True),
            lax.all_gather(up_raw, "col", axis=1, tiled=True),
            lax.all_gather(down_raw, "col", axis=0, tiled=True),
        )
        return (
            lax.all_gather(qkv_cols, "row", axis=0, tiled=True),
            lax.all_gather(out_cols, "row", axis=0, tiled=True),
            lax.all_gather(up_cols, "row", axis=0, tiled=True),
            lax.all_gather(down_cols, "row", axis=1, tiled=True),
        )

    current = hidden_in.astype(jnp.float32)
    layer_inputs = []
    kept_runs = []
    kept_weights = []
    for layer_at in range(depth_count):
        weights = gather_weights(layer_at)
        layer_inputs.append(current)
        current, kept_vals = layer_forward(current, weights, vectors[layer_at], allowed, None)
        kept_runs.append(kept_vals)
        kept_weights.append(weights)
    grad_current = cotangent
    grads_by_layer = [None] * depth_count
    vector_grads = [None] * depth_count
    for layer_at in reversed(range(depth_count)):
        weights = gather_weights(layer_at)
        unused_out, kept_vals = layer_forward(
            layer_inputs[layer_at], weights, vectors[layer_at], allowed, kept_runs[layer_at][3]
        )
        grad_current, matrix_grads, vector_grad = layer_backward(
            grad_current, layer_inputs[layer_at], kept_vals, weights, vectors[layer_at], allowed
        )
        rows_done = (
            lax.psum_scatter(
                matrix_grads[0].astype(jnp.bfloat16), "row", scatter_dimension=0, tiled=True
            ).astype(jnp.float32),
            lax.psum_scatter(
                matrix_grads[1].astype(jnp.bfloat16), "row", scatter_dimension=0, tiled=True
            ).astype(jnp.float32),
            lax.psum_scatter(
                matrix_grads[2].astype(jnp.bfloat16), "row", scatter_dimension=0, tiled=True
            ).astype(jnp.float32),
            lax.psum_scatter(
                matrix_grads[3].astype(jnp.bfloat16), "row", scatter_dimension=1, tiled=True
            ).astype(jnp.float32),
        )
        shards = (
            lax.psum_scatter(
                rows_done[0].astype(jnp.bfloat16), "col", scatter_dimension=1, tiled=True
            ).astype(jnp.float32),
            lax.psum_scatter(
                rows_done[1].astype(jnp.bfloat16), "col", scatter_dimension=1, tiled=True
            ).astype(jnp.float32),
            lax.psum_scatter(
                rows_done[2].astype(jnp.bfloat16), "col", scatter_dimension=1, tiled=True
            ).astype(jnp.float32),
            lax.psum_scatter(
                rows_done[3].astype(jnp.bfloat16), "col", scatter_dimension=0, tiled=True
            ).astype(jnp.float32),
        )
        grads_by_layer[layer_at] = shards
        vector_grads[layer_at] = vector_grad
    masters = (w_qkv, w_out, w_up, w_down)
    firsts = (m_qkv, m_out, m_up, m_down)
    seconds = (v_qkv, v_out, v_up, v_down)
    gradients = tuple(
        (
            jnp.stack([grads_by_layer[layer_at][kind] for layer_at in range(depth_count)])
            for kind in range(4)
        )
    )
    updates = [
        adam_direction(masters[kind], gradients[kind], firsts[kind], seconds[kind], 0.01)
        for kind in range(4)
    ]
    partial_sums = jnp.stack(
        [jnp.stack(matrix_sums(masters[kind], updates[kind][2]), axis=1) for kind in range(4)],
        axis=1,
    )
    grad_vectors, total_sums = lax.psum((jnp.stack(vector_grads), partial_sums), ("row", "col"))
    lamb_norms = jnp.sqrt(total_sums)
    trust_ratio = lamb_norms[:, :, 0] / lamb_norms[:, :, 1]
    new_masters = [
        masters[kind] - 0.5 * trust_ratio[:, kind, None, None] * updates[kind][2]
        for kind in range(4)
    ]
    vec_first, vec_second, new_vectors = vector_update(vectors, grad_vectors, m_vectors, v_vectors)
    return (
        current,
        grad_current,
        gradients[0],
        gradients[1],
        gradients[2],
        gradients[3],
        grad_vectors,
        updates[0][0],
        updates[0][1],
        updates[1][0],
        updates[1][1],
        updates[2][0],
        updates[2][1],
        updates[3][0],
        updates[3][1],
        vec_first,
        vec_second,
        new_masters[0],
        new_masters[1],
        new_masters[2],
        new_masters[3],
        new_vectors,
        new_masters[0].astype(jnp.bfloat16),
        new_masters[1].astype(jnp.bfloat16),
        new_masters[2].astype(jnp.bfloat16),
        new_masters[3].astype(jnp.bfloat16),
        lamb_norms,
    )


MESH = pl.DeviceIdType.MESH
F32 = jnp.float32
BF16 = jnp.bfloat16
NT = (((1,), (1,)), ((), ()))
CHUNK = 640
VM = pl.BlockSpec(memory_space=pltpu.VMEM)
ANY = pl.BlockSpec(memory_space=pl.ANY)
SCALE = HDIM ** (-0.5)
SCALE2 = SCALE * 1.4426950408889634
HEADS = 5
HW = HEADS * HDIM


def where_am_i():
    r = lax.axis_index("row")
    z = lax.axis_index("col")
    return r // 4, (r // 2) % 2, r % 2, z


def row_of(y, x, c):
    return (y * 2 + x) * 2 + c


def trade_partners(y, x, c, z):
    yf = y + (1 - c) * (1 - 2 * y)
    xf = x + c * (1 - 2 * x)
    yg = y + c * (1 - 2 * y)
    xg = x + (1 - c) * (1 - 2 * x)
    return (yf, xf), (yg, xg), (1 - y, 1 - x)


def greet(peers):
    barrier = pltpu.get_barrier_semaphore()
    for peer in peers:
        pl.semaphore_signal(barrier, inc=1, device_id=peer, device_id_type=MESH)
    pl.semaphore_wait(barrier, len(peers))


def remote(src, dst, send_sem, recv_sem, peer):
    return pltpu.make_async_remote_copy(
        src_ref=src, dst_ref=dst, send_sem=send_sem, recv_sem=recv_sem,
        device_id=peer, device_id_type=MESH,
    )


def total_kernel(x_ref, o_ref, rows, cols, rs_send, rs_recv, cs_send, cs_recv):
    y, x, c, z = where_am_i()
    r = row_of(y, x, c)
    row_peers = [(lax.rem(r + k, 8), z) for k in range(1, 8)]
    col_peers = [(r, lax.rem(z + k, 4)) for k in range(1, 4)]
    greet(row_peers + col_peers)
    rows[r] = x_ref[...]
    copies = [
        remote(x_ref, rows.at[r], rs_send.at[k], rs_recv.at[k], peer) for k, peer in enumerate(row_peers)
    ]
    for cp in copies:
        cp.start()
    for cp in copies:
        cp.wait()
    total = rows[0]
    for k in range(1, 8):
        total = total + rows[k]
    cols[z] = total
    copies = [
        remote(cols.at[z], cols.at[z], cs_send.at[k], cs_recv.at[k], peer) for k, peer in enumerate(col_peers)
    ]
    for cp in copies:
        cp.start()
    for cp in copies:
        cp.wait()
    o_ref[...] = cols[0] + cols[1] + cols[2] + cols[3]


def total_over_devices(x, cid):
    dma = pltpu.SemaphoreType.DMA
    return pl.pallas_call(
        total_kernel,
        name="total",
        out_shape=jax.ShapeDtypeStruct(x.shape, F32),
        in_specs=[VM],
        out_specs=VM,
        scratch_shapes=[
            pltpu.VMEM((8,) + x.shape, F32), pltpu.VMEM((4,) + x.shape, F32),
            dma((7,)), dma((7,)), dma((3,)), dma((3,)),
        ],
        compiler_params=pltpu.CompilerParams(collective_id=cid, has_side_effects=True),
    )(x)


def attention_peers(y, x, c, z):
    return c * 2 + z % 2, lambda b: (row_of(y, x, b // 2), (z // 2) * 2 + b % 2)


def norm_parts(values):
    average = jnp.mean(values, axis=-1, keepdims=True)
    centered = values - average
    variance = jnp.mean(centered * centered, axis=-1, keepdims=True)
    spread = lax.rsqrt(variance + 1e-05)
    return centered * spread, spread


def dot(a, b):
    return jnp.dot(a, b, preferred_element_type=F32)


def dot_nt(a, b):
    return lax.dot_general(a, b, NT, preferred_element_type=F32)


def piece(vec_ref, at, count=640):
    return vec_ref[0:1, at : at + count]


def exchange(me, peer_of, sbuf, rbuf, ss, rs):
    y, x, c, z = where_am_i()
    out = []
    for k in (1, 2, 3):
        b = lax.rem(me + k, 4)
        out.append(remote(sbuf.at[b], rbuf.at[me], ss.at[k], rs.at[k], peer_of(b)))
    for cp in out:
        cp.start()
    return out


def head_mask(h, rows):
    lane = lax.broadcasted_iota(jnp.int32, (rows, HW), 1)
    return (lane >= h * HDIM) & (lane < (h + 1) * HDIM)


def fold(values, n):
    rows = 320 // n
    return jnp.concatenate([values[rows * j : rows * (j + 1)] for j in range(n)], axis=1)


GROUPS = ((0, 2, 2), (2, 3, 4))


def group_shapes():
    return [(4, 320 // n, n * 3 * heads * HDIM) for _, heads, n in GROUPS]


def pack_group(group, parts):
    first, heads, n = GROUPS[group]
    cut = slice(first * HDIM, (first + heads) * HDIM)
    return fold(jnp.concatenate([part[:, cut] for part in parts], axis=1), n).astype(BF16)


def unpack_group(group, block, kind):
    _, heads, n = GROUPS[group]
    w = heads * HDIM
    return jnp.concatenate(
        [block[:, (3 * j + kind) * w : (3 * j + kind + 1) * w].astype(F32) for j in range(n)], axis=0
    )


QB = 256
LAYERS = 2
NCH = LAYERS * 5
PIECES = ((0, 0, 256), (0, 256, 256), (0, 512, 768)) + tuple(
    (layer, col, CHUNK) for layer in range(LAYERS) for col in range(0, 3200, CHUNK) if layer or col >= 1280
)


class Steps:
    def run(self, plan):
        for at in range(0, len(plan), 2):
            self.step(plan[at], int(plan[at + 1], 16))

    def run_at(self, plans, index):
        for at, plan in enumerate(plans):
            if plan:
                @pl.when(index == at)
                def _():
                    self.run(plan)


class Gather(Steps):
    def __init__(self, s_ref, w_ref, wbuf, zs, zr, ps, pr, own_sem, load_sem):
        y, x, c, z = where_am_i()
        self.s_ref, self.w_ref, self.wbuf = s_ref, w_ref, wbuf
        self.sems = zs, zr, ps, pr, own_sem, load_sem
        (yf, xf), (yg, xg), (yd, xd) = trade_partners(y, x, c, z)
        self.z, self.r = z, row_of(y, x, c)
        self.c, self.q, self.qf = c, y * 2 + x, yf * 2 + xf
        self.zpeers = [(self.r, lax.rem(z + k, 4)) for k in (1, 2, 3)]
        self.pf, self.pg, self.sib = (row_of(yf, xf, c), z), (row_of(yg, xg, c), z), (row_of(y, x, 1 - c), z)

    def cols(self, t):
        layer, col, width = PIECES[t]
        return layer, pl.ds(col, width)

    def zcopy(self, t, k):
        layer, cs = self.cols(t)
        zs, zr = self.sems[:2]
        return remote(
            self.s_ref.at[layer, :, cs], self.w_ref.at[layer, self.z, self.q, self.c, :, cs],
            zs.at[t, k], zr.at[t, k], self.zpeers[k],
        )

    def own(self, t):
        layer, cs = self.cols(t)
        return pltpu.make_async_copy(
            self.s_ref.at[layer, :, cs], self.w_ref.at[layer, self.z, self.q, self.c, :, cs], self.sems[4].at[t]
        )

    def hop(self, t, which):
        layer, cs = self.cols(t)
        chip, peer = (
            (self.q, self.pf), (self.q, self.pg), (self.qf, self.pg), (slice(None), self.sib)
        )[which]
        block = self.w_ref.at[layer, :, chip, self.c, :, cs]
        return remote(block, block, self.sems[2].at[t, which], self.sems[3].at[t, which], peer)

    def load(self, t):
        layer, cs = self.cols(t)
        return pltpu.make_async_copy(self.w_ref.at[layer, :, :, :, :, cs], self.wbuf.at[:, :, :, :, cs], self.sems[5].at[t])

    def step(self, name, t):
        if name == "Z":
            for k in range(3):
                self.zcopy(t, k).start()
            self.own(t).start()
        elif name == "z":
            for k in range(3):
                self.zcopy(t, k).wait()
            self.own(t).wait()
            for which in (0, 1):
                self.hop(t, which).start()
        elif name == "f":
            self.hop(t, 0).wait()
            self.hop(t, 2).start()
        elif name == "g":
            self.hop(t, 1).wait()
            self.hop(t, 2).wait()
            self.hop(t, 3).start()
        elif name == "s":
            self.hop(t, 3).wait()
        elif name == "L":
            self.load(t).start()
        elif name == "l":
            self.load(t).wait()


PLAN = {
    "start": "Z0",
    "first": "z0Z1f0z1Z2g0f1Z3g1s0L0s1L1z2Z4l0l1",
    "sent0": "z3Z5f2z4Z6",
    "heads0": ["f3z5Z7", "g2s2L2", "f4z6Z8", "g3s3L3", "f5"],
    "osent0": "l2g4z7Z9",
    "up0": ["s4L4", "", "f6z8Za", "g5", "l3", "", "s5L5", "z9f7"],
    "down0": ["l4", "l5"],
    "qkv1": "g6s6L6l6",
    "sent1": "f8g7za",
    "heads1": ["f9g8s7L7", "", "s8L8", "fag9", "s9L9"],
    "osent1": "ga",
    "up1": ["l7sa", "", "", "", "l8La", "", "", ""],
    "down1": ["l9", "la"],
}


def swap_partner(y, x, c, z):
    return row_of(y, x, 1 - c), lax.rem(z + 2, 4)


def move_tokens(src, dst, send, recv, then):
    y, x, c, z = where_am_i()
    goes = c != z // 2
    copy = remote(src, dst, send, recv, swap_partner(y, x, c, z))
    stay = pltpu.make_async_copy(src, dst, send)

    @pl.when(goes)
    def _():
        copy.wait() if then else copy.start()

    @pl.when(jnp.logical_not(goes))
    def _():
        stay.wait() if then else stay.start()


SAVED = ("x", "xm", "o", "hdn", "gp", "q", "k", "v", "oh", "lse")


def forward_kernel(hid_ref, cot_ref, seg_ref, vec_ref, s_ref,
                   w_ref, xo_ref, dx_ref, segr_ref, segc_ref,
                   x_out, xm_out, o_out, hdn_out, gp_out, q_out, k_out, v_out, oh_out, lse_out,
                   wbuf, hid, xcur, xm_s, o_s, hdn_s, gp_s, q_s, k_s, v_s, oh_s, lse_s,
                   abuf, ubuf, pbuf, segbuf, sbuf0, sbuf1, rbuf0, rbuf1, osbuf, orbuf, vt, ot,
                   zs, zr, ps, pr, own_sem, load_sem, ss, rs, oss, ors, save_sem, mv_s, mv_r):
    y, x, c, z = where_am_i()
    me, peer_of = attention_peers(y, x, c, z)
    sbufs, rbufs = (sbuf0, sbuf1), (rbuf0, rbuf1)
    net = Gather(s_ref, w_ref, wbuf, zs, zr, ps, pr, own_sem, load_sem)
    zx = z + 1 - 2 * lax.rem(z, 2)
    greet(net.zpeers + [net.pf, net.pg, net.sib, (row_of(y, x, 1 - c), zx), swap_partner(y, x, c, z)])
    move_tokens(hid_ref, hid, mv_s.at[0], mv_r.at[0], 0)
    seg_copy = remote(seg_ref, segbuf.at[1], mv_s.at[1], mv_r.at[1], net.sib)
    seg_copy.start()
    net.run(PLAN["start"])
    move_tokens(hid_ref, hid, mv_s.at[0], mv_r.at[0], 1)
    seg_copy.wait()
    segbuf[0] = seg_ref[...]
    segr_ref[...] = jnp.where(c == z // 2, segbuf[0], segbuf[1])
    segc_ref[...] = jnp.broadcast_to(segr_ref[...].astype(F32), (8, 1280)).T[:, 0:1].astype(jnp.int32)
    xcur[...] = hid[...].astype(F32)

    kept = dict(zip(SAVED, (
        (xcur, x_out), (xm_s, xm_out), (o_s, o_out), (hdn_s, hdn_out), (gp_s, gp_out),
        (q_s, q_out), (k_s, k_out), (v_s, v_out), (oh_s, oh_out), (lse_s, lse_out))))

    def save(name, layer):
        src, dst = kept[name]
        return pltpu.make_async_copy(src, dst.at[layer], save_sem.at[layer, SAVED.index(name)])

    def held(i, col, width):
        return wbuf[i, :, :, :, col : col + width].reshape(640, width)

    def before(name, layer):
        if layer:
            save(name, layer - 1).wait()

    for layer in range(LAYERS):
        vl = vec_ref.at[pl.ds(layer, 1), :]
        save("x", layer).start()
        n1, _ = norm_parts(xcur[...])
        a = (n1 * piece(vl, 0) + piece(vl, 640)).astype(BF16)
        net.run(PLAN["qkv1" if layer else "first"])
        abuf[...] = a

        for i in range(4):
            pbuf[i] = dot(abuf[...], held(i, 0, 512))

        blocks = [pbuf[b // 3, :, (b % 3) * HW : (b % 3 + 1) * HW] for b in range(12)]
        for b in range(4):
            q = blocks[b] + vl[0:1, 1280 + HW * b : 1280 + HW * (b + 1)]
            v = blocks[8 + b] + vl[0:1, 1920 + HW * b : 1920 + HW * (b + 1)]
            for g in range(2):
                sbufs[g][b] = pack_group(g, (q, blocks[4 + b], v))
        copies = exchange(me, peer_of, sbufs[0], rbufs[0], ss.at[layer, 0], rs.at[layer, 0])
        for name in ("q", "k", "v", "oh", "lse"):
            before(name, layer)
        if layer == 0:
            k_s[...] = jnp.zeros_like(k_s)
        net.run(PLAN["sent%d" % layer])
        lse_s[...] = jnp.zeros_like(lse_s)

        for g, (first, heads, _) in enumerate(GROUPS):
            rbufs[g][me] = sbufs[g][me]
            for cp in copies:
                cp.wait()
            if g == 0:
                copies = exchange(me, peer_of, sbufs[1], rbufs[1], ss.at[layer, 1], rs.at[layer, 1])
            cut = slice(first * HDIM, (first + heads) * HDIM)
            for b in range(4):
                rows = slice(320 * b, 320 * (b + 1))
                for kind, ref in enumerate((q_s, k_s, v_s)):
                    ref[rows, cut] = unpack_group(g, rbufs[g][b], kind).astype(BF16)
            wide = 128 if g == 0 else HW
            vt[cut, :] = v_s[:, 0:wide].astype(F32).T[cut, :].astype(BF16)
            if g == 1:
                for name in ("q", "k", "v"):
                    save(name, layer).start()

            @pl.loop(first, first + heads)
            def _(h):
                net.run_at(PLAN["heads%d" % layer][first : first + heads], h - first)

                @pl.loop(0, 5, unroll=5)
                def _(step):
                    at = pl.multiple_of(step * QB, QB)
                    qm = jnp.where(head_mask(h, QB), q_s[pl.ds(at, QB), :], jnp.zeros((), BF16))
                    s = dot_nt(k_s[...], qm)
                    s = jnp.where(segc_ref[...] == segr_ref[0:1, pl.ds(at, QB)], s, negative)
                    top = jnp.max(s, axis=0, keepdims=True)
                    p = jnp.exp2(s * SCALE2 - top * SCALE2)
                    total = jnp.sum(p, axis=0, keepdims=True)
                    rows = pl.ds(pl.multiple_of(h * HDIM, HDIM), HDIM)
                    ot[rows, pl.ds(at, QB)] = dot(vt[rows, :], p.astype(BF16)) / total
                    lse_s[pl.ds(h, 1), pl.ds(at, QB)] = top * SCALE2 + jnp.log2(total)

        save("lse", layer).start()
        oh_s[...] = ot[...].T.astype(BF16)
        save("oh", layer).start()
        for b in range(4):
            osbuf[b] = fold(oh_s[320 * b : 320 * (b + 1), :].astype(F32), 4).astype(BF16)
        copies = exchange(me, peer_of, osbuf, orbuf, oss.at[layer], ors.at[layer])
        orbuf[me] = osbuf[me]
        for name in ("o", "xm", "hdn", "gp"):
            before(name, layer)
        net.run(PLAN["osent%d" % layer])
        for cp in copies:
            cp.wait()
        for j in range(4):
            o_s[80 * j : 80 * (j + 1), :] = jnp.concatenate(
                [orbuf[b, :, HW * j : HW * (j + 1)].astype(F32) for b in range(4)], axis=1
            ).astype(BF16)
        save("o", layer).start()

        for i in range(4):
            pbuf[i, :, 0:256] = dot(o_s[...], held(i, 384, 256))

        yv = jnp.concatenate([pbuf[i, :, 96:256] for i in range(4)], axis=1)
        xm = xcur[...] + (yv + piece(vl, 2560))
        xm_s[...] = xm
        save("xm", layer).start()
        n2, _ = norm_parts(xm)
        abuf[...] = (n2 * piece(vl, 3200) + piece(vl, 3840)).astype(BF16)
        if layer == 0:
            move_tokens(cot_ref, dx_ref, mv_s.at[2], mv_r.at[2], 0)

        for half in range(2):
            @pl.loop(0, 4)
            def _(i):
                net.run_at(PLAN["up%d" % layer][4 * half : 4 * half + 4], i)

                to = pl.multiple_of(i * 1280 + half * 640, 640)
                ubuf[...] = dot(abuf[...], held(i, 640 * (half + 1), 640)) + vl[0:1, pl.ds(5120 + to, 640)]

                @pl.loop(0, 10)
                def _(j):
                    rows = pl.ds(pl.multiple_of(j * 32, 32), 32)
                    u = ubuf[rows, :]
                    cdf = 0.5 * (1.0 + lax.erf(u * (0.5**0.5)))
                    hdn_s[rows, pl.ds(to, 640)] = (u * cdf).astype(BF16)
                    gp_s[rows, pl.ds(to, 640)] = (
                        cdf + u * (jnp.exp(-0.5 * u * u) * 0.3989422804014327)
                    ).astype(BF16)

        save("hdn", layer).start()
        save("gp", layer).start()
        save("x", layer).wait()
        xcur[...] = xm_s[...] + piece(vl, 4480)
        for half in range(2):
            net.run(PLAN["down%d" % layer][half])

            @pl.loop(0, 4)
            def _(i):
                to = pl.multiple_of(i * 1280 + half * 640, 640)
                xcur[...] += dot_nt(hdn_s[:, pl.ds(to, 640)], held(i, 640 * (half + 3), 640))


    xo_ref[...] = xcur[...]
    for name in SAVED[1:]:
        save(name, LAYERS - 1).wait()
    move_tokens(cot_ref, dx_ref, mv_s.at[2], mv_r.at[2], 1)


def forward_all(hidden, cotangent, segments, vectors, shards):
    dma = pltpu.SemaphoreType.DMA
    sds = jax.ShapeDtypeStruct
    vmem = pltpu.VMEM
    return pl.pallas_call(
        forward_kernel,
        name="forward",
        out_shape=(
            sds((LAYERS, 4, 4, 2, 80, 3200), BF16), sds((320, 640), F32), sds((320, 640), F32),
            sds((1, 1280), jnp.int32), sds((1280, 1), jnp.int32),
            sds((LAYERS, 320, 640), F32), sds((LAYERS, 320, 640), F32), sds((LAYERS, 320, 640), BF16),
            sds((LAYERS, 320, 5120), BF16), sds((LAYERS, 320, 5120), BF16),
            sds((LAYERS, 1280, HW), BF16), sds((LAYERS, 1280, HW), BF16), sds((LAYERS, 1280, HW), BF16),
            sds((LAYERS, 1280, HW), BF16), sds((LAYERS, 8, 1280), F32),
        ),
        in_specs=[ANY, ANY, VM, VM, ANY],
        out_specs=(ANY, VM, ANY, VM, VM) + (ANY,) * 10,
        scratch_shapes=[
            vmem((4, 4, 2, 80, 3200), BF16), vmem((320, 640), BF16), vmem((320, 640), F32),
            vmem((320, 640), F32), vmem((320, 640), BF16), vmem((320, 5120), BF16), vmem((320, 5120), BF16),
            vmem((1280, HW), BF16), vmem((1280, HW), BF16), vmem((1280, HW), BF16), vmem((1280, HW), BF16),
            vmem((8, 1280), F32),
            vmem((320, 640), BF16), vmem((320, 640), F32), vmem((4, 320, 512), F32), vmem((2, 1, 1280), jnp.int32),
            *[vmem(shape, BF16) for shape in group_shapes() * 2],
            vmem((4, 80, 640), BF16), vmem((4, 80, 640), BF16),
            vmem((HW, 1280), BF16), vmem((HW, 1280), F32),
            *[dma((len(PIECES),) + shape) for shape in ((3,), (3,), (4,), (4,), (), ())],
            dma((LAYERS, 2, 4)), dma((LAYERS, 2, 4)), dma((LAYERS, 4)), dma((LAYERS, 4)),
            dma((LAYERS, len(SAVED))), dma((3,)), dma((3,)),
        ],
        compiler_params=pltpu.CompilerParams(
            collective_id=0, has_side_effects=True, vmem_limit_bytes=56 << 20
        ),
    )(hidden, cotangent, segments, vectors, shards)


def norm_back(dy, n, spread, gain):
    dn = dy * gain
    mean1 = jnp.mean(dn, axis=-1, keepdims=True)
    mean2 = jnp.mean(dn * n, axis=-1, keepdims=True)
    return spread * (dn - mean1 - n * mean2)


def col_sum(values):
    return jnp.sum(values, axis=0, keepdims=True)


ORDER = (3, 1, 4, 2, 0)
OWN, LAND = 4, 2
HELD = {(1, 3): 0, (1, 1): 1, (1, 4): 2, (1, 2): 3, (1, 0): 0, (0, 3): 1, (0, 1): 2, (0, 4): 3, (0, 2): 0, (0, 0): 1}


class Scatter(Steps):
    def __init__(self, g_ref, out_ref, own, sibr, p2r, p1r, zr, fin, fsem, sems):
        y, x, c, z = where_am_i()
        (yf, xf), (yg, xg), (yd, xd) = trade_partners(y, x, c, z)
        self.c, self.z = c, z
        self.q, self.qf, self.qg, self.qd = y * 2 + x, yf * 2 + xf, yg * 2 + xg, yd * 2 + xd
        r = row_of(y, x, c)
        self.zpeers = [(r, lax.rem(z + k, 4)) for k in (1, 2, 3)]
        self.pf, self.pg = (self.qf * 2 + c, z), (self.qg * 2 + c, z)
        self.sib = (row_of(y, x, 1 - c), z)
        self.g_ref, self.out_ref = g_ref, out_ref
        self.own, self.sibr, self.p2r, self.p1r, self.zr = own, sibr, p2r, p1r, zr
        self.fin, self.fsem, self.sems = fin, fsem, sems

    def where(self, t):
        return LAYERS - 1 - t // 5, ORDER[t % 5] * CHUNK

    def part(self, t, core):
        layer, col = self.where(t)
        return self.g_ref.at[layer, :, :, core, :, pl.ds(col, CHUNK)]

    def own_copy(self, t):
        return pltpu.make_async_copy(self.part(t, self.c), self.own.at[t % OWN], self.sems[0].at[t % OWN])

    def sib_copy(self, t):
        k = t % LAND
        return remote(
            self.part(t, 1 - self.c), self.sibr.at[k], self.sems[1].at[k], self.sems[2].at[k], self.sib
        )

    def p2_copy(self, t, j):
        k = t % LAND
        return remote(
            self.own.at[t % OWN, :, (self.qg, self.qd)[j]], self.p2r.at[k, j],
            self.sems[3].at[k, j], self.sems[4].at[k, j], self.pg,
        )

    def p1_copy(self, t):
        k = t % LAND
        return remote(
            self.own.at[t % OWN, :, self.qf], self.p1r.at[k], self.sems[5].at[k], self.sems[6].at[k], self.pf
        )

    def z_copy(self, t, j):
        k = t % LAND
        return remote(
            self.own.at[t % OWN, lax.rem(self.z + j + 1, 4), self.q], self.zr.at[k, j],
            self.sems[7].at[k, j], self.sems[8].at[k, j], self.zpeers[j],
        )

    def put_out(self, t):
        layer, col = self.where(t)
        k = t % LAND
        return pltpu.make_async_copy(self.fin.at[k], self.out_ref.at[layer, :, pl.ds(col, CHUNK)], self.fsem.at[k])

    def add(self, dst, src):
        @pl.loop(0, 4)
        def _(i):
            dst[i] = dst[i] + src[i]

    def step(self, name, t):
        own = self.own.at[t % OWN]
        k = t % LAND
        if name == "a":
            self.sib_copy(t).start()
            self.own_copy(t).start()
        elif name == "b":
            self.sib_copy(t).wait()
            self.own_copy(t).wait()
            self.add(own, self.sibr.at[k])

            for j in range(2):
                self.p2_copy(t, j).start()
        elif name == "c":
            for j in range(2):
                self.p2_copy(t, j).wait()
            self.add(own.at[:, self.q], self.p2r.at[k, 0])
            self.add(own.at[:, self.qf], self.p2r.at[k, 1])
            self.p1_copy(t).start()
        elif name == "d":
            self.p1_copy(t).wait()
            self.add(own.at[:, self.q], self.p1r.at[k])
            for j in range(3):
                self.z_copy(t, j).start()
        elif name == "e":
            for j in range(3):
                self.z_copy(t, j).wait()
            total = own[self.z, self.q].astype(F32)
            for j in range(3):
                total = total + self.zr[k, j].astype(F32)
            if t >= LAND:
                self.put_out(t - LAND).wait()
            self.fin[k] = total
            self.put_out(t).start()


BACK = {
    "f1": ["", "", "", "", "a0", "", "b0", "a1"],
    "ffn1": "",
    "wo1": "c0b1a2",
    "heads1": ["", "", "d0", "c1b2", ""],
    "psent1": "a3e0d1c2b3",
    "end1": "a4",
    "f0": ["e1d2c3", "b4", "", "", "e2d3a5", "c4", "", "b5e3d4"],
    "ffn0": "",
    "wo0": "a6c5e4b6a7",
    "heads0": ["", "d5", "c6b7", "", "e5d6a8c7"],
    "psent0": "b8e6",
    "end0": ["a9", "d7c8", "b9e7", "d8", "c9e8", "d9e9"],
}


def backward_kernel(dx_ref, last_ref, xs_ref, xms_ref, os_ref, hdns_ref, gps_ref, qs_ref, ks_ref, vs_ref, ohs_ref, lses_ref,
                    vec_ref, segr_ref, segc_ref, w_ref,
                    hout_ref, gin_ref, gv_ref, gout_ref, g_ref,
                    wbuf, x_s, xm_s, o_s, hdn_s, gp_s, q_s, k_s, v_s, oh_s, lse_s,
                    gbuf, at_s, dy, dyt, da2, dosend, dorecv, dos, kt, dqt, dk, dv, delta, psend0, psend1, precv0, precv1, dp4,
                    own, sibr, p2r, p1r, zr, fin, dxo_ref, vgot, dpad,
                    wsem, lsem, gsem, ss, rs, oss, ors, fsem, mv_s, mv_r, vs_sem, vr_sem, *net_sems):
    y, x, c, z = where_am_i()
    me, peer_of = attention_peers(y, x, c, z)
    psends, precvs = (psend0, psend1), (precv0, precv1)
    net = Scatter(g_ref, gout_ref, own, sibr, p2r, p1r, zr, fin, fsem, net_sems)

    def load_w(layer, i):
        return pltpu.make_async_copy(w_ref.at[layer, :, :, pl.ds(i * CHUNK, CHUNK)], wbuf.at[HELD[layer, i]], wsem.at[i])

    saved = {
        "x": (xs_ref, x_s), "xm": (xms_ref, xm_s), "o": (os_ref, o_s), "hdn": (hdns_ref, hdn_s), "gp": (gps_ref, gp_s),
        "q": (qs_ref, q_s), "k": (ks_ref, k_s), "v": (vs_ref, v_s), "oh": (ohs_ref, oh_s), "lse": (lses_ref, lse_s),
    }

    def load(name, layer):
        src, dst = saved[name]
        return pltpu.make_async_copy(src.at[layer], dst, lsem.at[SAVED.index(name)])

    def fetch(layer, names):
        for name in names:
            if isinstance(name, int):
                load_w(layer, name).start()
            else:
                load(name, layer).start()

    def arrive(layer, *names):
        for name in names:
            if isinstance(name, int):
                load_w(layer, name).wait()
            else:
                load(name, layer).wait()

    fetch(1, ["xm", "hdn", "gp", 3, 1, 4, 2, "k", "q", "v", "oh", "lse", "o", "x"])
    zx = z + 1 - 2 * lax.rem(z, 2)
    greet(net.zpeers + [net.pf, net.pg, net.sib, (row_of(y, x, 1 - c), zx), swap_partner(y, x, c, z)])
    move_tokens(last_ref, hout_ref, mv_s.at[0], mv_r.at[0], 0)
    dxo_ref[...] = dx_ref[...]

    ends = [net.sib, (row_of(y, 1 - x, c), z), (row_of(1 - y, x, c), z), (row_of(y, x, c), zx),
            (row_of(y, x, c), lax.rem(z + 2, 4))]

    def vector_hop(k):
        return remote(gv_ref, vgot.at[k], vs_sem.at[k], vr_sem.at[k], ends[k])

    for layer in reversed(range(LAYERS)):
        vl = vec_ref.at[pl.ds(layer, 1), :]
        gl = gv_ref.at[pl.ds(layer, 1), :]
        dy[...] = dxo_ref[...].astype(BF16)
        dyf = dy[...].astype(F32)
        dyt[...] = dyf.T.astype(BF16)
        gl[0:1, 4480:5120] = col_sum(dyf)
        arrive(layer, "xm")
        n2, spread2 = norm_parts(xm_s[...])
        g2 = piece(vl, 3200)
        at_s[...] = (n2 * g2 + piece(vl, 3840)).T.astype(BF16)
        da2[...] = jnp.zeros_like(da2)
        arrive(layer, "hdn", "gp")

        def put(slot, i, col):
            return pltpu.make_async_copy(gbuf.at[slot], g_ref.at[layer, i, :, :, :, pl.ds(col, CHUNK)], gsem.at[slot])

        for half in range(2):
            arrive(layer, 3 + half, 1 + half)

            @pl.loop(0, 4, unroll=4)
            def _(i):
                net.run_at(BACK["f%d" % layer][4 * half : 4 * half + 4], i)
                to = pl.multiple_of(i * 1280 + half * CHUNK, CHUNK)

                gdown = dot(dyt[...], hdn_s[:, pl.ds(to, CHUNK)]).astype(BF16)

                @pl.when(i > 0)
                def _():
                    put(0, 0, 0).wait()

                gbuf[0] = gdown.reshape(4, 2, 80, CHUNK)
                put(0, i, 1920 + half * CHUNK).start()
                dh = dot(dy[...], wbuf[HELD[layer, 3 + half], i])
                du = (dh * gp_s[:, pl.ds(to, CHUNK)].astype(F32)).astype(BF16)
                gl[0:1, pl.ds(5120 + to, CHUNK)] = col_sum(du.astype(F32))
                gup = dot(at_s[...], du).astype(BF16)

                @pl.when(i > 0)
                def _():
                    put(1, 0, 0).wait()

                gbuf[1] = gup.reshape(4, 2, 80, CHUNK)
                put(1, i, 640 + half * CHUNK).start()
                da2[...] += dot_nt(du, wbuf[HELD[layer, 1 + half], i])

            put(0, 0, 0).wait()
            put(1, 0, 0).wait()
            if half == 0:
                fetch(layer, [0])
            elif layer:
                fetch(layer - 1, [3, 1, 4])
            if half:
                net.run(BACK["ffn%d" % layer])

        da2v = da2[...]
        gl[0:1, 3200:3840] = col_sum(da2v * n2)
        gl[0:1, 3840:4480] = col_sum(da2v)
        dxm = dxo_ref[...] + norm_back(da2v, n2, spread2, g2)
        dxo_ref[...] = dxm
        if layer:
            fetch(layer - 1, ["hdn", "gp", "xm"])
        dy1f = dxm.astype(BF16).astype(F32)
        dy[...] = dxm.astype(BF16)
        gl[0:1, 2560:3200] = col_sum(dy1f)
        arrive(layer, 0)
        wa = wbuf.at[HELD[layer, 0]]
        zpad = jnp.zeros((320, 96), F32)
        for i in range(4):
            dpad[i] = jnp.concatenate([zpad, dy1f[:, HW * i : HW * (i + 1)]], axis=1).astype(BF16)
        da2[...] = jnp.zeros_like(da2)

        for i in range(4):
            da2[...] += dot_nt(dpad[i], wa[i, :, 384:640])

        for b in range(4):
            dosend[b] = fold(da2[:, HW * b : HW * (b + 1)], 4).astype(BF16)
        copies = exchange(me, peer_of, dosend, dorecv, oss.at[layer], ors.at[layer])
        dorecv[me] = dosend[me]
        arrive(layer, "k", "q", "v", "oh", "lse")
        kt[...] = k_s[...].astype(F32).T.astype(BF16)
        dk[...] = jnp.zeros_like(dk)
        dv[...] = jnp.zeros_like(dv)
        net.run(BACK["wo%d" % layer])
        for cp in copies:
            cp.wait()
        for b in range(4):
            for j in range(4):
                dos[320 * b + 80 * j : 320 * b + 80 * (j + 1), :] = (
                    dorecv[b, :, HW * j : HW * (j + 1)].astype(F32).astype(BF16)
                )
        lane = lax.broadcasted_iota(jnp.int32, (8, HW), 1)
        head = lax.broadcasted_iota(jnp.int32, (8, HW), 0)
        pick = jnp.where((lane >= head * HDIM) & (lane < (head + 1) * HDIM), 1.0, 0.0).astype(F32)
        delta[...] = lax.dot_general(
            pick, dos[...].astype(F32) * oh_s[...].astype(F32), NT,
            precision=lax.Precision.HIGHEST, preferred_element_type=F32,
        )

        groups = {}
        for g in (1, 0):
            first, heads, _ = GROUPS[g]
            plans = BACK["heads%d" % layer][0:3] if g else BACK["heads%d" % layer][3:5]

            @pl.loop(first, first + heads)
            def _(h):
                net.run_at(plans, h - first)

                @pl.loop(0, 5, unroll=5)
                def _(step):
                    at = pl.multiple_of(step * QB, QB)
                    zero = jnp.zeros((), BF16)
                    mask = head_mask(h, QB)
                    qm = jnp.where(mask, q_s[pl.ds(at, QB), :], zero)
                    dm = jnp.where(mask, dos[pl.ds(at, QB), :], zero)
                    s = dot_nt(k_s[...], qm)
                    s = jnp.where(segc_ref[...] == segr_ref[0:1, pl.ds(at, QB)], s, negative)
                    p = jnp.exp2(s * SCALE2 - lse_s[pl.ds(h, 1), pl.ds(at, QB)])
                    dp = dot_nt(v_s[...], dm)
                    ds = (p * (dp - delta[pl.ds(h, 1), pl.ds(at, QB)])).astype(BF16)
                    dv[...] += dot(p.astype(BF16), dm)
                    dk[...] += dot(ds, qm)
                    rows = pl.ds(pl.multiple_of(h * HDIM, HDIM), HDIM)
                    dqt[rows, pl.ds(at, QB)] = dot(kt[rows, :], ds)

            if layer and g == 0:
                fetch(layer - 1, ["k", "q", "v", "oh", "lse"])
            dq = dqt[...].T * SCALE
            for b in range(4):
                rows = slice(320 * b, 320 * (b + 1))
                psends[g][b] = pack_group(g, (dq[rows], dk[rows, :] * SCALE, dv[rows, :]))
            groups[g] = exchange(me, peer_of, psends[g], precvs[g], ss.at[layer, g], rs.at[layer, g])
            precvs[g][me] = psends[g][me]
        copies = groups[1] + groups[0]
        zpad = jnp.zeros((320, 32), F32)
        arrive(layer, "x", "o")
        n1, spread1 = norm_parts(x_s[...])
        g1 = piece(vl, 0)
        at_s[...] = (n1 * g1 + piece(vl, 640)).T.astype(BF16)
        dyt[...] = o_s[...].astype(F32).T.astype(BF16)
        if layer:
            fetch(layer - 1, ["x", "o"])
        net.run(BACK["psent%d" % layer])
        for cp in copies:
            cp.wait()
        blocks = []
        for kind in range(3):
            own_kind = [
                jnp.concatenate([unpack_group(g, precvs[g][b], kind) for g in range(2)], axis=1) for b in range(4)
            ]
            if kind != 1:
                at = 1280 if kind == 0 else 1920
                gl[0:1, at : at + 640] = jnp.concatenate([col_sum(part) for part in own_kind], axis=1)
            blocks += own_kind
        for i in range(4):
            dp4[i] = jnp.concatenate(blocks[3 * i : 3 * i + 3] + [zpad], axis=1).astype(BF16)
        da2[...] = jnp.zeros_like(da2)

        for i in range(4):
            slot = i % 2
            part = dot(at_s[...], dp4[i])
            rest = dot(dyt[...], dpad[i])
            if i > 1:
                put(slot, 0, 0).wait()

            gbuf[slot, :, :, :, 0:384] = part[:, 0:384].astype(BF16).reshape(4, 2, 80, 384)
            gbuf[slot, :, :, :, 384:512] = (part[:, 384:512] + rest[:, 0:128]).astype(BF16).reshape(4, 2, 80, 128)
            gbuf[slot, :, :, :, 512:640] = rest[:, 128:256].astype(BF16).reshape(4, 2, 80, 128)
            put(slot, i, 0).start()
            da2[...] += dot_nt(dp4[i], wa[i, :, 0:512])

        da = da2[...]
        if layer:
            fetch(layer - 1, [2])
        gl[0:1, 0:640] = col_sum(da * n1)
        gl[0:1, 640:1280] = col_sum(da)
        dxo_ref[...] = dxo_ref[...] + norm_back(da, n1, spread1, g1)
        put(0, 0, 0).wait()
        put(1, 0, 0).wait()
        if layer:
            net.run(BACK["end%d" % layer])
    move_tokens(dxo_ref, gin_ref, mv_s.at[1], mv_r.at[1], 0)
    for k, plan in enumerate(BACK["end0"]):
        if k:
            vector_hop(k - 1).wait()
            gv_ref[...] += vgot[k - 1]
        if k < 5:
            vector_hop(k).start()
        net.run(plan)
    for t in range(NCH - LAND, NCH):
        net.put_out(t).wait()
    move_tokens(last_ref, hout_ref, mv_s.at[0], mv_r.at[0], 1)
    move_tokens(dxo_ref, gin_ref, mv_s.at[1], mv_r.at[1], 1)


def backward_all(dx, last, kept, vec, segr, segc, weights):
    dma = pltpu.SemaphoreType.DMA
    sds = jax.ShapeDtypeStruct
    vmem = pltpu.VMEM
    return pl.pallas_call(
        backward_kernel,
        name="backward",
        out_shape=(
            sds((320, 640), F32), sds((320, 640), F32), sds((LAYERS, 10240), F32), sds((LAYERS, 80, 3200), F32),
            sds((LAYERS, 4, 4, 2, 80, 3200), BF16),
        ),
        in_specs=[VM] + [ANY] * 11 + [VM, VM, VM, ANY],
        out_specs=(ANY, ANY, VM, ANY, ANY),
        scratch_shapes=[
            vmem((4, 4, 640, CHUNK), BF16),
            vmem((320, 640), F32), vmem((320, 640), F32), vmem((320, 640), BF16),
            vmem((320, 5120), BF16), vmem((320, 5120), BF16),
            vmem((1280, HW), BF16), vmem((1280, HW), BF16), vmem((1280, HW), BF16), vmem((1280, HW), BF16),
            vmem((8, 1280), F32),
            vmem((2, 4, 2, 80, CHUNK), BF16), vmem((640, 320), BF16),
            vmem((320, 640), BF16), vmem((640, 320), BF16), vmem((320, 640), F32),
            vmem((4, 80, 640), BF16), vmem((4, 80, 640), BF16), vmem((1280, HW), BF16),
            vmem((HW, 1280), BF16), vmem((HW, 1280), F32),
            vmem((1280, HW), F32), vmem((1280, HW), F32), vmem((8, 1280), F32),
            *[vmem(shape, BF16) for shape in group_shapes() * 2], vmem((4, 320, 512), BF16),
            vmem((OWN, 4, 4, 80, CHUNK), BF16), vmem((LAND, 4, 4, 80, CHUNK), BF16),
            vmem((LAND, 2, 4, 80, CHUNK), BF16), vmem((LAND, 4, 80, CHUNK), BF16), vmem((LAND, 3, 80, CHUNK), BF16),
            vmem((LAND, 80, CHUNK), F32), vmem((320, 640), F32), vmem((5, LAYERS, 10240), F32),
            vmem((4, 320, 256), BF16),
            dma((5,)), dma((len(SAVED),)), dma((2,)),
            dma((LAYERS, 2, 4)), dma((LAYERS, 2, 4)), dma((LAYERS, 4)), dma((LAYERS, 4)), dma((LAND,)),
            dma((2,)), dma((2,)), dma((5,)), dma((5,)),
            dma((OWN,)), dma((LAND,)), dma((LAND,)), dma((LAND, 2)), dma((LAND, 2)),
            dma((LAND,)), dma((LAND,)), dma((LAND, 3)), dma((LAND, 3)),
        ],
        compiler_params=pltpu.CompilerParams(
            collective_id=1, has_side_effects=True, vmem_limit_bytes=60 << 20
        ),
    )(dx, last, *kept, vec, segr, segc, weights)


def per_device_fast(
    hidden_in, cotangent, segment_ids, w_qkv, w_out, w_up, w_down, vectors,
    m_qkv, v_qkv, m_out, v_out, m_up, v_up, m_down, v_down, m_vectors, v_vectors,
):
    depth = w_qkv.shape[0]
    shards = jnp.concatenate(
        [w_qkv.astype(BF16), w_out.astype(BF16), w_up.astype(BF16), w_down.astype(BF16).transpose(0, 2, 1)], axis=2
    )
    weights, x, dx, segr, segc, *kept = forward_all(hidden_in, cotangent, segment_ids, vectors, shards)
    hidden_out, grad_in, grad_vectors, grad_all, _ = backward_all(
        dx, x, kept, vectors, segr, segc, weights.reshape(depth, 4, 640, 3200)
    )
    gradients = (
        grad_all[:, :, 0:480], grad_all[:, :, 480:640], grad_all[:, :, 640:1920],
        grad_all[:, :, 1920:3200].transpose(0, 2, 1),
    )
    masters = (w_qkv, w_out, w_up, w_down)
    firsts = (m_qkv, m_out, m_up, m_down)
    seconds = (v_qkv, v_out, v_up, v_down)
    updates = [
        adam_direction(masters[kind], gradients[kind], firsts[kind], seconds[kind], 0.01) for kind in range(4)
    ]
    partial_sums = jnp.stack(
        [jnp.stack(matrix_sums(masters[kind], updates[kind][2]), axis=1) for kind in range(4)], axis=1
    )
    flat = jnp.pad(partial_sums.reshape(1, -1), ((0, 7), (0, 128 - partial_sums.size)))
    total_sums = total_over_devices(flat, 3)[0, : partial_sums.size].reshape(partial_sums.shape)
    lamb_norms = jnp.sqrt(total_sums)
    trust_ratio = lamb_norms[:, :, 0] / lamb_norms[:, :, 1]
    new_masters = [
        masters[kind] - 0.5 * trust_ratio[:, kind, None, None] * updates[kind][2] for kind in range(4)
    ]
    vec_first, vec_second, new_vectors = vector_update(vectors, grad_vectors, m_vectors, v_vectors)
    moments = [part for kind in range(4) for part in updates[kind][:2]]
    return (
        hidden_out, grad_in, *gradients, grad_vectors, *moments, vec_first, vec_second,
        *new_masters, new_vectors, *[w.astype(BF16) for w in new_masters], lamb_norms,
    )


def solution(mesh):
    fast = mesh.shape["row"] == 8 and mesh.shape["col"] == 4
    per_device = per_device_fast if fast else per_device_any
    return jax.shard_map(
        per_device,
        mesh=mesh,
        in_specs=(
            P(("row", "col"), None),
            P(("row", "col"), None),
            P("row", None),
            P(None, "row", "col"),
            P(None, "row", "col"),
            P(None, "row", "col"),
            P(None, "col", "row"),
            P(),
            P(None, "row", "col"),
            P(None, "row", "col"),
            P(None, "row", "col"),
            P(None, "row", "col"),
            P(None, "row", "col"),
            P(None, "row", "col"),
            P(None, "col", "row"),
            P(None, "col", "row"),
            P(),
            P(),
        ),
        out_specs=(
            P(("row", "col"), None),
            P(("row", "col"), None),
            P(None, "row", "col"),
            P(None, "row", "col"),
            P(None, "row", "col"),
            P(None, "col", "row"),
            P(),
            P(None, "row", "col"),
            P(None, "row", "col"),
            P(None, "row", "col"),
            P(None, "row", "col"),
            P(None, "row", "col"),
            P(None, "row", "col"),
            P(None, "col", "row"),
            P(None, "col", "row"),
            P(),
            P(),
            P(None, "row", "col"),
            P(None, "row", "col"),
            P(None, "row", "col"),
            P(None, "col", "row"),
            P(),
            P(None, "row", "col"),
            P(None, "row", "col"),
            P(None, "row", "col"),
            P(None, "col", "row"),
            P(),
        ),
        check_vma=False,
    )
```

```python
import functools
from functools import partial

import jax
import jax.numpy as jnp
from jax import lax
from jax.experimental import pallas as pl
from jax.experimental.pallas import tpu as pltpu
from jax.sharding import PartitionSpec as P

D = 640
HDIM = 32
FF = 5120
STEP = 5


head_groups = 4
negative = -1e30


def layer_norm(values_in, norm_gain, norm_bias):
    average = jnp.mean(values_in, axis=-1, keepdims=True)
    centered = values_in - average
    variance = jnp.mean(centered * centered, axis=-1, keepdims=True)
    return centered * lax.rsqrt(variance + 1e-05) * norm_gain + norm_bias


def to_groups(matrix):
    tokens = matrix.shape[0]
    return matrix.reshape(tokens, head_groups, -1, HDIM).transpose(1, 2, 0, 3)


def from_groups(blocks):
    return blocks.transpose(2, 0, 1, 3).reshape(blocks.shape[2], -1)


def contract_rows(left, right):
    return lax.dot_general(
        left, right, (((0,), (0,)), ((), ())), preferred_element_type=jnp.float32
    )


def contract_cols(left, right):
    return lax.dot_general(
        left, right, (((1,), (1,)), ((), ())), preferred_element_type=jnp.float32
    )


def column_total(matrix):
    return jnp.sum(matrix.astype(jnp.float32), axis=0)


def masked_scores(query_block, key_block, allowed):
    scores = jnp.einsum(
        "hqd,hkd->hqk", query_block, key_block, preferred_element_type=jnp.float32
    ) * HDIM ** (-0.5)
    return jnp.where(allowed[None, :, :], scores, negative)


def attend(queries, all_kv, allowed, kept_lse):
    features = queries.shape[1]
    tokens = queries.shape[0]
    q_groups = to_groups(queries)
    k_groups = to_groups(all_kv[:, :features])
    v_groups = to_groups(all_kv[:, features:])
    if kept_lse is None:

        def first_group(members):
            q_block, k_block, v_block = members
            scores = masked_scores(q_block, k_block, allowed)
            row_max = jnp.max(scores, axis=-1)
            log_total = row_max + jnp.log(jnp.sum(jnp.exp(scores - row_max[..., None]), axis=-1))
            softmax = jnp.exp(scores - log_total[..., None]).astype(jnp.bfloat16)
            return (
                jnp.einsum("hqk,hkd->hqd", softmax, v_block, preferred_element_type=jnp.float32),
                log_total,
            )

        attended, log_total = lax.map(first_group, (q_groups, k_groups, v_groups))
    else:
        log_total = kept_lse.reshape(head_groups, -1, tokens)

        def again_group(members):
            q_block, k_block, v_block, lse_block = members
            softmax = jnp.exp(
                masked_scores(q_block, k_block, allowed) - lse_block[..., None]
            ).astype(jnp.bfloat16)
            return jnp.einsum("hqk,hkd->hqd", softmax, v_block, preferred_element_type=jnp.float32)

        attended = lax.map(again_group, (q_groups, k_groups, v_groups, log_total))
    return (from_groups(attended).astype(jnp.bfloat16), log_total.reshape(-1, tokens))


def attention_back(queries, all_kv, grad_mixed, kept_lse, allowed):
    features = queries.shape[1]
    tokens = queries.shape[0]
    inv_root = HDIM ** (-0.5)
    q_groups = to_groups(queries)
    k_groups = to_groups(all_kv[:, :features])
    v_groups = to_groups(all_kv[:, features:])
    g_groups = to_groups(grad_mixed)
    lse_groups = kept_lse.reshape(head_groups, -1, tokens)

    def one_group(members):
        q_block, k_block, v_block, g_block, lse_block = members
        softmax = jnp.exp(masked_scores(q_block, k_block, allowed) - lse_block[..., None])
        grad_probs = jnp.einsum(
            "hqd,hkd->hqk", g_block, v_block, preferred_element_type=jnp.float32
        )
        row_dot = jnp.sum(softmax * grad_probs, axis=-1, keepdims=True)
        grad_scores = (softmax * (grad_probs - row_dot)).astype(jnp.bfloat16)
        grad_q = (
            jnp.einsum("hqk,hkd->hqd", grad_scores, k_block, preferred_element_type=jnp.float32)
            * inv_root
        )
        grad_k = (
            jnp.einsum("hqk,hqd->hkd", grad_scores, q_block, preferred_element_type=jnp.float32)
            * inv_root
        )
        grad_v = jnp.einsum(
            "hqk,hqd->hkd",
            softmax.astype(jnp.bfloat16),
            g_block,
            preferred_element_type=jnp.float32,
        )
        return (grad_q, grad_k, grad_v)

    grad_q, grad_k, grad_v = lax.map(
        one_group, (q_groups, k_groups, v_groups, g_groups, lse_groups)
    )
    return (
        from_groups(grad_q),
        jnp.concatenate([from_groups(grad_k), from_groups(grad_v)], axis=1),
    )


def layer_forward(state_in, weights, vector, allowed, kept_lse):
    w_qkv_full, w_out_full, w_up_part, w_down_part = weights
    features = state_in.shape[1]
    normed = layer_norm(state_in, vector[0:features], vector[features : 2 * features]).astype(
        jnp.bfloat16
    )
    projected = jnp.dot(normed, w_qkv_full, preferred_element_type=jnp.float32)
    queries = (projected[:, :features] + vector[2 * features : 3 * features]).astype(jnp.bfloat16)
    kv_bias = jnp.concatenate(
        [jnp.zeros((features,), jnp.float32), vector[3 * features : 4 * features]]
    )
    own_kv = (projected[:, features:] + kv_bias).astype(jnp.bfloat16)
    all_kv = lax.all_gather(own_kv, "col", axis=0, tiled=True)
    attended, log_total = attend(queries, all_kv, allowed, kept_lse)
    middle = state_in + (
        jnp.dot(attended, w_out_full, preferred_element_type=jnp.float32)
        + vector[4 * features : 5 * features]
    )
    normed_ffn = layer_norm(
        middle, vector[5 * features : 6 * features], vector[6 * features : 7 * features]
    ).astype(jnp.bfloat16)
    before = (
        jnp.dot(normed_ffn, w_up_part, preferred_element_type=jnp.float32) + vector[8 * features :]
    )
    hidden = jax.nn.gelu(before, approximate=False).astype(jnp.bfloat16)
    branch = jnp.dot(hidden, w_down_part, preferred_element_type=jnp.float32)
    state_out = middle + (branch + vector[7 * features : 8 * features])
    kept_vals = (normed, queries, all_kv, log_total, attended, middle, normed_ffn, before, hidden)
    return (state_out, kept_vals)


def layer_backward(grad_state, state_in, kept_vals, weights, vector, allowed):
    w_qkv_full, w_out_full, w_up_part, w_down_part = weights
    normed, queries, all_kv, log_total, attended, middle, ffn_rows, before, hidden = kept_vals
    features = state_in.shape[1]
    grad_branch = grad_state.astype(jnp.bfloat16)
    gelu_vjp = jax.vjp(partial(jax.nn.gelu, approximate=False), before)[1]
    grad_down = contract_rows(hidden, grad_branch)
    grad_before = gelu_vjp(contract_cols(grad_branch, w_down_part))[0].astype(jnp.bfloat16)
    grad_up = contract_rows(ffn_rows, grad_before)
    grad_up_bias = column_total(grad_before)
    grad_normed_ffn = contract_cols(grad_before, w_up_part)
    norm_two = jax.vjp(
        layer_norm, middle, vector[5 * features : 6 * features], vector[6 * features : 7 * features]
    )[1]
    grad_middle_norm, grad_gain_two, grad_bias_two = norm_two(grad_normed_ffn)
    grad_middle = grad_state + grad_middle_norm
    grad_attn_out = grad_middle.astype(jnp.bfloat16)
    grad_out_w = contract_rows(attended, grad_attn_out)
    grad_mixed = contract_cols(grad_attn_out, w_out_full).astype(jnp.bfloat16)
    grad_queries, kv_terms = attention_back(queries, all_kv, grad_mixed, log_total, allowed)
    grad_kv = lax.psum_scatter(
        kv_terms.astype(jnp.bfloat16), "col", scatter_dimension=0, tiled=True
    )
    grad_queries = grad_queries.astype(jnp.bfloat16)
    grad_proj = jnp.concatenate([grad_queries, grad_kv], axis=1)
    grad_qkv_w = contract_rows(normed, grad_proj)
    grad_normed = contract_cols(grad_proj, w_qkv_full)
    norm_one = jax.vjp(layer_norm, state_in, vector[0:features], vector[features : 2 * features])[1]
    grad_input_norm, grad_gain_one, grad_bias_one = norm_one(grad_normed)
    grad_input = grad_middle + grad_input_norm
    grad_vector = jnp.concatenate(
        [
            grad_gain_one,
            grad_bias_one,
            column_total(grad_queries),
            column_total(grad_kv[:, features:]),
            column_total(grad_attn_out),
            grad_gain_two,
            grad_bias_two,
            column_total(grad_branch),
            grad_up_bias,
        ]
    )
    return (grad_input, (grad_qkv_w, grad_out_w, grad_up, grad_down), grad_vector)


def adam_direction(weight, gradient, first_mom, second_mom, decay_rate):
    first_new = 0.9 * first_mom + 0.1 * gradient
    second_new = 0.999 * second_mom + 0.001 * gradient * gradient
    direction = (
        first_new / (1.0 - 0.9**STEP) / (jnp.sqrt(second_new / (1.0 - 0.999**STEP)) + 1e-06)
        + decay_rate * weight
    )
    return (first_new, second_new, direction)


def matrix_sums(weight, direction):
    return (jnp.sum(weight * weight, axis=(1, 2)), jnp.sum(direction * direction, axis=(1, 2)))


def vector_update(vector, gradient, first_mom, second_mom):
    first_new, second_new, direction = adam_direction(vector, gradient, first_mom, second_mom, 0.0)
    depth_count = vector.shape[0]
    head_part = 8 * D

    def ratio_of(weight_part, step_part):
        return jnp.sqrt(jnp.sum(weight_part * weight_part, axis=-1, keepdims=True)) / jnp.sqrt(
            jnp.sum(step_part * step_part, axis=-1, keepdims=True)
        )

    lead_ratio = ratio_of(
        vector[:, :head_part].reshape(depth_count, 8, D),
        direction[:, :head_part].reshape(depth_count, 8, D),
    )
    tail_ratio = ratio_of(vector[:, head_part:], direction[:, head_part:])
    trust_ratio = jnp.concatenate(
        [
            jnp.broadcast_to(lead_ratio, (depth_count, 8, D)).reshape(depth_count, head_part),
            jnp.broadcast_to(tail_ratio, (depth_count, FF)),
        ],
        axis=1,
    )
    return (first_new, second_new, vector - 0.5 * trust_ratio * direction)


def per_device_any(
    hidden_in,
    cotangent,
    segment_ids,
    w_qkv,
    w_out,
    w_up,
    w_down,
    vectors,
    m_qkv,
    v_qkv,
    m_out,
    v_out,
    m_up,
    v_up,
    m_down,
    v_down,
    m_vectors,
    v_vectors,
):
    tokens = hidden_in.shape[0]
    depth_count = w_qkv.shape[0]
    group_ids = segment_ids[0]
    own_ids = lax.dynamic_slice_in_dim(group_ids, lax.axis_index("col") * tokens, tokens)
    allowed = own_ids[:, None] == group_ids[None, :]

    def gather_weights(layer_at):
        qkv_raw = w_qkv[layer_at].astype(jnp.bfloat16)
        out_raw = w_out[layer_at].astype(jnp.bfloat16)
        up_raw = w_up[layer_at].astype(jnp.bfloat16)
        down_raw = w_down[layer_at].astype(jnp.bfloat16)
        qkv_cols, out_cols, up_cols, down_cols = (
            lax.all_gather(qkv_raw, "col", axis=1, tiled=True),
            lax.all_gather(out_raw, "col", axis=1, tiled=True),
            lax.all_gather(up_raw, "col", axis=1, tiled=True),
            lax.all_gather(down_raw, "col", axis=0, tiled=True),
        )
        return (
            lax.all_gather(qkv_cols, "row", axis=0, tiled=True),
            lax.all_gather(out_cols, "row", axis=0, tiled=True),
            lax.all_gather(up_cols, "row", axis=0, tiled=True),
            lax.all_gather(down_cols, "row", axis=1, tiled=True),
        )

    current = hidden_in.astype(jnp.float32)
    layer_inputs = []
    kept_runs = []
    kept_weights = []
    for layer_at in range(depth_count):
        weights = gather_weights(layer_at)
        layer_inputs.append(current)
        current, kept_vals = layer_forward(current, weights, vectors[layer_at], allowed, None)
        kept_runs.append(kept_vals)
        kept_weights.append(weights)
    grad_current = cotangent
    grads_by_layer = [None] * depth_count
    vector_grads = [None] * depth_count
    for layer_at in reversed(range(depth_count)):
        weights = gather_weights(layer_at)
        unused_out, kept_vals = layer_forward(
            layer_inputs[layer_at], weights, vectors[layer_at], allowed, kept_runs[layer_at][3]
        )
        grad_current, matrix_grads, vector_grad = layer_backward(
            grad_current, layer_inputs[layer_at], kept_vals, weights, vectors[layer_at], allowed
        )
        rows_done = (
            lax.psum_scatter(
                matrix_grads[0].astype(jnp.bfloat16), "row", scatter_dimension=0, tiled=True
            ).astype(jnp.float32),
            lax.psum_scatter(
                matrix_grads[1].astype(jnp.bfloat16), "row", scatter_dimension=0, tiled=True
            ).astype(jnp.float32),
            lax.psum_scatter(
                matrix_grads[2].astype(jnp.bfloat16), "row", scatter_dimension=0, tiled=True
            ).astype(jnp.float32),
            lax.psum_scatter(
                matrix_grads[3].astype(jnp.bfloat16), "row", scatter_dimension=1, tiled=True
            ).astype(jnp.float32),
        )
        shards = (
            lax.psum_scatter(
                rows_done[0].astype(jnp.bfloat16), "col", scatter_dimension=1, tiled=True
            ).astype(jnp.float32),
            lax.psum_scatter(
                rows_done[1].astype(jnp.bfloat16), "col", scatter_dimension=1, tiled=True
            ).astype(jnp.float32),
            lax.psum_scatter(
                rows_done[2].astype(jnp.bfloat16), "col", scatter_dimension=1, tiled=True
            ).astype(jnp.float32),
            lax.psum_scatter(
                rows_done[3].astype(jnp.bfloat16), "col", scatter_dimension=0, tiled=True
            ).astype(jnp.float32),
        )
        grads_by_layer[layer_at] = shards
        vector_grads[layer_at] = vector_grad
    masters = (w_qkv, w_out, w_up, w_down)
    firsts = (m_qkv, m_out, m_up, m_down)
    seconds = (v_qkv, v_out, v_up, v_down)
    gradients = tuple(
        (
            jnp.stack([grads_by_layer[layer_at][kind] for layer_at in range(depth_count)])
            for kind in range(4)
        )
    )
    updates = [
        adam_direction(masters[kind], gradients[kind], firsts[kind], seconds[kind], 0.01)
        for kind in range(4)
    ]
    partial_sums = jnp.stack(
        [jnp.stack(matrix_sums(masters[kind], updates[kind][2]), axis=1) for kind in range(4)],
        axis=1,
    )
    grad_vectors, total_sums = lax.psum((jnp.stack(vector_grads), partial_sums), ("row", "col"))
    lamb_norms = jnp.sqrt(total_sums)
    trust_ratio = lamb_norms[:, :, 0] / lamb_norms[:, :, 1]
    new_masters = [
        masters[kind] - 0.5 * trust_ratio[:, kind, None, None] * updates[kind][2]
        for kind in range(4)
    ]
    vec_first, vec_second, new_vectors = vector_update(vectors, grad_vectors, m_vectors, v_vectors)
    return (
        current,
        grad_current,
        gradients[0],
        gradients[1],
        gradients[2],
        gradients[3],
        grad_vectors,
        updates[0][0],
        updates[0][1],
        updates[1][0],
        updates[1][1],
        updates[2][0],
        updates[2][1],
        updates[3][0],
        updates[3][1],
        vec_first,
        vec_second,
        new_masters[0],
        new_masters[1],
        new_masters[2],
        new_masters[3],
        new_vectors,
        new_masters[0].astype(jnp.bfloat16),
        new_masters[1].astype(jnp.bfloat16),
        new_masters[2].astype(jnp.bfloat16),
        new_masters[3].astype(jnp.bfloat16),
        lamb_norms,
    )


MESH = pl.DeviceIdType.MESH
F32 = jnp.float32
BF16 = jnp.bfloat16
NT = (((1,), (1,)), ((), ()))
CHUNK = 640
VM = pl.BlockSpec(memory_space=pltpu.VMEM)
ANY = pl.BlockSpec(memory_space=pl.ANY)
SCALE = HDIM ** (-0.5)
SCALE2 = SCALE * 1.4426950408889634
HEADS = 5
HW = HEADS * HDIM


def where_am_i():
    r = lax.axis_index("row")
    z = lax.axis_index("col")
    return r // 4, (r // 2) % 2, r % 2, z


def row_of(y, x, c):
    return (y * 2 + x) * 2 + c


def trade_partners(y, x, c, z):
    yf = y + (1 - c) * (1 - 2 * y)
    xf = x + c * (1 - 2 * x)
    yg = y + c * (1 - 2 * y)
    xg = x + (1 - c) * (1 - 2 * x)
    return (yf, xf), (yg, xg), (1 - y, 1 - x)


def greet(peers):
    barrier = pltpu.get_barrier_semaphore()
    for peer in peers:
        pl.semaphore_signal(barrier, inc=1, device_id=peer, device_id_type=MESH)
    pl.semaphore_wait(barrier, len(peers))


def remote(src, dst, send_sem, recv_sem, peer):
    return pltpu.make_async_remote_copy(
        src_ref=src, dst_ref=dst, send_sem=send_sem, recv_sem=recv_sem,
        device_id=peer, device_id_type=MESH,
    )


def total_kernel(x_ref, o_ref, rows, cols, rs_send, rs_recv, cs_send, cs_recv):
    y, x, c, z = where_am_i()
    r = row_of(y, x, c)
    row_peers = [(lax.rem(r + k, 8), z) for k in range(1, 8)]
    col_peers = [(r, lax.rem(z + k, 4)) for k in range(1, 4)]
    greet(row_peers + col_peers)
    rows[r] = x_ref[...]
    copies = [
        remote(x_ref, rows.at[r], rs_send.at[k], rs_recv.at[k], peer) for k, peer in enumerate(row_peers)
    ]
    for cp in copies:
        cp.start()
    for cp in copies:
        cp.wait()
    total = rows[0]
    for k in range(1, 8):
        total = total + rows[k]
    cols[z] = total
    copies = [
        remote(cols.at[z], cols.at[z], cs_send.at[k], cs_recv.at[k], peer) for k, peer in enumerate(col_peers)
    ]
    for cp in copies:
        cp.start()
    for cp in copies:
        cp.wait()
    o_ref[...] = cols[0] + cols[1] + cols[2] + cols[3]


def total_over_devices(x, cid):
    dma = pltpu.SemaphoreType.DMA
    return pl.pallas_call(
        total_kernel,
        name="total",
        out_shape=jax.ShapeDtypeStruct(x.shape, F32),
        in_specs=[VM],
        out_specs=VM,
        scratch_shapes=[
            pltpu.VMEM((8,) + x.shape, F32), pltpu.VMEM((4,) + x.shape, F32),
            dma((7,)), dma((7,)), dma((3,)), dma((3,)),
        ],
        compiler_params=pltpu.CompilerParams(collective_id=cid, has_side_effects=True),
    )(x)


def attention_peers(y, x, c, z):
    return c * 2 + z % 2, lambda b: (row_of(y, x, b // 2), (z // 2) * 2 + b % 2)


def norm_parts(values):
    average = jnp.mean(values, axis=-1, keepdims=True)
    centered = values - average
    variance = jnp.mean(centered * centered, axis=-1, keepdims=True)
    spread = lax.rsqrt(variance + 1e-05)
    return centered * spread, spread


def dot(a, b):
    return jnp.dot(a, b, preferred_element_type=F32)


def dot_nt(a, b):
    return lax.dot_general(a, b, NT, preferred_element_type=F32)


def piece(vec_ref, at, count=640):
    return vec_ref[0:1, at : at + count]


def exchange(me, peer_of, sbuf, rbuf, ss, rs):
    y, x, c, z = where_am_i()
    out = []
    for k in (1, 2, 3):
        b = lax.rem(me + k, 4)
        out.append(remote(sbuf.at[b], rbuf.at[me], ss.at[k], rs.at[k], peer_of(b)))
    for cp in out:
        cp.start()
    return out


def head_mask(h, rows):
    lane = lax.broadcasted_iota(jnp.int32, (rows, HW), 1)
    return (lane >= h * HDIM) & (lane < (h + 1) * HDIM)


def fold(values, n):
    rows = 320 // n
    return jnp.concatenate([values[rows * j : rows * (j + 1)] for j in range(n)], axis=1)


GROUPS = ((0, 2, 2), (2, 3, 4))


def group_shapes():
    return [(4, 320 // n, n * 3 * heads * HDIM) for _, heads, n in GROUPS]


def pack_group(group, parts):
    first, heads, n = GROUPS[group]
    cut = slice(first * HDIM, (first + heads) * HDIM)
    return fold(jnp.concatenate([part[:, cut] for part in parts], axis=1), n).astype(BF16)


def unpack_group(group, block, kind):
    _, heads, n = GROUPS[group]
    w = heads * HDIM
    return jnp.concatenate(
        [block[:, (3 * j + kind) * w : (3 * j + kind + 1) * w].astype(F32) for j in range(n)], axis=0
    )


QB = 256
LAYERS = 2
NCH = LAYERS * 5
PIECES = ((0, 0, 256), (0, 256, 256), (0, 512, 768)) + tuple(
    (layer, col, CHUNK) for layer in range(LAYERS) for col in range(0, 3200, CHUNK) if layer or col >= 1280
)


class Steps:
    def run(self, plan):
        for at in range(0, len(plan), 2):
            self.step(plan[at], int(plan[at + 1], 16))

    def run_at(self, plans, index):
        for at, plan in enumerate(plans):
            if plan:
                @pl.when(index == at)
                def _():
                    self.run(plan)


class Gather(Steps):
    def __init__(self, s_ref, w_ref, wbuf, zs, zr, ps, pr, own_sem, load_sem):
        y, x, c, z = where_am_i()
        self.s_ref, self.w_ref, self.wbuf = s_ref, w_ref, wbuf
        self.sems = zs, zr, ps, pr, own_sem, load_sem
        (yf, xf), (yg, xg), (yd, xd) = trade_partners(y, x, c, z)
        self.z, self.r = z, row_of(y, x, c)
        self.c, self.q, self.qf = c, y * 2 + x, yf * 2 + xf
        self.zpeers = [(self.r, lax.rem(z + k, 4)) for k in (1, 2, 3)]
        self.pf, self.pg, self.sib = (row_of(yf, xf, c), z), (row_of(yg, xg, c), z), (row_of(y, x, 1 - c), z)

    def cols(self, t):
        layer, col, width = PIECES[t]
        return layer, pl.ds(col, width)

    def zcopy(self, t, k):
        layer, cs = self.cols(t)
        zs, zr = self.sems[:2]
        return remote(
            self.s_ref.at[layer, :, cs], self.w_ref.at[layer, self.z, self.q, self.c, :, cs],
            zs.at[t, k], zr.at[t, k], self.zpeers[k],
        )

    def own(self, t):
        layer, cs = self.cols(t)
        return pltpu.make_async_copy(
            self.s_ref.at[layer, :, cs], self.w_ref.at[layer, self.z, self.q, self.c, :, cs], self.sems[4].at[t]
        )

    def hop(self, t, which):
        layer, cs = self.cols(t)
        chip, peer = (
            (self.q, self.pf), (self.q, self.pg), (self.qf, self.pg), (slice(None), self.sib)
        )[which]
        block = self.w_ref.at[layer, :, chip, self.c, :, cs]
        return remote(block, block, self.sems[2].at[t, which], self.sems[3].at[t, which], peer)

    def load(self, t):
        layer, cs = self.cols(t)
        return pltpu.make_async_copy(self.w_ref.at[layer, :, :, :, :, cs], self.wbuf.at[:, :, :, :, cs], self.sems[5].at[t])

    def step(self, name, t):
        if name == "Z":
            for k in range(3):
                self.zcopy(t, k).start()
            self.own(t).start()
        elif name == "z":
            for k in range(3):
                self.zcopy(t, k).wait()
            self.own(t).wait()
            for which in (0, 1):
                self.hop(t, which).start()
        elif name == "f":
            self.hop(t, 0).wait()
            self.hop(t, 2).start()
        elif name == "g":
            self.hop(t, 1).wait()
            self.hop(t, 2).wait()
            self.hop(t, 3).start()
        elif name == "s":
            self.hop(t, 3).wait()
        elif name == "L":
            self.load(t).start()
        elif name == "l":
            self.load(t).wait()


PLAN = {
    "start": "Z0",
    "first": "z0Z1f0z1Z2g0f1Z3g1s0L0s1L1z2Z4l0l1",
    "sent0": "z3Z5f2z4Z6",
    "heads0": ["f3z5Z7", "g2s2L2", "f4z6Z8", "g3s3L3", "f5"],
    "osent0": "l2g4z7Z9",
    "up0": ["s4L4", "", "f6z8Za", "g5", "l3", "", "s5L5", "z9f7"],
    "down0": ["l4", "l5"],
    "qkv1": "g6s6L6l6",
    "sent1": "f8g7za",
    "heads1": ["f9g8s7L7", "", "s8L8", "fag9", "s9L9"],
    "osent1": "ga",
    "up1": ["l7sa", "", "", "", "l8La", "", "", ""],
    "down1": ["l9", "la"],
}


def swap_partner(y, x, c, z):
    return row_of(y, x, 1 - c), lax.rem(z + 2, 4)


def move_tokens(src, dst, send, recv, then):
    y, x, c, z = where_am_i()
    goes = c != z // 2
    copy = remote(src, dst, send, recv, swap_partner(y, x, c, z))
    stay = pltpu.make_async_copy(src, dst, send)

    @pl.when(goes)
    def _():
        copy.wait() if then else copy.start()

    @pl.when(jnp.logical_not(goes))
    def _():
        stay.wait() if then else stay.start()


SAVED = ("x", "xm", "o", "hdn", "gp", "q", "k", "v", "oh", "lse")


def forward_kernel(hid_ref, cot_ref, seg_ref, vec_ref, s_ref,
                   w_ref, xo_ref, dx_ref, segr_ref, segc_ref,
                   x_out, xm_out, o_out, hdn_out, gp_out, q_out, k_out, v_out, oh_out, lse_out,
                   wbuf, hid, xcur, xm_s, o_s, hdn_s, gp_s, q_s, k_s, v_s, oh_s, lse_s,
                   abuf, ubuf, pbuf, segbuf, sbuf0, sbuf1, rbuf0, rbuf1, osbuf, orbuf, vt, ot,
                   zs, zr, ps, pr, own_sem, load_sem, ss, rs, oss, ors, save_sem, mv_s, mv_r):
    y, x, c, z = where_am_i()
    me, peer_of = attention_peers(y, x, c, z)
    sbufs, rbufs = (sbuf0, sbuf1), (rbuf0, rbuf1)
    net = Gather(s_ref, w_ref, wbuf, zs, zr, ps, pr, own_sem, load_sem)
    zx = z + 1 - 2 * lax.rem(z, 2)
    greet(net.zpeers + [net.pf, net.pg, net.sib, (row_of(y, x, 1 - c), zx), swap_partner(y, x, c, z)])
    move_tokens(hid_ref, hid, mv_s.at[0], mv_r.at[0], 0)
    seg_copy = remote(seg_ref, segbuf.at[1], mv_s.at[1], mv_r.at[1], net.sib)
    seg_copy.start()
    net.run(PLAN["start"])
    move_tokens(hid_ref, hid, mv_s.at[0], mv_r.at[0], 1)
    seg_copy.wait()
    segbuf[0] = seg_ref[...]
    segr_ref[...] = jnp.where(c == z // 2, segbuf[0], segbuf[1])
    segc_ref[...] = jnp.broadcast_to(segr_ref[...].astype(F32), (8, 1280)).T[:, 0:1].astype(jnp.int32)
    xcur[...] = hid[...].astype(F32)

    kept = dict(zip(SAVED, (
        (xcur, x_out), (xm_s, xm_out), (o_s, o_out), (hdn_s, hdn_out), (gp_s, gp_out),
        (q_s, q_out), (k_s, k_out), (v_s, v_out), (oh_s, oh_out), (lse_s, lse_out))))

    def save(name, layer):
        src, dst = kept[name]
        return pltpu.make_async_copy(src, dst.at[layer], save_sem.at[layer, SAVED.index(name)])

    def held(i, col, width):
        return wbuf[i, :, :, :, col : col + width].reshape(640, width)

    def before(name, layer):
        if layer:
            save(name, layer - 1).wait()

    for layer in range(LAYERS):
        vl = vec_ref.at[pl.ds(layer, 1), :]
        save("x", layer).start()
        n1, _ = norm_parts(xcur[...])
        a = (n1 * piece(vl, 0) + piece(vl, 640)).astype(BF16)
        net.run(PLAN["qkv1" if layer else "first"])
        abuf[...] = a

        for i in range(4):
            pbuf[i] = dot(abuf[...], held(i, 0, 512))

        blocks = [pbuf[b // 3, :, (b % 3) * HW : (b % 3 + 1) * HW] for b in range(12)]
        for b in range(4):
            q = blocks[b] + vl[0:1, 1280 + HW * b : 1280 + HW * (b + 1)]
            v = blocks[8 + b] + vl[0:1, 1920 + HW * b : 1920 + HW * (b + 1)]
            for g in range(2):
                sbufs[g][b] = pack_group(g, (q, blocks[4 + b], v))
        copies = exchange(me, peer_of, sbufs[0], rbufs[0], ss.at[layer, 0], rs.at[layer, 0])
        for name in ("q", "k", "v", "oh", "lse"):
            before(name, layer)
        if layer == 0:
            k_s[...] = jnp.zeros_like(k_s)
        net.run(PLAN["sent%d" % layer])
        lse_s[...] = jnp.zeros_like(lse_s)

        for g, (first, heads, _) in enumerate(GROUPS):
            rbufs[g][me] = sbufs[g][me]
            for cp in copies:
                cp.wait()
            if g == 0:
                copies = exchange(me, peer_of, sbufs[1], rbufs[1], ss.at[layer, 1], rs.at[layer, 1])
            cut = slice(first * HDIM, (first + heads) * HDIM)
            for b in range(4):
                rows = slice(320 * b, 320 * (b + 1))
                for kind, ref in enumerate((q_s, k_s, v_s)):
                    ref[rows, cut] = unpack_group(g, rbufs[g][b], kind).astype(BF16)
            wide = 128 if g == 0 else HW
            vt[cut, :] = v_s[:, 0:wide].astype(F32).T[cut, :].astype(BF16)
            if g == 1:
                for name in ("q", "k", "v"):
                    save(name, layer).start()

            @pl.loop(first, first + heads)
            def _(h):
                net.run_at(PLAN["heads%d" % layer][first : first + heads], h - first)

                @pl.loop(0, 5, unroll=5)
                def _(step):
                    at = pl.multiple_of(step * QB, QB)
                    qm = jnp.where(head_mask(h, QB), q_s[pl.ds(at, QB), :], jnp.zeros((), BF16))
                    s = dot_nt(k_s[...], qm)
                    s = jnp.where(segc_ref[...] == segr_ref[0:1, pl.ds(at, QB)], s, negative)
                    top = jnp.max(s, axis=0, keepdims=True)
                    p = jnp.exp2(s * SCALE2 - top * SCALE2)
                    total = jnp.sum(p, axis=0, keepdims=True)
                    rows = pl.ds(pl.multiple_of(h * HDIM, HDIM), HDIM)
                    ot[rows, pl.ds(at, QB)] = dot(vt[rows, :], p.astype(BF16)) / total
                    lse_s[pl.ds(h, 1), pl.ds(at, QB)] = top * SCALE2 + jnp.log2(total)

        save("lse", layer).start()
        oh_s[...] = ot[...].T.astype(BF16)
        save("oh", layer).start()
        for b in range(4):
            osbuf[b] = fold(oh_s[320 * b : 320 * (b + 1), :].astype(F32), 4).astype(BF16)
        copies = exchange(me, peer_of, osbuf, orbuf, oss.at[layer], ors.at[layer])
        orbuf[me] = osbuf[me]
        for name in ("o", "xm", "hdn", "gp"):
            before(name, layer)
        net.run(PLAN["osent%d" % layer])
        for cp in copies:
            cp.wait()
        for j in range(4):
            o_s[80 * j : 80 * (j + 1), :] = jnp.concatenate(
                [orbuf[b, :, HW * j : HW * (j + 1)].astype(F32) for b in range(4)], axis=1
            ).astype(BF16)
        save("o", layer).start()

        for i in range(4):
            pbuf[i, :, 0:256] = dot(o_s[...], held(i, 384, 256))

        yv = jnp.concatenate([pbuf[i, :, 96:256] for i in range(4)], axis=1)
        xm = xcur[...] + (yv + piece(vl, 2560))
        xm_s[...] = xm
        save("xm", layer).start()
        n2, _ = norm_parts(xm)
        abuf[...] = (n2 * piece(vl, 3200) + piece(vl, 3840)).astype(BF16)
        if layer == 0:
            move_tokens(cot_ref, dx_ref, mv_s.at[2], mv_r.at[2], 0)

        for half in range(2):
            @pl.loop(0, 4)
            def _(i):
                net.run_at(PLAN["up%d" % layer][4 * half : 4 * half + 4], i)

                to = pl.multiple_of(i * 1280 + half * 640, 640)
                ubuf[...] = dot(abuf[...], held(i, 640 * (half + 1), 640)) + vl[0:1, pl.ds(5120 + to, 640)]

                @pl.loop(0, 10)
                def _(j):
                    rows = pl.ds(pl.multiple_of(j * 32, 32), 32)
                    u = ubuf[rows, :]
                    cdf = 0.5 * (1.0 + lax.erf(u * (0.5**0.5)))
                    hdn_s[rows, pl.ds(to, 640)] = (u * cdf).astype(BF16)
                    gp_s[rows, pl.ds(to, 640)] = (
                        cdf + u * (jnp.exp(-0.5 * u * u) * 0.3989422804014327)
                    ).astype(BF16)

        save("hdn", layer).start()
        save("gp", layer).start()
        save("x", layer).wait()
        xcur[...] = xm_s[...] + piece(vl, 4480)
        for half in range(2):
            net.run(PLAN["down%d" % layer][half])

            @pl.loop(0, 4)
            def _(i):
                to = pl.multiple_of(i * 1280 + half * 640, 640)
                xcur[...] += dot_nt(hdn_s[:, pl.ds(to, 640)], held(i, 640 * (half + 3), 640))


    xo_ref[...] = xcur[...]
    for name in SAVED[1:]:
        save(name, LAYERS - 1).wait()
    move_tokens(cot_ref, dx_ref, mv_s.at[2], mv_r.at[2], 1)


def forward_all(hidden, cotangent, segments, vectors, shards):
    dma = pltpu.SemaphoreType.DMA
    sds = jax.ShapeDtypeStruct
    vmem = pltpu.VMEM
    return pl.pallas_call(
        forward_kernel,
        name="forward",
        out_shape=(
            sds((LAYERS, 4, 4, 2, 80, 3200), BF16), sds((320, 640), F32), sds((320, 640), F32),
            sds((1, 1280), jnp.int32), sds((1280, 1), jnp.int32),
            sds((LAYERS, 320, 640), F32), sds((LAYERS, 320, 640), F32), sds((LAYERS, 320, 640), BF16),
            sds((LAYERS, 320, 5120), BF16), sds((LAYERS, 320, 5120), BF16),
            sds((LAYERS, 1280, HW), BF16), sds((LAYERS, 1280, HW), BF16), sds((LAYERS, 1280, HW), BF16),
            sds((LAYERS, 1280, HW), BF16), sds((LAYERS, 8, 1280), F32),
        ),
        in_specs=[ANY, ANY, VM, VM, ANY],
        out_specs=(ANY, VM, ANY, VM, VM) + (ANY,) * 10,
        scratch_shapes=[
            vmem((4, 4, 2, 80, 3200), BF16), vmem((320, 640), BF16), vmem((320, 640), F32),
            vmem((320, 640), F32), vmem((320, 640), BF16), vmem((320, 5120), BF16), vmem((320, 5120), BF16),
            vmem((1280, HW), BF16), vmem((1280, HW), BF16), vmem((1280, HW), BF16), vmem((1280, HW), BF16),
            vmem((8, 1280), F32),
            vmem((320, 640), BF16), vmem((320, 640), F32), vmem((4, 320, 512), F32), vmem((2, 1, 1280), jnp.int32),
            *[vmem(shape, BF16) for shape in group_shapes() * 2],
            vmem((4, 80, 640), BF16), vmem((4, 80, 640), BF16),
            vmem((HW, 1280), BF16), vmem((HW, 1280), F32),
            *[dma((len(PIECES),) + shape) for shape in ((3,), (3,), (4,), (4,), (), ())],
            dma((LAYERS, 2, 4)), dma((LAYERS, 2, 4)), dma((LAYERS, 4)), dma((LAYERS, 4)),
            dma((LAYERS, len(SAVED))), dma((3,)), dma((3,)),
        ],
        compiler_params=pltpu.CompilerParams(
            collective_id=0, has_side_effects=True, vmem_limit_bytes=56 << 20
        ),
    )(hidden, cotangent, segments, vectors, shards)


def norm_back(dy, n, spread, gain):
    dn = dy * gain
    mean1 = jnp.mean(dn, axis=-1, keepdims=True)
    mean2 = jnp.mean(dn * n, axis=-1, keepdims=True)
    return spread * (dn - mean1 - n * mean2)


def col_sum(values):
    return jnp.sum(values, axis=0, keepdims=True)


ORDER = (3, 1, 4, 2, 0)
OWN, LAND = 4, 2
HELD = {(1, 3): 0, (1, 1): 1, (1, 4): 2, (1, 2): 3, (1, 0): 0, (0, 3): 1, (0, 1): 2, (0, 4): 3, (0, 2): 0, (0, 0): 1}


class Scatter(Steps):
    def __init__(self, g_ref, out_ref, own, sibr, p2r, p1r, zr, fin, fsem, sems):
        y, x, c, z = where_am_i()
        (yf, xf), (yg, xg), (yd, xd) = trade_partners(y, x, c, z)
        self.c, self.z = c, z
        self.q, self.qf, self.qg, self.qd = y * 2 + x, yf * 2 + xf, yg * 2 + xg, yd * 2 + xd
        r = row_of(y, x, c)
        self.zpeers = [(r, lax.rem(z + k, 4)) for k in (1, 2, 3)]
        self.pf, self.pg = (self.qf * 2 + c, z), (self.qg * 2 + c, z)
        self.sib = (row_of(y, x, 1 - c), z)
        self.g_ref, self.out_ref = g_ref, out_ref
        self.own, self.sibr, self.p2r, self.p1r, self.zr = own, sibr, p2r, p1r, zr
        self.fin, self.fsem, self.sems = fin, fsem, sems

    def where(self, t):
        return LAYERS - 1 - t // 5, ORDER[t % 5] * CHUNK

    def part(self, t, core):
        layer, col = self.where(t)
        return self.g_ref.at[layer, :, :, core, :, pl.ds(col, CHUNK)]

    def own_copy(self, t):
        return pltpu.make_async_copy(self.part(t, self.c), self.own.at[t % OWN], self.sems[0].at[t % OWN])

    def sib_copy(self, t):
        k = t % LAND
        return remote(
            self.part(t, 1 - self.c), self.sibr.at[k], self.sems[1].at[k], self.sems[2].at[k], self.sib
        )

    def p2_copy(self, t, j):
        k = t % LAND
        return remote(
            self.own.at[t % OWN, :, (self.qg, self.qd)[j]], self.p2r.at[k, j],
            self.sems[3].at[k, j], self.sems[4].at[k, j], self.pg,
        )

    def p1_copy(self, t):
        k = t % LAND
        return remote(
            self.own.at[t % OWN, :, self.qf], self.p1r.at[k], self.sems[5].at[k], self.sems[6].at[k], self.pf
        )

    def z_copy(self, t, j):
        k = t % LAND
        return remote(
            self.own.at[t % OWN, lax.rem(self.z + j + 1, 4), self.q], self.zr.at[k, j],
            self.sems[7].at[k, j], self.sems[8].at[k, j], self.zpeers[j],
        )

    def put_out(self, t):
        layer, col = self.where(t)
        k = t % LAND
        return pltpu.make_async_copy(self.fin.at[k], self.out_ref.at[layer, :, pl.ds(col, CHUNK)], self.fsem.at[k])

    def add(self, dst, src):
        @pl.loop(0, 4)
        def _(i):
            dst[i] = dst[i] + src[i]

    def step(self, name, t):
        own = self.own.at[t % OWN]
        k = t % LAND
        if name == "a":
            self.sib_copy(t).start()
            self.own_copy(t).start()
        elif name == "b":
            self.sib_copy(t).wait()
            self.own_copy(t).wait()
            self.add(own, self.sibr.at[k])

            for j in range(2):
                self.p2_copy(t, j).start()
        elif name == "c":
            for j in range(2):
                self.p2_copy(t, j).wait()
            self.add(own.at[:, self.q], self.p2r.at[k, 0])
            self.add(own.at[:, self.qf], self.p2r.at[k, 1])
            self.p1_copy(t).start()
        elif name == "d":
            self.p1_copy(t).wait()
            self.add(own.at[:, self.q], self.p1r.at[k])
            for j in range(3):
                self.z_copy(t, j).start()
        elif name == "e":
            for j in range(3):
                self.z_copy(t, j).wait()
            total = own[self.z, self.q].astype(F32)
            for j in range(3):
                total = total + self.zr[k, j].astype(F32)
            if t >= LAND:
                self.put_out(t - LAND).wait()
            self.fin[k] = total
            self.put_out(t).start()


BACK = {
    "f1": ["", "", "", "", "a0", "", "b0", "a1"],
    "ffn1": "",
    "wo1": "c0b1a2",
    "heads1": ["", "", "d0", "c1b2", ""],
    "psent1": "a3e0d1c2b3",
    "end1": "a4",
    "f0": ["e1d2c3", "b4", "", "", "e2d3a5", "c4", "", "b5e3d4"],
    "ffn0": "",
    "wo0": "a6c5e4b6a7",
    "heads0": ["", "d5", "c6b7", "", "e5d6a8c7"],
    "psent0": "b8e6",
    "end0": ["a9", "d7c8", "b9e7", "d8", "c9e8", "d9e9"],
}


def backward_kernel(dx_ref, last_ref, xs_ref, xms_ref, os_ref, hdns_ref, gps_ref, qs_ref, ks_ref, vs_ref, ohs_ref, lses_ref,
                    vec_ref, segr_ref, segc_ref, w_ref,
                    hout_ref, gin_ref, gv_ref, gout_ref, g_ref,
                    wbuf, x_s, xm_s, o_s, hdn_s, gp_s, q_s, k_s, v_s, oh_s, lse_s,
                    gbuf, at_s, dy, dyt, da2, dosend, dorecv, dos, kt, dqt, dk, dv, delta, psend0, psend1, precv0, precv1, dp4,
                    own, sibr, p2r, p1r, zr, fin, dxo_ref, vgot, dpad,
                    wsem, lsem, gsem, ss, rs, oss, ors, fsem, mv_s, mv_r, vs_sem, vr_sem, *net_sems):
    y, x, c, z = where_am_i()
    me, peer_of = attention_peers(y, x, c, z)
    psends, precvs = (psend0, psend1), (precv0, precv1)
    net = Scatter(g_ref, gout_ref, own, sibr, p2r, p1r, zr, fin, fsem, net_sems)

    def load_w(layer, i):
        return pltpu.make_async_copy(w_ref.at[layer, :, :, pl.ds(i * CHUNK, CHUNK)], wbuf.at[HELD[layer, i]], wsem.at[i])

    saved = {
        "x": (xs_ref, x_s), "xm": (xms_ref, xm_s), "o": (os_ref, o_s), "hdn": (hdns_ref, hdn_s), "gp": (gps_ref, gp_s),
        "q": (qs_ref, q_s), "k": (ks_ref, k_s), "v": (vs_ref, v_s), "oh": (ohs_ref, oh_s), "lse": (lses_ref, lse_s),
    }

    def load(name, layer):
        src, dst = saved[name]
        return pltpu.make_async_copy(src.at[layer], dst, lsem.at[SAVED.index(name)])

    def fetch(layer, names):
        for name in names:
            if isinstance(name, int):
                load_w(layer, name).start()
            else:
                load(name, layer).start()

    def arrive(layer, *names):
        for name in names:
            if isinstance(name, int):
                load_w(layer, name).wait()
            else:
                load(name, layer).wait()

    fetch(1, ["xm", "hdn", "gp", 3, 1, 4, 2, "k", "q", "v", "oh", "lse", "o", "x"])
    zx = z + 1 - 2 * lax.rem(z, 2)
    greet(net.zpeers + [net.pf, net.pg, net.sib, (row_of(y, x, 1 - c), zx), swap_partner(y, x, c, z)])
    move_tokens(last_ref, hout_ref, mv_s.at[0], mv_r.at[0], 0)
    dxo_ref[...] = dx_ref[...]

    ends = [net.sib, (row_of(y, 1 - x, c), z), (row_of(1 - y, x, c), z), (row_of(y, x, c), zx),
            (row_of(y, x, c), lax.rem(z + 2, 4))]

    def vector_hop(k):
        return remote(gv_ref, vgot.at[k], vs_sem.at[k], vr_sem.at[k], ends[k])

    for layer in reversed(range(LAYERS)):
        vl = vec_ref.at[pl.ds(layer, 1), :]
        gl = gv_ref.at[pl.ds(layer, 1), :]
        dy[...] = dxo_ref[...].astype(BF16)
        dyf = dy[...].astype(F32)
        dyt[...] = dyf.T.astype(BF16)
        gl[0:1, 4480:5120] = col_sum(dyf)
        arrive(layer, "xm")
        n2, spread2 = norm_parts(xm_s[...])
        g2 = piece(vl, 3200)
        at_s[...] = (n2 * g2 + piece(vl, 3840)).T.astype(BF16)
        da2[...] = jnp.zeros_like(da2)
        arrive(layer, "hdn")

        def put(slot, i, col):
            return pltpu.make_async_copy(gbuf.at[slot], g_ref.at[layer, i, :, :, :, pl.ds(col, CHUNK)], gsem.at[slot])

        for half in range(2):
            @pl.loop(0, 4, unroll=4)
            def _(i):
                net.run_at(BACK["f%d" % layer][4 * half : 4 * half + 4], i)
                to = pl.multiple_of(i * 1280 + half * CHUNK, CHUNK)

                gdown = dot(dyt[...], hdn_s[:, pl.ds(to, CHUNK)]).astype(BF16)

                @pl.when(i == 0)
                def _():
                    if half == 0:
                        arrive(layer, "gp")
                    arrive(layer, 3 + half, 1 + half)

                @pl.when(i > 0)
                def _():
                    put(0, 0, 0).wait()

                gbuf[0] = gdown.reshape(4, 2, 80, CHUNK)
                put(0, i, 1920 + half * CHUNK).start()
                dh = dot(dy[...], wbuf[HELD[layer, 3 + half], i])
                du = (dh * gp_s[:, pl.ds(to, CHUNK)].astype(F32)).astype(BF16)
                gl[0:1, pl.ds(5120 + to, CHUNK)] = col_sum(du.astype(F32))
                gup = dot(at_s[...], du).astype(BF16)

                @pl.when(i > 0)
                def _():
                    put(1, 0, 0).wait()

                gbuf[1] = gup.reshape(4, 2, 80, CHUNK)
                put(1, i, 640 + half * CHUNK).start()
                da2[...] += dot_nt(du, wbuf[HELD[layer, 1 + half], i])

            put(0, 0, 0).wait()
            put(1, 0, 0).wait()
            if half == 0:
                fetch(layer, [0])
            elif layer:
                fetch(layer - 1, [3, 1, 4])
            if half:
                net.run(BACK["ffn%d" % layer])

        da2v = da2[...]
        gl[0:1, 3200:3840] = col_sum(da2v * n2)
        gl[0:1, 3840:4480] = col_sum(da2v)
        dxm = dxo_ref[...] + norm_back(da2v, n2, spread2, g2)
        dxo_ref[...] = dxm
        if layer:
            fetch(layer - 1, ["hdn", "gp", "xm"])
        dy1f = dxm.astype(BF16).astype(F32)
        dy[...] = dxm.astype(BF16)
        gl[0:1, 2560:3200] = col_sum(dy1f)
        arrive(layer, 0)
        wa = wbuf.at[HELD[layer, 0]]
        zpad = jnp.zeros((320, 96), F32)
        for i in range(4):
            dpad[i] = jnp.concatenate([zpad, dy1f[:, HW * i : HW * (i + 1)]], axis=1).astype(BF16)
        da2[...] = jnp.zeros_like(da2)

        for i in range(4):
            da2[...] += dot_nt(dpad[i], wa[i, :, 384:640])

        for b in range(4):
            dosend[b] = fold(da2[:, HW * b : HW * (b + 1)], 4).astype(BF16)
        copies = exchange(me, peer_of, dosend, dorecv, oss.at[layer], ors.at[layer])
        dorecv[me] = dosend[me]
        arrive(layer, "k", "q", "v", "oh", "lse")
        kt[...] = k_s[...].astype(F32).T.astype(BF16)
        dk[...] = jnp.zeros_like(dk)
        dv[...] = jnp.zeros_like(dv)
        net.run(BACK["wo%d" % layer])
        for cp in copies:
            cp.wait()
        for b in range(4):
            for j in range(4):
                dos[320 * b + 80 * j : 320 * b + 80 * (j + 1), :] = (
                    dorecv[b, :, HW * j : HW * (j + 1)].astype(F32).astype(BF16)
                )
        lane = lax.broadcasted_iota(jnp.int32, (8, HW), 1)
        head = lax.broadcasted_iota(jnp.int32, (8, HW), 0)
        pick = jnp.where((lane >= head * HDIM) & (lane < (head + 1) * HDIM), 1.0, 0.0).astype(F32)
        delta[...] = lax.dot_general(
            pick, dos[...].astype(F32) * oh_s[...].astype(F32), NT,
            precision=lax.Precision.HIGHEST, preferred_element_type=F32,
        )

        groups = {}
        for g in (1, 0):
            first, heads, _ = GROUPS[g]
            plans = BACK["heads%d" % layer][0:3] if g else BACK["heads%d" % layer][3:5]

            @pl.loop(first, first + heads)
            def _(h):
                net.run_at(plans, h - first)

                @pl.loop(0, 5, unroll=5)
                def _(step):
                    at = pl.multiple_of(step * QB, QB)
                    zero = jnp.zeros((), BF16)
                    mask = head_mask(h, QB)
                    qm = jnp.where(mask, q_s[pl.ds(at, QB), :], zero)
                    dm = jnp.where(mask, dos[pl.ds(at, QB), :], zero)
                    s = dot_nt(k_s[...], qm)
                    s = jnp.where(segc_ref[...] == segr_ref[0:1, pl.ds(at, QB)], s, negative)
                    p = jnp.exp2(s * SCALE2 - lse_s[pl.ds(h, 1), pl.ds(at, QB)])
                    dp = dot_nt(v_s[...], dm)
                    ds = (p * (dp - delta[pl.ds(h, 1), pl.ds(at, QB)])).astype(BF16)
                    dv[...] += dot(p.astype(BF16), dm)
                    dk[...] += dot(ds, qm)
                    rows = pl.ds(pl.multiple_of(h * HDIM, HDIM), HDIM)
                    dqt[rows, pl.ds(at, QB)] = dot(kt[rows, :], ds)

            if layer and g == 0:
                fetch(layer - 1, ["k", "q", "v", "oh", "lse"])
            dq = dqt[...].T * SCALE
            for b in range(4):
                rows = slice(320 * b, 320 * (b + 1))
                psends[g][b] = pack_group(g, (dq[rows], dk[rows, :] * SCALE, dv[rows, :]))
            groups[g] = exchange(me, peer_of, psends[g], precvs[g], ss.at[layer, g], rs.at[layer, g])
            precvs[g][me] = psends[g][me]
        copies = groups[1] + groups[0]
        zpad = jnp.zeros((320, 32), F32)
        arrive(layer, "x", "o")
        n1, spread1 = norm_parts(x_s[...])
        g1 = piece(vl, 0)
        at_s[...] = (n1 * g1 + piece(vl, 640)).T.astype(BF16)
        dyt[...] = o_s[...].astype(F32).T.astype(BF16)
        if layer:
            fetch(layer - 1, ["x", "o"])
        net.run(BACK["psent%d" % layer])
        for cp in copies:
            cp.wait()
        blocks = []
        for kind in range(3):
            own_kind = [
                jnp.concatenate([unpack_group(g, precvs[g][b], kind) for g in range(2)], axis=1) for b in range(4)
            ]
            if kind != 1:
                at = 1280 if kind == 0 else 1920
                gl[0:1, at : at + 640] = jnp.concatenate([col_sum(part) for part in own_kind], axis=1)
            blocks += own_kind
        for i in range(4):
            dp4[i] = jnp.concatenate(blocks[3 * i : 3 * i + 3] + [zpad], axis=1).astype(BF16)
        da2[...] = jnp.zeros_like(da2)

        for i in range(4):
            slot = i % 2
            part = dot(at_s[...], dp4[i])
            rest = dot(dyt[...], dpad[i])
            if i > 1:
                put(slot, 0, 0).wait()

            gbuf[slot, :, :, :, 0:384] = part[:, 0:384].astype(BF16).reshape(4, 2, 80, 384)
            gbuf[slot, :, :, :, 384:512] = (part[:, 384:512] + rest[:, 0:128]).astype(BF16).reshape(4, 2, 80, 128)
            gbuf[slot, :, :, :, 512:640] = rest[:, 128:256].astype(BF16).reshape(4, 2, 80, 128)
            put(slot, i, 0).start()
            da2[...] += dot_nt(dp4[i], wa[i, :, 0:512])

        da = da2[...]
        if layer:
            fetch(layer - 1, [2])
        gl[0:1, 0:640] = col_sum(da * n1)
        gl[0:1, 640:1280] = col_sum(da)
        dxo_ref[...] = dxo_ref[...] + norm_back(da, n1, spread1, g1)
        put(0, 0, 0).wait()
        put(1, 0, 0).wait()
        if layer:
            net.run(BACK["end%d" % layer])
    move_tokens(dxo_ref, gin_ref, mv_s.at[1], mv_r.at[1], 0)
    for k, plan in enumerate(BACK["end0"]):
        if k:
            vector_hop(k - 1).wait()
            gv_ref[...] += vgot[k - 1]
        if k < 5:
            vector_hop(k).start()
        net.run(plan)
    for t in range(NCH - LAND, NCH):
        net.put_out(t).wait()
    move_tokens(last_ref, hout_ref, mv_s.at[0], mv_r.at[0], 1)
    move_tokens(dxo_ref, gin_ref, mv_s.at[1], mv_r.at[1], 1)


def backward_all(dx, last, kept, vec, segr, segc, weights):
    dma = pltpu.SemaphoreType.DMA
    sds = jax.ShapeDtypeStruct
    vmem = pltpu.VMEM
    return pl.pallas_call(
        backward_kernel,
        name="backward",
        out_shape=(
            sds((320, 640), F32), sds((320, 640), F32), sds((LAYERS, 10240), F32), sds((LAYERS, 80, 3200), F32),
            sds((LAYERS, 4, 4, 2, 80, 3200), BF16),
        ),
        in_specs=[VM] + [ANY] * 11 + [VM, VM, VM, ANY],
        out_specs=(ANY, ANY, VM, ANY, ANY),
        scratch_shapes=[
            vmem((4, 4, 640, CHUNK), BF16),
            vmem((320, 640), F32), vmem((320, 640), F32), vmem((320, 640), BF16),
            vmem((320, 5120), BF16), vmem((320, 5120), BF16),
            vmem((1280, HW), BF16), vmem((1280, HW), BF16), vmem((1280, HW), BF16), vmem((1280, HW), BF16),
            vmem((8, 1280), F32),
            vmem((2, 4, 2, 80, CHUNK), BF16), vmem((640, 320), BF16),
            vmem((320, 640), BF16), vmem((640, 320), BF16), vmem((320, 640), F32),
            vmem((4, 80, 640), BF16), vmem((4, 80, 640), BF16), vmem((1280, HW), BF16),
            vmem((HW, 1280), BF16), vmem((HW, 1280), F32),
            vmem((1280, HW), F32), vmem((1280, HW), F32), vmem((8, 1280), F32),
            *[vmem(shape, BF16) for shape in group_shapes() * 2], vmem((4, 320, 512), BF16),
            vmem((OWN, 4, 4, 80, CHUNK), BF16), vmem((LAND, 4, 4, 80, CHUNK), BF16),
            vmem((LAND, 2, 4, 80, CHUNK), BF16), vmem((LAND, 4, 80, CHUNK), BF16), vmem((LAND, 3, 80, CHUNK), BF16),
            vmem((LAND, 80, CHUNK), F32), vmem((320, 640), F32), vmem((5, LAYERS, 10240), F32),
            vmem((4, 320, 256), BF16),
            dma((5,)), dma((len(SAVED),)), dma((2,)),
            dma((LAYERS, 2, 4)), dma((LAYERS, 2, 4)), dma((LAYERS, 4)), dma((LAYERS, 4)), dma((LAND,)),
            dma((2,)), dma((2,)), dma((5,)), dma((5,)),
            dma((OWN,)), dma((LAND,)), dma((LAND,)), dma((LAND, 2)), dma((LAND, 2)),
            dma((LAND,)), dma((LAND,)), dma((LAND, 3)), dma((LAND, 3)),
        ],
        compiler_params=pltpu.CompilerParams(
            collective_id=1, has_side_effects=True, vmem_limit_bytes=60 << 20
        ),
    )(dx, last, *kept, vec, segr, segc, weights)


def per_device_fast(
    hidden_in, cotangent, segment_ids, w_qkv, w_out, w_up, w_down, vectors,
    m_qkv, v_qkv, m_out, v_out, m_up, v_up, m_down, v_down, m_vectors, v_vectors,
):
    depth = w_qkv.shape[0]
    shards = jnp.concatenate(
        [w_qkv.astype(BF16), w_out.astype(BF16), w_up.astype(BF16), w_down.astype(BF16).transpose(0, 2, 1)], axis=2
    )
    weights, x, dx, segr, segc, *kept = forward_all(hidden_in, cotangent, segment_ids, vectors, shards)
    hidden_out, grad_in, grad_vectors, grad_all, _ = backward_all(
        dx, x, kept, vectors, segr, segc, weights.reshape(depth, 4, 640, 3200)
    )
    gradients = (
        grad_all[:, :, 0:480], grad_all[:, :, 480:640], grad_all[:, :, 640:1920],
        grad_all[:, :, 1920:3200].transpose(0, 2, 1),
    )
    masters = (w_qkv, w_out, w_up, w_down)
    firsts = (m_qkv, m_out, m_up, m_down)
    seconds = (v_qkv, v_out, v_up, v_down)
    updates = [
        adam_direction(masters[kind], gradients[kind], firsts[kind], seconds[kind], 0.01) for kind in range(4)
    ]
    partial_sums = jnp.stack(
        [jnp.stack(matrix_sums(masters[kind], updates[kind][2]), axis=1) for kind in range(4)], axis=1
    )
    flat = jnp.pad(partial_sums.reshape(1, -1), ((0, 7), (0, 128 - partial_sums.size)))
    total_sums = total_over_devices(flat, 3)[0, : partial_sums.size].reshape(partial_sums.shape)
    lamb_norms = jnp.sqrt(total_sums)
    trust_ratio = lamb_norms[:, :, 0] / lamb_norms[:, :, 1]
    new_masters = [
        masters[kind] - 0.5 * trust_ratio[:, kind, None, None] * updates[kind][2] for kind in range(4)
    ]
    vec_first, vec_second, new_vectors = vector_update(vectors, grad_vectors, m_vectors, v_vectors)
    moments = [part for kind in range(4) for part in updates[kind][:2]]
    return (
        hidden_out, grad_in, *gradients, grad_vectors, *moments, vec_first, vec_second,
        *new_masters, new_vectors, *[w.astype(BF16) for w in new_masters], lamb_norms,
    )


def solution(mesh):
    fast = mesh.shape["row"] == 8 and mesh.shape["col"] == 4
    per_device = per_device_fast if fast else per_device_any
    return jax.shard_map(
        per_device,
        mesh=mesh,
        in_specs=(
            P(("row", "col"), None),
            P(("row", "col"), None),
            P("row", None),
            P(None, "row", "col"),
            P(None, "row", "col"),
            P(None, "row", "col"),
            P(None, "col", "row"),
            P(),
            P(None, "row", "col"),
            P(None, "row", "col"),
            P(None, "row", "col"),
            P(None, "row", "col"),
            P(None, "row", "col"),
            P(None, "row", "col"),
            P(None, "col", "row"),
            P(None, "col", "row"),
            P(),
            P(),
        ),
        out_specs=(
            P(("row", "col"), None),
            P(("row", "col"), None),
            P(None, "row", "col"),
            P(None, "row", "col"),
            P(None, "row", "col"),
            P(None, "col", "row"),
            P(),
            P(None, "row", "col"),
            P(None, "row", "col"),
            P(None, "row", "col"),
            P(None, "row", "col"),
            P(None, "row", "col"),
            P(None, "row", "col"),
            P(None, "col", "row"),
            P(None, "col", "row"),
            P(),
            P(),
            P(None, "row", "col"),
            P(None, "row", "col"),
            P(None, "row", "col"),
            P(None, "col", "row"),
            P(),
            P(None, "row", "col"),
            P(None, "row", "col"),
            P(None, "row", "col"),
            P(None, "col", "row"),
            P(),
        ),
        check_vma=False,
    )
```
